32 devices in a mesh: dp: 16 (over z, x, core), sp: 2 (over y).
Axes of the slice: x: 2, y: 2, z: 4, core: 2. Of those that a mesh axis runs over, the one named last changes fastest.
Arguments:
- tokens: bfloat16 [2, 32768, 1024], P(None, ('dp', 'sp')), may hold values from -6 to 6
- doc_lengths: int32 [16, 2, 4], P('dp'), may hold values from 0 to 2048, as said below
- out_cotangent: bfloat16 [2, 32768, 1024], P(None, ('dp', 'sp')), may hold values from -6 to 6
- in_gain: bfloat16 [1024], P(('dp', 'sp')), may hold values from 0.099609375 to 1.8984375
- in_bias: bfloat16 [1024], P(('dp', 'sp')), may hold values from -3 to 3
- qkv_weight: bfloat16 [1024, 3072], P(('dp', 'sp')), may hold values from -0.1875 to 0.1875
- q_bias: bfloat16 [1024], P(('dp', 'sp')), may hold values from -3 to 3
- v_bias: bfloat16 [1024], P(('dp', 'sp')), may hold values from -3 to 3
- head_scale: bfloat16 [16], P('sp'), may hold values from 0.5 to 2
- attn_gain: bfloat16 [1024], P(('dp', 'sp')), may hold values from 0.099609375 to 1.8984375
- attn_bias: bfloat16 [1024], P(('dp', 'sp')), may hold values from -3 to 3
- out_weight: bfloat16 [1024, 1024], P(('dp', 'sp')), may hold values from -0.1875 to 0.1875
- out_bias: bfloat16 [1024], P(('dp', 'sp')), may hold values from -3 to 3
- ffn_gain: bfloat16 [1024], P(('dp', 'sp')), may hold values from 0.099609375 to 1.8984375
- ffn_bias: bfloat16 [1024], P(('dp', 'sp')), may hold values from -3 to 3
- fc1_weight: bfloat16 [1024, 4096], P(('dp', 'sp')), may hold values from -0.1875 to 0.1875
- fc1_bias: bfloat16 [4096], P(('dp', 'sp')), may hold values from -3 to 3
- mid_gain: bfloat16 [4096], P(('dp', 'sp')), may hold values from 0.099609375 to 1.8984375
- mid_bias: bfloat16 [4096], P(('dp', 'sp')), may hold values from -3 to 3
- fc2_weight: bfloat16 [4096, 1024], P(('dp', 'sp')), may hold values from -0.09375 to 0.09375
- fc2_bias: bfloat16 [1024], P(('dp', 'sp')), may hold values from -3 to 3
Outputs:
- layer_out: bfloat16 [2, 32768, 1024], P(None, ('dp', 'sp'))
- input_grad: float32 [2, 32768, 1024], P(None, ('dp', 'sp'))
- in_gain_grad: float32 [1024], P(('dp', 'sp'))
- in_bias_grad: float32 [1024], P(('dp', 'sp'))
- qkv_weight_grad: float32 [1024, 3072], P(('dp', 'sp'))
- q_bias_grad: float32 [1024], P(('dp', 'sp'))
- v_bias_grad: float32 [1024], P(('dp', 'sp'))
- head_scale_grad: float32 [16], P('sp')
- attn_gain_grad: float32 [1024], P(('dp', 'sp'))
- attn_bias_grad: float32 [1024], P(('dp', 'sp'))
- out_weight_grad: float32 [1024, 1024], P(('dp', 'sp'))
- out_bias_grad: float32 [1024], P(('dp', 'sp'))
- ffn_gain_grad: float32 [1024], P(('dp', 'sp'))
- ffn_bias_grad: float32 [1024], P(('dp', 'sp'))
- fc1_weight_grad: float32 [1024, 4096], P(('dp', 'sp'))
- fc1_bias_grad: float32 [4096], P(('dp', 'sp'))
- mid_gain_grad: float32 [4096], P(('dp', 'sp'))
- mid_bias_grad: float32 [4096], P(('dp', 'sp'))
- fc2_weight_grad: float32 [4096, 1024], P(('dp', 'sp'))
- fc2_bias_grad: float32 [1024], P(('dp', 'sp'))
The draws below stay inside these ranges and needn't reach their ends.
Inputs may be any that keep to these rules, and one draw needn't show every extreme that they name: `doc_lengths`: entries 4 w to 4 w + 3 of row [g, m] list, in order and followed by zeros, the lengths of the sequences packed into window w of 2048 tokens of group g's buffer of micro-batch m, each 512, 1024 or 2048, summing to 2048; in every micro-batch at least one group holds a single sequence of 2048 tokens in every window.
All inputs are finite; a program needn't handle non-finite values.
Results may differ from the reference program's by a relative error of at most 0.018.
Values may be sent and summed in bfloat16 or wider, within the bound.
A program may use at most 448 MiB of HBM per device.

```python
import math
import jax
import jax.numpy as jnp
import numpy as np
from jax import lax

H = 16
D = 1024
FF = 4096
MICRO = 2
LONGEST = 2048
GROUPS = 16
WINDOWS = 1
SLOTS = 4
TOKENS = 32768


def draw_doc_lengths(key, part):
    patterns = jnp.asarray(np.array([[4, 0, 0, 0], [2, 2, 0, 0], [2, 1, 1, 0], [1, 2, 1, 0], [1, 1, 2, 0], [1, 1, 1, 1]], dtype=np.int32))
    key_pick = jax.random.fold_in(key, 11)
    key_force = jax.random.fold_in(key, 23)
    chosen = jax.random.randint(key_pick, (GROUPS, MICRO, WINDOWS), 0, 6)
    forced = jax.random.randint(key_force, (MICRO,), 0, GROUPS)
    full_row = jnp.arange(GROUPS, dtype=jnp.int32)[:, None] == forced[None, :]
    chosen = jnp.where(full_row[:, :, None], 0, chosen)
    table = patterns[chosen] * (LONGEST // 4)
    return table.reshape(GROUPS, MICRO, SLOTS).astype(jnp.int32)


def block_levels(stream_key, extent, pieces, smallest, top_value):
    factor_of = 1.0
    for axis_at, shards_of in pieces:
        steps = jax.random.uniform(jax.random.fold_in(jax.random.fold_in(stream_key, 6), axis_at), (shards_of,), jnp.float32, smallest / len(pieces), top_value / len(pieces))
        factor_of = factor_of * jnp.repeat(jnp.exp(steps), extent[axis_at] // shards_of).reshape((-1,) + (1,) * (len(extent) - 1 - axis_at))
    return factor_of


def centred(key, extent, width, limit, pieces=(), kind=jnp.bfloat16):
    values = width * jax.random.normal(key, extent, jnp.float32)
    if pieces:
        values = values * block_levels(key, extent, pieces, -0.22, 0.18)
    return jnp.clip(values, -limit, limit).astype(kind)


def setup_inputs(seed: int = 0) -> dict:
    key_list = jax.random.split(jax.random.key(seed), 22)
    tokens = centred(key_list[0], (MICRO, TOKENS, D), 1.0, 6.0, ((1, 32),))
    doc_lengths = draw_doc_lengths(jax.random.fold_in(key_list[21], 71), 0)
    out_cotangent = centred(key_list[2], (MICRO, TOKENS, D), 1.0, 6.0, ((1, 32),))
    in_gain = jnp.clip(1.0 + 0.18 * jax.random.normal(key_list[3], (D,), jnp.float32), 0.099609375, 1.8984375).astype(jnp.bfloat16)
    in_bias = centred(key_list[4], (D,), 0.5, 3.0, ((0, 32),))
    qkv_weight = centred(key_list[5], (D, 3 * D), D ** -0.5, 0.1875, ((0, 32),))
    q_bias = centred(key_list[6], (D,), 0.5, 3.0, ((0, 32),))
    v_bias = centred(key_list[7], (D,), 0.5, 3.0, ((0, 32),))
    head_scale = jnp.clip(jnp.exp(math.log(2.0) - 1.3862944 * jax.random.uniform(key_list[8], (H,), jnp.float32) ** block_levels(key_list[8], (H,), ((0, 2),), -0.2, 0.2)), 0.5, 2.0).astype(jnp.bfloat16)
    attn_gain = jnp.clip(1.0 + 0.18 * jax.random.normal(key_list[9], (D,), jnp.float32), 0.099609375, 1.8984375).astype(jnp.bfloat16)
    attn_bias = centred(key_list[10], (D,), 0.5, 3.0, ((0, 32),))
    out_weight = centred(key_list[11], (D, D), D ** -0.5, 0.1875, ((0, 32),))
    out_bias = centred(key_list[12], (D,), 0.5, 3.0, ((0, 32),))
    ffn_gain = jnp.clip(1.0 + 0.18 * jax.random.normal(key_list[13], (D,), jnp.float32), 0.099609375, 1.8984375).astype(jnp.bfloat16)
    ffn_bias = centred(key_list[14], (D,), 0.5, 3.0, ((0, 32),))
    fc1_weight = centred(key_list[15], (D, FF), D ** -0.5, 0.1875, ((0, 32),))
    fc1_bias = centred(key_list[16], (FF,), 0.5, 3.0, ((0, 32),))
    mid_gain = jnp.clip(1.0 + 0.18 * jax.random.normal(key_list[17], (FF,), jnp.float32), 0.099609375, 1.8984375).astype(jnp.bfloat16)
    mid_bias = centred(key_list[18], (FF,), 0.5, 3.0, ((0, 32),))
    fc2_weight = centred(key_list[19], (FF, D), FF ** -0.5, 0.09375, ((0, 32),))
    fc2_bias = centred(key_list[20], (D,), 0.5, 3.0, ((0, 32),))
    return dict(tokens=tokens, doc_lengths=doc_lengths, out_cotangent=out_cotangent, in_gain=in_gain, in_bias=in_bias, qkv_weight=qkv_weight, q_bias=q_bias, v_bias=v_bias, head_scale=head_scale, attn_gain=attn_gain, attn_bias=attn_bias, out_weight=out_weight, out_bias=out_bias, ffn_gain=ffn_gain, ffn_bias=ffn_bias, fc1_weight=fc1_weight, fc1_bias=fc1_bias, mid_gain=mid_gain, mid_bias=mid_bias, fc2_weight=fc2_weight, fc2_bias=fc2_bias)


EPS = 1e-05
HIGH = lax.Precision.HIGHEST

@jax.custom_vjp
def low(v):
    return lax.optimization_barrier(v.astype(jnp.bfloat16)).astype(jnp.float32)

@jax.custom_vjp
def low_back(v):
    return v

def low_keep(v):
    return (low(v), None)

def low_pass(kept, grad):
    return (grad,)

def back_keep(v):
    return (v, None)

def back_low(kept, grad):
    return (low(grad),)
low.defvjp(low_keep, low_pass)
low_back.defvjp(back_keep, back_low)

def layer_norm(values, norm_gain, norm_shift):
    center = values - lax.optimization_barrier(jnp.mean(values, axis=-1, keepdims=True))
    spread = lax.optimization_barrier(jnp.mean(center * center, axis=-1, keepdims=True))
    return center * lax.rsqrt(spread + EPS) * norm_gain + norm_shift

def doc_index(lengths, row_count):
    seq_ends = jnp.cumsum(lengths)
    places = jnp.arange(row_count, dtype=jnp.int32)
    return lax.optimization_barrier(jnp.sum((places[:, None] >= seq_ends[None, :]).astype(jnp.int32), axis=1))

def to_heads(matrix, row_count, head_count):
    return matrix.reshape(row_count, head_count, -1)

def layer_rows(params, head_gains, tok_rows, doc_ids):
    in_gain, in_bias, qkv_weight, q_bias, v_bias, attn_gain, attn_bias, out_weight, out_bias, ffn_gain, ffn_bias, fc1_weight, fc1_bias, mid_gain, mid_bias, fc2_weight, fc2_bias = params
    row_count = tok_rows.shape[0]
    model_width = tok_rows.shape[1]
    head_count = head_gains.shape[0]
    score_scale = 1.0 / math.sqrt(model_width // head_count)
    normed = low(layer_norm(tok_rows, in_gain, in_bias))
    projected = jnp.dot(normed, qkv_weight, precision=HIGH)
    queries = low(low_back(projected[:, :model_width] + q_bias))
    key_rows = low(low_back(projected[:, model_width:2 * model_width]))
    value_rows = low(low_back(projected[:, 2 * model_width:] + v_bias))
    scores = low_back(jnp.einsum('qhd,khd->hqk', to_heads(queries, row_count, head_count), to_heads(key_rows, row_count, head_count), precision=HIGH) * score_scale)
    places = jnp.arange(row_count, dtype=jnp.int32)
    allowed = (doc_ids[:, None] == doc_ids[None, :]) & (places[None, :] <= places[:, None])
    probs = jax.nn.softmax(jnp.where(allowed[None], scores, -1e+30), axis=-1)
    mixed = low_back(jnp.einsum('hqk,khd->qhd', low(probs), to_heads(value_rows, row_count, head_count), precision=HIGH))
    scaled = low(low_back((mixed * head_gains[None, :, None]).reshape(row_count, model_width)))
    post_norm = low(layer_norm(scaled, attn_gain, attn_bias))
    hidden = tok_rows + low_back(jnp.dot(post_norm, out_weight, precision=HIGH)) + out_bias
    ffn_in = low(layer_norm(hidden, ffn_gain, ffn_bias))
    ffn_inner = low_back(jnp.dot(ffn_in, fc1_weight, precision=HIGH) + fc1_bias)
    active = low(layer_norm(jax.nn.gelu(ffn_inner), mid_gain, mid_bias))
    return hidden + low_back(jnp.dot(active, fc2_weight, precision=HIGH)) + fc2_bias

def reference(tokens, doc_lengths, out_cotangent, in_gain, in_bias, qkv_weight, q_bias, v_bias, head_scale, attn_gain, attn_bias, out_weight, out_bias, ffn_gain, ffn_bias, fc1_weight, fc1_bias, mid_gain, mid_bias, fc2_weight, fc2_bias):
    params = tuple((item.astype(jnp.float32) for item in (in_gain, in_bias, qkv_weight, q_bias, v_bias, attn_gain, attn_bias, out_weight, out_bias, ffn_gain, ffn_bias, fc1_weight, fc1_bias, mid_gain, mid_bias, fc2_weight, fc2_bias)))
    head_gains = head_scale.astype(jnp.float32)
    inputs = tokens.astype(jnp.float32)
    micro_count, total_rows, model_width = tokens.shape
    group_count = doc_lengths.shape[0]
    group_rows = total_rows // group_count
    window_count = group_rows // LONGEST
    lens_flat = jnp.transpose(doc_lengths, (1, 0, 2)).reshape(micro_count * group_count, -1)
    buffer_ids = jax.vmap(lambda lengths: doc_index(lengths, group_rows))(lens_flat)
    window_ids = buffer_ids.reshape(micro_count * group_count * window_count, LONGEST).astype(jnp.int32)

    def forward(params, head_gains, inputs):
        windows = inputs.reshape(micro_count * group_count * window_count, LONGEST, model_width)
        one_window = jax.checkpoint(lambda tok_rows, doc_ids: layer_rows(params, head_gains, tok_rows, doc_ids))

        def scan_step(carry, pair):
            return (carry, one_window(pair[0], pair[1]))
        _, results = lax.scan(scan_step, None, (windows, window_ids))
        return results.reshape(micro_count, total_rows, model_width)
    outputs, pullback = jax.vjp(forward, params, head_gains, inputs)
    grad_params, grad_scale, grad_input = pullback(out_cotangent.astype(jnp.float32))
    return (outputs.astype(jnp.bfloat16), grad_input, grad_params[0], grad_params[1], grad_params[2], grad_params[3], grad_params[4], grad_scale, grad_params[5], grad_params[6], grad_params[7], grad_params[8], grad_params[9], grad_params[10], grad_params[11], grad_params[12], grad_params[13], grad_params[14], grad_params[15], grad_params[16])
```

```python
import functools
import math

import jax
import jax.numpy as jnp
from jax import lax
from jax.experimental import pallas as pl
from jax.experimental.pallas import tpu as pltpu
from jax.sharding import PartitionSpec as P

EPS = 1e-05
BLOCK = 512
LOG2E = math.log2(math.e)
NEG = -1e30
F32 = jnp.float32
BF16 = jnp.bfloat16
VMEM_CAP = 60 * 1024 * 1024
NT = (((1,), (1,)), ((), ()))
NN = (((1,), (0,)), ((), ()))
FWD_STEPS = ((4, 8, 12, 16, 20), (8, 12, 16, 20, 24), (12, 17, 22, 27, 31), (16, 21, 26, 31, 31))
BWD_STEPS = ((1, 2, 3, 4, 5), (7, 13, 18, 23, 26), (10, 16, 21, 26, 29), (14, 20, 25, 30, 32))


def mm(a, b, dims=NN):
    return lax.dot_general(a, b, dims, preferred_element_type=F32)


class Place:
    def __init__(self, depth):
        d = lax.axis_index("dp")
        self.depth = depth
        self.y = lax.axis_index("sp")
        self.c = d % 2
        self.x = (d // 2) % 2
        self.z = d // 4
        self.next_y = self.device(self.z, self.x, self.c, 1 - self.y)
        self.next_x = self.device(self.z, 1 - self.x, self.c, self.y)
        self.twin = self.device(self.z, self.x, 1 - self.c, self.y)

    def device(self, z, x, c, y):
        return ((z * 2 + x) * 2 + c, y)

    def along(self, step):
        return (self.z + step) % self.depth

    def column(self, step):
        return self.device(self.along(step), self.x, self.c, self.y)

    def greet(self):
        barrier = pltpu.get_barrier_semaphore()
        peers = [self.column(s) for s in range(1, self.depth)] + [self.next_x, self.next_y, self.twin]
        for peer in peers:
            pl.semaphore_signal(barrier, inc=1, device_id=peer, device_id_type=pl.DeviceIdType.MESH)
        pl.semaphore_wait(barrier, len(peers))


def remote(src, dst, send, recv, peer):
    return pltpu.make_async_remote_copy(
        src_ref=src, dst_ref=dst, send_sem=send, recv_sem=recv, device_id=peer, device_id_type=pl.DeviceIdType.MESH
    )


class Gather:
    def __init__(self, me, shard, whole, at, count, local, send, recv):
        self.me, self.shard, self.whole = me, shard.at[pl.ds(at, count)], whole
        self.rows = pl.ds(at, count)
        self.local, self.send, self.recv = local, send, recv

    def own(self, z):
        me = self.me
        return self.whole.at[z, me.x, me.c, me.y, self.rows]

    def keep(self):
        return pltpu.make_async_copy(self.shard, self.own(self.me.z), self.local)

    def depth_hop(self, s, landed):
        me = self.me
        z = me.along(me.depth - s) if landed else me.z
        return remote(self.shard, self.own(z), self.send.at[6 + s], self.recv.at[6 + s], me.column(s))

    def hop(self, x, y, n, peer, c=None):
        group = self.whole.at[:, x, self.me.c if c is None else c, y, self.rows]
        return remote(group, group, self.send.at[n], self.recv.at[n], peer)

    def path(self, n, c=None):
        me = self.me
        x, y = me.x, me.y
        gx = 1 - x if n in (5, 6) else x
        gy = 1 - y if n in (2, 4, 6) else y
        peer = me.next_y if n == 0 else me.next_x if n < 3 else me.twin
        return self.hop(gx, gy, n, peer, c)

    def begin(self):
        self.keep().start()
        for s in range(1, self.me.depth):
            self.depth_hop(s, False).start()

    def spread(self):
        self.keep().wait()
        for s in range(1, self.me.depth):
            self.depth_hop(s, True).wait()
        for n in (0, 1, 3):
            self.path(n).start()

    def from_y(self):
        me = self.me
        self.hop(me.x, 1 - me.y, 0, me.next_y).wait_recv()
        self.path(2).start()
        self.path(4).start()

    def from_x(self):
        me = self.me
        self.hop(1 - me.x, me.y, 1, me.next_x).wait_recv()
        self.path(5).start()

    def from_corner(self):
        me = self.me
        self.hop(1 - me.x, 1 - me.y, 2, me.next_x).wait_recv()
        self.path(6).start()

    def end(self):
        for n in range(7):
            self.path(n).wait_send()
        for n in range(3, 7):
            self.path(n, 1 - self.me.c).wait_recv()


class Swap:
    def __init__(self, me, sent, landing, kept, place, local, send, recv):
        self.out = remote(sent, landing(me.y), send, recv, me.next_y)
        self.into = remote(sent, landing(1 - me.y), send, recv, me.next_y)
        self.keep = pltpu.make_async_copy(kept, place, local)

    def begin(self):
        self.out.start()
        self.keep.start()

    def end(self):
        self.out.wait_send()
        self.into.wait_recv()
        self.keep.wait()


def add_group(own, x, y, taken):
    def body(s, _):
        own[s, x, y] = (own[s, x, y].astype(F32) + taken(s).astype(F32)).astype(own.dtype)
        return 0

    lax.fori_loop(0, own.shape[0], body, 0)


class Scatter:
    def __init__(self, me, part, at, count, own, got0, got1, got3, local, send, recv, total):
        self.me, self.part, self.rows = me, part, pl.ds(at, count)
        self.own, self.got0, self.got1, self.got3 = own, got0, got1, got3
        self.local, self.send, self.recv, self.total = local, send, recv, total

    def mine(self):
        return pltpu.make_async_copy(self.part.at[:, :, self.me.c, :, self.rows], self.own, self.local)

    def halves(self):
        return remote(
            self.part.at[:, :, 1 - self.me.c, :, self.rows], self.got0, self.send.at[0], self.recv.at[0], self.me.twin
        )

    def to_x(self, n):
        me = self.me
        y = me.y if n == 0 else 1 - me.y
        return remote(self.own.at[:, 1 - me.x, y], self.got1.at[n], self.send.at[1 + n], self.recv.at[1 + n], me.next_x)

    def to_y(self):
        me = self.me
        return remote(self.own.at[:, me.x, 1 - me.y], self.got1.at[2], self.send.at[3], self.recv.at[3], me.next_y)

    def to_z(self, s):
        me = self.me
        return remote(
            self.own.at[me.along(s), me.x, me.y], self.got3.at[s - 1], self.send.at[3 + s], self.recv.at[3 + s],
            me.column(s),
        )

    def begin(self):
        self.mine().start()
        self.halves().start()

    def across(self):
        me, own, got = self.me, self.own, self.got0
        self.mine().wait()
        self.halves().wait()
        for n, x, y in ((1, 1 - me.x, 1 - me.y), (0, 1 - me.x, me.y)):
            add_group(own, x, y, lambda s: got[s, x, y])
            self.to_x(n).start()
        for x, y in ((me.x, 1 - me.y), (me.x, me.y)):
            add_group(own, x, y, lambda s: got[s, x, y])

    def along_x(self):
        me, own, got = self.me, self.own, self.got1
        self.to_x(1).wait_recv()
        add_group(own, me.x, 1 - me.y, lambda s: got[1, s])
        self.to_y().start()
        self.to_x(0).wait_recv()
        add_group(own, me.x, me.y, lambda s: got[0, s])

    def along_y(self):
        me, own, got = self.me, self.own, self.got1
        self.to_y().wait_recv()
        add_group(own, me.x, me.y, lambda s: got[2, s])
        for s in range(1, me.depth):
            self.to_z(s).start()

    def end(self):
        me = self.me
        total = self.own[me.z, me.x, me.y].astype(F32)
        for s in range(1, me.depth):
            self.to_z(s).wait_recv()
            total = total + self.got3[s - 1].astype(F32)
        self.total[self.rows] = total
        self.to_x(0).wait_send()
        self.to_x(1).wait_send()
        self.to_y().wait_send()
        for s in range(1, me.depth):
            self.to_z(s).wait_send()


def scatter_scratch(pieces, depth):
    out = []
    for rows, cols, dtype in pieces:
        for lead in ((depth, 2, 2), (depth, 2, 2), (3, depth), (depth - 1,)):
            out.append(pltpu.VMEM(lead + (rows, cols), dtype))
    return out


def perform(step, plan):
    for due in sorted(plan):

        @pl.when(step == due)
        def _(actions=plan[due]):
            for action in actions:
                action()


def due(plan, step, action):
    plan.setdefault(step, []).append(action)


def head_pair_masks():
    lanes = lax.broadcasted_iota(jnp.int32, (1, 128), 1)
    return (lanes < 64, lanes >= 64)


def attend_fwd_kernel(depth, pieces, *refs):
    ids, hs, q_ref, k_ref, v_ref = refs[:5]
    shards = refs[5:8]
    cot = refs[8]
    o_ref, mixed_ref, lse_ref = refs[9:12]
    wholes = refs[12:15]
    cot_whole = refs[15]
    vt, local, send, recv = refs[16:]
    pair = pl.program_id(0)
    me = Place(depth)
    half = cot.shape[1]
    gathers = [
        Gather(me, shards[a], wholes[a], at, count, local.at[n], send.at[n], recv.at[n])
        for n, (a, at, count) in enumerate(pieces)
    ]
    n = len(pieces)
    swap = Swap(
        me, cot.at[1 - me.y], lambda y: cot_whole.at[y], cot.at[me.y], cot_whole.at[me.y],
        local.at[n], send.at[n, 0], recv.at[n, 0],
    )
    plan = {}
    due(plan, 0, me.greet)
    for g in gathers:
        due(plan, 0, g.begin)
    due(plan, 10, swap.begin)
    for n, g in enumerate(gathers):
        due(plan, FWD_STEPS[0][n], g.spread)
        due(plan, FWD_STEPS[1][n], g.from_y)
        due(plan, FWD_STEPS[2][n], g.from_x)
        due(plan, FWD_STEPS[3][n], g.from_corner)
        due(plan, 31, g.end)
    due(plan, 31, swap.end)
    last = plan.pop(31)
    rows = q_ref.shape[0]
    blocks = rows // BLOCK
    factor = LOG2E / 8.0
    masks = head_pair_masks()
    gains = jnp.where(masks[0], hs[2 * pair], hs[2 * pair + 1])
    for j in range(blocks):
        vtr = v_ref[j * BLOCK : (j + 1) * BLOCK, :].astype(F32).T.astype(BF16)
        for h in range(2):
            vt[j, h, 0:64, :] = vtr[h * 64 : (h + 1) * 64]
            vt[j, h, 64:80, :] = jnp.ones((16, BLOCK), BF16)
    key_at = lax.broadcasted_iota(jnp.int32, (BLOCK, BLOCK), 0)
    query_at = lax.broadcasted_iota(jnp.int32, (BLOCK, BLOCK), 1)

    def one_query(i, _):
        perform(pair * blocks + i, plan)
        q = q_ref[pl.ds(i * BLOCK, BLOCK), :]
        qh = [jnp.where(m, q, jnp.zeros_like(q)) for m in masks]

        def step(kb, carry, diag):
            k = k_ref[pl.ds(kb * BLOCK, BLOCK), :]
            out = []
            for h in range(2):
                s = mm(k, qh[h], NT)
                if diag:
                    s = jnp.where(key_at <= query_at, s, NEG)
                    m = jnp.max(s, axis=0, keepdims=True)
                    p = jnp.exp2(s * factor - m * factor).astype(BF16)
                    out.append((m, mm(vt[kb, h], p)))
                else:
                    bias = jnp.where(ids[i] == ids[kb], 0.0, NEG)
                    m_old, acc = carry[h]
                    m = jnp.maximum(m_old, jnp.max(s, axis=0, keepdims=True) + bias)
                    p = jnp.exp2(s * factor - (m - bias) * factor).astype(BF16)
                    alpha = jnp.exp2((m_old - m) * factor)
                    out.append((m, acc * alpha + mm(vt[kb, h], p)))
            return tuple(out)

        carry = step(i, None, True)
        carry = lax.fori_loop(0, i, lambda kb, c: step(kb, c, False), carry)
        outs = []
        for h in range(2):
            m, acc = carry[h]
            total = acc[64:65]
            outs.append(acc[:64] / total)
            lse_ref[0, h, pl.ds(i, 1), :] = m * factor + jnp.log2(total)
        both = jnp.concatenate(outs, axis=0).T
        mixed_ref[pl.ds(i * BLOCK, BLOCK), :] = both
        o_ref[pl.ds(i * BLOCK, BLOCK), :] = (both * gains).astype(BF16)
        return 0

    lax.fori_loop(0, blocks, one_query, 0)
    perform(pair, {pl.num_programs(0) - 1: last})


def attend_fwd(qkv, ids, hs, shards, cot, depth, collective_id):
    rows, width3 = qkv.shape
    width = width3 // 3
    pairs = width // 128
    blocks = rows // BLOCK
    spec = lambda part: pl.BlockSpec((rows, 128), lambda p, part=part: (0, part * pairs + p))
    smem = pl.BlockSpec(memory_space=pltpu.SMEM)
    anywhere = pl.BlockSpec(memory_space=pl.ANY)
    pieces = [(0, 0, shards[0].shape[0])]
    for a in (1, 2):
        part = shards[a].shape[0] // 2
        pieces += [(a, 0, part), (a, part, part)]
    count = len(pieces) + 1
    out = pl.pallas_call(
        functools.partial(attend_fwd_kernel, depth, pieces),
        grid=(pairs,),
        in_specs=[smem, smem, spec(0), spec(1), spec(2)] + [anywhere] * 4,
        out_specs=[
            pl.BlockSpec((rows, 128), lambda p: (0, p)),
            pl.BlockSpec((rows, 128), lambda p: (0, p)),
            pl.BlockSpec((1, 2, blocks, BLOCK), lambda p: (p, 0, 0, 0)),
        ]
        + [anywhere] * 4,
        out_shape=[
            jax.ShapeDtypeStruct((rows, width), BF16),
            jax.ShapeDtypeStruct((rows, width), F32),
            jax.ShapeDtypeStruct((pairs, 2, blocks, BLOCK), F32),
        ]
        + [jax.ShapeDtypeStruct((depth, 2, 2, 2) + s.shape, s.dtype) for s in shards]
        + [jax.ShapeDtypeStruct(cot.shape, cot.dtype)],
        scratch_shapes=[
            pltpu.VMEM((blocks, 2, 80, BLOCK), BF16),
            pltpu.SemaphoreType.DMA((count,)),
            pltpu.SemaphoreType.DMA((count, 6 + depth)),
            pltpu.SemaphoreType.DMA((count, 6 + depth)),
        ],
        compiler_params=pltpu.CompilerParams(
            vmem_limit_bytes=VMEM_CAP, collective_id=collective_id, has_side_effects=True
        ),
        name="attend_fwd",
    )(ids, hs, qkv, qkv, qkv, *shards, cot)
    wholes = [w.reshape((depth * 8 * w.shape[4],) + w.shape[5:]) for w in out[3:6]]
    return out[0], out[1], out[2], wholes, out[6].reshape(rows, width)


def attend_bwd_kernel(depth, pieces, *refs):
    ids, hs, q_ref, k_ref, v_ref, o_ref, g_ref, lse_ref = refs[:8]
    parts = refs[8:11]
    layer = refs[11]
    dq_ref, dk_ref, dv_ref, delta_ref = refs[12:16]
    sums = refs[16:19]
    layer_out = refs[19]
    kt, dk_acc, dv_acc, local, send, recv = refs[20:26]
    scratch = refs[26:]
    pair = pl.program_id(0)
    me = Place(depth)
    scatters = [
        Scatter(
            me, parts[a], at, count, *scratch[4 * n : 4 * n + 4], local.at[n], send.at[n], recv.at[n], sums[a]
        )
        for n, (a, at, count) in enumerate(pieces)
    ]
    n = len(pieces)
    half = layer_out.shape[1]
    swap = Swap(
        me, layer.at[pl.ds((1 - me.y) * half, half)], lambda y: layer_out.at[y],
        layer.at[pl.ds(me.y * half, half)], layer_out.at[me.y], local.at[n], send.at[n, 0], recv.at[n, 0],
    )
    plan = {}
    due(plan, 0, me.greet)
    for s in scatters:
        due(plan, 0, s.begin)
    for n, s in enumerate(scatters):
        due(plan, BWD_STEPS[0][n], s.across)
        due(plan, BWD_STEPS[1][n], s.along_x)
        due(plan, BWD_STEPS[2][n], s.along_y)
        due(plan, BWD_STEPS[3][n], s.end)
    due(plan, 14, swap.begin)
    due(plan, 32, swap.end)
    last = plan.pop(32)
    rows = q_ref.shape[0]
    blocks = rows // BLOCK
    factor = LOG2E / 8.0
    masks = head_pair_masks()
    for j in range(blocks):
        kt[j] = k_ref[j * BLOCK : (j + 1) * BLOCK, :].astype(F32).T.astype(BF16)
    key_at = lax.broadcasted_iota(jnp.int32, (BLOCK, BLOCK), 0)
    query_at = lax.broadcasted_iota(jnp.int32, (BLOCK, BLOCK), 1)
    gains = jnp.where(masks[0], hs[2 * pair], hs[2 * pair + 1])
    picks = jnp.concatenate([m.astype(F32) for m in masks] + [jnp.zeros((6, 128), F32)], axis=0).astype(BF16)

    def one_query(i, _):
        perform(pair * blocks + i, plan)
        at = pl.ds(i * BLOCK, BLOCK)
        q = q_ref[at, :]
        g = (g_ref[at, :].astype(F32) * gains).astype(BF16)
        prod = g.astype(F32) * o_ref[at, :]
        hi = prod.astype(BF16)
        lo = (prod - hi.astype(F32)).astype(BF16)
        deltas = mm(picks, hi, NT) + mm(picks, lo, NT)
        qh = [jnp.where(m, q, jnp.zeros_like(q)) for m in masks]
        gh = [jnp.where(m, g, jnp.zeros_like(g)) for m in masks]
        delta = [deltas[h : h + 1] for h in range(2)]
        lse = [lse_ref[0, h, pl.ds(i, 1), :] for h in range(2)]
        for h in range(2):
            delta_ref[0, h, pl.ds(i, 1), :] = delta[h]

        def step(kb, carry, diag):
            ks = pl.ds(kb * BLOCK, BLOCK)
            k = k_ref[ks, :]
            v = v_ref[ks, :]
            out = []
            dk_part = None
            dv_part = None
            for h in range(2):
                s = mm(k, qh[h], NT)
                dp = mm(v, gh[h], NT)
                if diag:
                    p = jnp.exp2(s * factor - lse[h])
                    p = jnp.where(key_at <= query_at, p, 0.0)
                else:
                    bias = jnp.where(ids[i] == ids[kb], 0.0, -NEG)
                    p = jnp.exp2(s * factor - (lse[h] + bias))
                ds = (p * (dp - delta[h])).astype(BF16)
                dvh = mm(p.astype(BF16), gh[h])
                dkh = mm(ds, qh[h])
                dk_part = dkh if dk_part is None else dk_part + dkh
                dv_part = dvh if dv_part is None else dv_part + dvh
                dqh = mm(kt[kb, h * 64 : (h + 1) * 64, :], ds)
                out.append(dqh if diag else carry[h] + dqh)
            if diag:
                dk_acc[ks, :] = dk_part
                dv_acc[ks, :] = dv_part
            else:
                dk_acc[ks, :] += dk_part
                dv_acc[ks, :] += dv_part
            return tuple(out)

        carry = step(i, None, True)
        carry = lax.fori_loop(0, i, lambda kb, c: step(kb, c, False), carry)
        both = jnp.concatenate(carry, axis=0) * 0.125
        dq_ref[at, :] = both.T.astype(BF16)
        return 0

    lax.fori_loop(0, blocks, one_query, 0)
    dk_ref[...] = (dk_acc[...] * 0.125).astype(BF16)
    dv_ref[...] = dv_acc[...].astype(BF16)
    perform(pair, {pl.num_programs(0) - 1: last})


def shard_view(part, depth):
    return part.reshape((depth, 2, 2, 2, part.shape[0] // (depth * 8)) + part.shape[1:])


def attend_bwd(qkv, mixed, d_scaled, lse, ids, hs, parts, layer, depth, collective_id):
    rows, width3 = qkv.shape
    width = width3 // 3
    pairs = width // 128
    blocks = rows // BLOCK
    spec = lambda part: pl.BlockSpec((rows, 128), lambda p, part=part: (0, part * pairs + p))
    col = pl.BlockSpec((rows, 128), lambda p: (0, p))
    stat = pl.BlockSpec((1, 2, blocks, BLOCK), lambda p: (p, 0, 0, 0))
    smem = pl.BlockSpec(memory_space=pltpu.SMEM)
    anywhere = pl.BlockSpec(memory_space=pl.ANY)
    parts = [shard_view(p, depth) for p in parts]
    pieces = []
    for a in (0, 1):
        part = parts[a].shape[4] // 2
        pieces += [(a, 0, part), (a, part, part)]
    pieces.append((2, 0, parts[2].shape[4]))
    count = len(pieces) + 1
    out = pl.pallas_call(
        functools.partial(attend_bwd_kernel, depth, pieces),
        grid=(pairs,),
        in_specs=[smem, smem, spec(0), spec(1), spec(2), col, col, stat] + [anywhere] * 4,
        out_specs=[col, col, col, stat]
        + [pl.BlockSpec(p.shape[4:], lambda p: (0, 0)) for p in parts]
        + [anywhere],
        out_shape=[jax.ShapeDtypeStruct((rows, width), BF16)] * 3
        + [jax.ShapeDtypeStruct((pairs, 2, blocks, BLOCK), F32)]
        + [jax.ShapeDtypeStruct(p.shape[4:], F32) for p in parts]
        + [jax.ShapeDtypeStruct((2, rows // 2, width), BF16)],
        scratch_shapes=[
            pltpu.VMEM((blocks, 128, BLOCK), BF16),
            pltpu.VMEM((rows, 128), F32),
            pltpu.VMEM((rows, 128), F32),
            pltpu.SemaphoreType.DMA((count,)),
            pltpu.SemaphoreType.DMA((count, 3 + depth)),
            pltpu.SemaphoreType.DMA((count, 3 + depth)),
        ]
        + scatter_scratch([(count, parts[a].shape[5], parts[a].dtype) for a, _, count in pieces], depth),
        compiler_params=pltpu.CompilerParams(
            vmem_limit_bytes=VMEM_CAP, collective_id=collective_id, has_side_effects=True
        ),
        name="attend_bwd",
    )(ids, hs, qkv, qkv, qkv, mixed, d_scaled, lse, *parts, layer)
    return out[:4], out[4:7], out[7]


def row_norm(values):
    center = values - jnp.mean(values, axis=-1, keepdims=True)
    spread = jnp.mean(center * center, axis=-1, keepdims=True)
    rstd = lax.rsqrt(spread + EPS)
    return center * rstd, rstd


def row_norm_back(grad, hat, rstd):
    first = jnp.mean(grad, axis=-1, keepdims=True)
    second = jnp.mean(grad * hat, axis=-1, keepdims=True)
    return rstd * (grad - first - hat * second)


def fold_rows(values):
    return jnp.sum(values.reshape(values.shape[0] // 8, 8, values.shape[1]), axis=0)


def resident(shape):
    return pl.BlockSpec(shape, lambda i: (0,) * len(shape), pipeline_mode=pl.Buffered(1))


def qkv_kernel(x_ref, w_ref, p_ref, bias_ref, normed_ref, out_ref):
    hat, _ = row_norm(x_ref[...].astype(F32))
    normed = (hat * p_ref[0:1] + p_ref[1:2]).astype(BF16)
    normed_ref[...] = normed
    cols = out_ref.shape[1]
    for j in range(cols // 512):
        at = slice(j * 512, (j + 1) * 512)
        out_ref[:, at] = (mm(normed, w_ref[:, at]) + bias_ref[:, at]).astype(BF16)


def qkv_project(x, weight, params, bias):
    rows, width = x.shape
    cols = weight.shape[1]
    tile = 256
    return pl.pallas_call(
        qkv_kernel,
        grid=(rows // tile,),
        in_specs=[
            pl.BlockSpec((tile, width), lambda i: (i, 0)),
            resident(weight.shape),
            resident(params.shape),
            resident(bias.shape),
        ],
        out_specs=[
            pl.BlockSpec((tile, width), lambda i: (i, 0)),
            pl.BlockSpec((tile, cols), lambda i: (i, 0)),
        ],
        out_shape=[jax.ShapeDtypeStruct((rows, width), BF16), jax.ShapeDtypeStruct((rows, cols), BF16)],
        compiler_params=pltpu.CompilerParams(vmem_limit_bytes=VMEM_CAP),
        name="qkv_project",
    )(x, weight, params, bias)


GELU_A = math.sqrt(2.0 / math.pi)
GELU_B = 0.044715
CHUNK = 512


def middle_kernel(
    sc_ref, x_ref, dy_ref, wout, w1, w2, nar, wide,
    lay_ref, post_ref, fin_ref, act_ref, din_ref, dhid_ref, dlow_ref, dsc_ref, gn_ref, gw_ref,
    n_s, gp_s, dn_s,
):
    @pl.when(pl.program_id(0) == 0)
    def _():
        gn_ref[...] = jnp.zeros_like(gn_ref)
        gw_ref[...] = jnp.zeros_like(gw_ref)

    tile, width = x_ref.shape
    ff = w1.shape[1]
    chunks = ff // CHUNK
    ahat, arstd = row_norm(sc_ref[...].astype(F32))
    post = (ahat * nar[0:1] + nar[1:2]).astype(BF16)
    post_ref[...] = post
    hidden = x_ref[...].astype(F32) + mm(post, wout[...]) + nar[2:3]
    hhat, hrstd = row_norm(hidden)
    fin = (hhat * nar[3:4] + nar[4:5]).astype(BF16)
    fin_ref[...] = fin

    def lanes(values):
        return jnp.sum(values.reshape(tile, CHUNK // 128, 128), axis=1)

    def inner(j, total):
        at = pl.ds(pl.multiple_of(j * CHUNK, CHUNK), CHUNK)
        u = mm(fin, w1[:, at]) + wide[0:1, at]
        u2 = u * u
        t = jnp.tanh(u * (GELU_A + GELU_A * GELU_B * u2))
        half = 0.5 * (1.0 + t)
        n = u * half
        gp_s[:, at] = (half + n * (1.0 - t) * (GELU_A + 3.0 * GELU_A * GELU_B * u2)).astype(BF16)
        n_s[:, at] = n
        for q in range(CHUNK // 128):
            total = total + n[:, q * 128 : (q + 1) * 128]
        return total

    zero = jnp.zeros((tile, 128), F32)
    total = lax.fori_loop(0, chunks, inner, zero, unroll=2)
    nmean = jnp.sum(total, axis=-1, keepdims=True) / ff

    def square(j, total):
        at = pl.ds(pl.multiple_of(j * 128, 128), 128)
        c = n_s[:, at] - nmean
        return total + c * c

    total = lax.fori_loop(0, ff // 128, square, zero, unroll=4)
    nrstd = lax.rsqrt(jnp.sum(total, axis=-1, keepdims=True) / ff + EPS)
    dyl = dy_ref[...]

    def outer(j, carry):
        acc, s1, s2 = carry
        at = pl.ds(pl.multiple_of(j * CHUNK, CHUNK), CHUNK)
        nh = (n_s[:, at] - nmean) * nrstd
        n_s[:, at] = nh
        act = (nh * wide[1:2, at] + wide[2:3, at]).astype(BF16)
        act_ref[:, at] = act
        acc = acc + mm(act, w2[at, :])
        da = mm(dyl, w2[at, :], NT)
        danh = da * nh
        gw_ref[1, :, at] += fold_rows(danh)
        gw_ref[2, :, at] += fold_rows(da)
        gain = wide[1:2, at]
        dg = da * gain
        dgn = danh * gain
        dn_s[:, at] = dg
        for q in range(CHUNK // 128):
            s1 = s1 + dg[:, q * 128 : (q + 1) * 128]
            s2 = s2 + dgn[:, q * 128 : (q + 1) * 128]
        return acc, s1, s2

    acc, s1, s2 = lax.fori_loop(0, chunks, outer, (jnp.zeros((tile, width), F32), zero, zero), unroll=2)
    lay_ref[...] = (hidden + acc + nar[5:6]).astype(BF16)
    s1 = jnp.sum(s1, axis=-1, keepdims=True) / ff
    s2 = jnp.sum(s2, axis=-1, keepdims=True) / ff

    def inner_back(j, acc):
        at = pl.ds(pl.multiple_of(j * CHUNK, CHUNK), CHUNK)
        dn = nrstd * (dn_s[:, at] - s1 - n_s[:, at] * s2)
        din = (dn * gp_s[:, at].astype(F32)).astype(BF16)
        din_ref[:, at] = din
        gw_ref[0, :, at] += fold_rows(din.astype(F32))
        return acc + mm(din, w1[:, at], NT)

    dffn = lax.fori_loop(0, chunks, inner_back, jnp.zeros((tile, width), F32), unroll=2)
    dy = dyl.astype(F32)
    gn_ref[5] += fold_rows(dy)
    gn_ref[3] += fold_rows(dffn * hhat)
    gn_ref[4] += fold_rows(dffn)
    dhid = dy + row_norm_back(dffn * nar[3:4], hhat, hrstd)
    dhid_ref[...] = dhid
    gn_ref[2] += fold_rows(dhid)
    dlow = dhid.astype(BF16)
    dlow_ref[...] = dlow
    dpost = mm(dlow, wout[...], NT)
    gn_ref[0] += fold_rows(dpost * ahat)
    gn_ref[1] += fold_rows(dpost)
    dsc_ref[...] = row_norm_back(dpost * nar[0:1], ahat, arstd).astype(BF16)


def middle(scaled, x, dy, wout, w1, w2, narrow, wide):
    rows, width = x.shape
    ff = w1.shape[1]
    tile = 256
    thin = pl.BlockSpec((tile, width), lambda i: (i, 0))
    fat = pl.BlockSpec((tile, ff), lambda i: (i, 0))
    keep = lambda shape: pl.BlockSpec(shape, lambda i: (0,) * len(shape))
    return pl.pallas_call(
        middle_kernel,
        grid=(rows // tile,),
        in_specs=[
            thin, thin, thin,
            resident(wout.shape), resident(w1.shape), resident(w2.shape),
            resident(narrow.shape), resident(wide.shape),
        ],
        out_specs=[thin, thin, thin, fat, fat, thin, thin, thin, keep((6, 8, width)), keep((3, 8, ff))],
        out_shape=[
            jax.ShapeDtypeStruct((rows, width), BF16),
            jax.ShapeDtypeStruct((rows, width), BF16),
            jax.ShapeDtypeStruct((rows, width), BF16),
            jax.ShapeDtypeStruct((rows, ff), BF16),
            jax.ShapeDtypeStruct((rows, ff), BF16),
            jax.ShapeDtypeStruct((rows, width), F32),
            jax.ShapeDtypeStruct((rows, width), BF16),
            jax.ShapeDtypeStruct((rows, width), BF16),
            jax.ShapeDtypeStruct((6, 8, width), F32),
            jax.ShapeDtypeStruct((3, 8, ff), F32),
        ],
        scratch_shapes=[
            pltpu.VMEM((tile, ff), F32),
            pltpu.VMEM((tile, ff), BF16),
            pltpu.VMEM((tile, ff), F32),
        ],
        compiler_params=pltpu.CompilerParams(vmem_limit_bytes=VMEM_CAP),
        name="middle",
    )(scaled, x, dy, wout, w1, w2, narrow, wide)


def tail_kernel(dq_ref, dk_ref, dv_ref, x_ref, dhid_ref, w_ref, p_ref, out_ref, g_ref):
    @pl.when(pl.program_id(0) == 0)
    def _():
        g_ref[...] = jnp.zeros_like(g_ref)

    width = x_ref.shape[1]
    hat, rstd = row_norm(x_ref[...].astype(F32))
    dnormed = mm(dq_ref[...], w_ref[:, 0:width], NT)
    dnormed = dnormed + mm(dk_ref[...], w_ref[:, width : 2 * width], NT)
    dnormed = dnormed + mm(dv_ref[...], w_ref[:, 2 * width : 3 * width], NT)
    g_ref[0] += fold_rows(dnormed * hat)
    g_ref[1] += fold_rows(dnormed)
    g_ref[2] += fold_rows(dq_ref[...].astype(F32))
    g_ref[3] += fold_rows(dv_ref[...].astype(F32))
    out_ref[...] = dhid_ref[...] + row_norm_back(dnormed * p_ref[0:1], hat, rstd)


def tail(dq, dk, dv, x, dhid, weight, params):
    rows, width = x.shape
    tile = 256
    thin = pl.BlockSpec((tile, width), lambda i: (i, 0))
    return pl.pallas_call(
        tail_kernel,
        grid=(rows // tile,),
        in_specs=[thin] * 5 + [resident(weight.shape), resident(params.shape)],
        out_specs=[thin, pl.BlockSpec((4, 8, width), lambda i: (0, 0, 0))],
        out_shape=[jax.ShapeDtypeStruct((rows, width), F32), jax.ShapeDtypeStruct((4, 8, width), F32)],
        compiler_params=pltpu.CompilerParams(vmem_limit_bytes=VMEM_CAP),
        name="tail",
    )(dq, dk, dv, x, dhid, weight, params)


def enter_kernel(depth, pieces, *refs):
    shards = refs[:2]
    tok = refs[2]
    wholes = refs[3:5]
    tok_whole = refs[5]
    local, send, recv = refs[6:]
    me = Place(depth)
    gathers = [
        Gather(me, shards[a], wholes[a], at, count, local.at[n], send.at[n], recv.at[n])
        for n, (a, at, count) in enumerate(pieces)
    ]
    n = len(pieces)
    swap = Swap(
        me, tok.at[1 - me.y], lambda y: tok_whole.at[y], tok.at[me.y], tok_whole.at[me.y],
        local.at[n], send.at[n, 0], recv.at[n, 0],
    )
    me.greet()
    for g in gathers:
        g.begin()
    for g in gathers:
        g.spread()
    swap.begin()
    for g in gathers:
        g.from_y()
        g.from_x()
    for g in gathers:
        g.from_corner()
    for g in gathers:
        g.end()
    swap.end()


def enter(small, qkv_weight, tokens, depth, collective_id):
    shards = [small, qkv_weight]
    part = qkv_weight.shape[0] // 2
    pieces = [(0, 0, small.shape[0]), (1, 0, part), (1, part, part)]
    count = len(pieces) + 1
    anywhere = pl.BlockSpec(memory_space=pl.ANY)
    out = pl.pallas_call(
        functools.partial(enter_kernel, depth, pieces),
        in_specs=[anywhere] * 3,
        out_specs=[anywhere] * 3,
        out_shape=[jax.ShapeDtypeStruct((depth, 2, 2, 2) + s.shape, s.dtype) for s in shards]
        + [jax.ShapeDtypeStruct(tokens.shape, tokens.dtype)],
        scratch_shapes=[
            pltpu.SemaphoreType.DMA((count,)),
            pltpu.SemaphoreType.DMA((count, 6 + depth)),
            pltpu.SemaphoreType.DMA((count, 6 + depth)),
        ],
        compiler_params=pltpu.CompilerParams(
            collective_id=collective_id, has_side_effects=True, vmem_limit_bytes=1024 * 1024
        ),
        name="enter",
    )(small, qkv_weight, tokens)
    wholes = [w.reshape((depth * 8 * w.shape[4],) + w.shape[5:]) for w in out[:2]]
    return wholes[0], wholes[1], out[2].reshape(-1, tokens.shape[2])


def leave_kernel(depth, pieces, *refs):
    arrays = len(pieces)
    parts, sums = refs[:arrays], refs[arrays : 2 * arrays]
    local, send, recv = refs[2 * arrays : 2 * arrays + 3]
    scratch = refs[2 * arrays + 3 :]
    me = Place(depth)
    scatters = [
        Scatter(me, parts[n], 0, piece[0], *scratch[4 * n : 4 * n + 4], local.at[n], send.at[n], recv.at[n], sums[n])
        for n, piece in enumerate(pieces)
    ]
    me.greet()
    for s in scatters:
        s.begin()
    for s in scatters:
        s.across()
    for s in scatters:
        s.along_x()
    for s in scatters:
        s.along_y()
    for s in scatters:
        s.end()


def leave(parts, depth, collective_id):
    parts = [shard_view(p, depth) for p in parts]
    pieces = [(p.shape[4], p.shape[5], p.dtype) for p in parts]
    count = len(parts)
    anywhere = pl.BlockSpec(memory_space=pl.ANY)
    vmem = pl.BlockSpec(memory_space=pltpu.VMEM)
    return pl.pallas_call(
        functools.partial(leave_kernel, depth, pieces),
        in_specs=[anywhere] * count,
        out_specs=[vmem] * count,
        out_shape=[jax.ShapeDtypeStruct(p.shape[4:], F32) for p in parts],
        scratch_shapes=[
            pltpu.SemaphoreType.DMA((count,)),
            pltpu.SemaphoreType.DMA((count, 3 + depth)),
            pltpu.SemaphoreType.DMA((count, 3 + depth)),
        ]
        + scatter_scratch(pieces, depth),
        compiler_params=pltpu.CompilerParams(
            collective_id=collective_id, has_side_effects=True, vmem_limit_bytes=VMEM_CAP
        ),
        name="leave",
    )(*parts)


def fast_shards(
    tokens, doc_lengths, out_cotangent, in_gain, in_bias, qkv_weight, q_bias, v_bias, head_scale, attn_gain,
    attn_bias, out_weight, out_bias, ffn_gain, ffn_bias, fc1_weight, fc1_bias, mid_gain, mid_bias, fc2_weight,
    fc2_bias,
):
    depth = lax.axis_size("dp") // 4
    devices = depth * 8
    half = tokens.shape[1]
    rows = 2 * half
    width = tokens.shape[2]
    ff = fc1_weight.shape[1]
    me = lax.axis_index("sp")
    swap = [(0, 1), (1, 0)]

    narrow_in = [in_gain, in_bias, q_bias, v_bias, attn_gain, attn_bias, out_bias, ffn_gain, ffn_bias, fc2_bias]
    wide_in = [fc1_bias, mid_gain, mid_bias]
    part = width // devices
    wide_part = ff // devices
    small = jnp.concatenate(narrow_in + wide_in + [head_scale])
    used = small.shape[0]
    small_rows = 16
    small = jnp.pad(small, (0, small_rows * 128 - used)).reshape(small_rows, 128)
    small, wqkv, x = enter(small, qkv_weight, tokens, depth, 0)
    small = small.reshape(devices, small_rows * 128).astype(F32)
    nn = len(narrow_in)
    narrow = small[:, : nn * part].reshape(devices, nn, part).transpose(1, 0, 2).reshape(nn, width)
    base = nn * part
    wide = small[:, base : base + 3 * wide_part].reshape(devices, 3, wide_part).transpose(1, 0, 2).reshape(3, ff)
    base = base + 3 * wide_part
    heads_each = head_scale.shape[0]
    hs = small[0:2, base : base + heads_each].reshape(2 * heads_each)

    lengths = lax.dynamic_index_in_dim(doc_lengths[0], me, 0, keepdims=False)
    starts = jnp.arange(rows // BLOCK, dtype=jnp.int32) * BLOCK
    ids = jnp.sum((starts[:, None] >= jnp.cumsum(lengths)[None, :]).astype(jnp.int32), axis=1)

    in_params = narrow[0:2]
    bias_row = jnp.concatenate([narrow[2], jnp.zeros_like(narrow[2]), narrow[3]])[None, :]
    normed, qkv = qkv_project(x, wqkv, in_params, bias_row)
    scaled, mixed, lse, (wout, w1, w2), dy = attend_fwd(
        qkv, ids, hs, [out_weight, fc1_weight, fc2_weight], out_cotangent, depth, 1
    )
    layer, post, ffn_in, active, d_inner, d_hidden, d_low, d_scaled, grads_narrow, grads_wide = middle(
        scaled, x, dy, wout, w1, w2, narrow[4:10], wide
    )

    def weight_grad(left, right):
        return jnp.einsum("ti,tj->ij", left, right, preferred_element_type=F32).astype(BF16)

    g_fc2 = weight_grad(active, dy)
    g_fc1 = weight_grad(ffn_in, d_inner)
    g_out = weight_grad(post, d_low)
    (dq, dk, dv, delta), (s_fc2, s_fc1, s_out), layer_out = attend_bwd(
        qkv, mixed, d_scaled, lse, ids, hs, [g_fc2, g_fc1, g_out], layer, depth, 2
    )
    g_q = weight_grad(normed, dq)
    g_k = weight_grad(normed, dk)
    g_v = weight_grad(normed, dv)
    d_input, grads_in = tail(dq, dk, dv, x, d_hidden, wqkv, in_params)
    d_sent = lax.dynamic_slice_in_dim(d_input, (1 - me) * half, half, 0).astype(BF16)
    d_got = lax.ppermute(d_sent, "sp", swap).astype(F32)
    d_kept = lax.dynamic_slice_in_dim(d_input, me * half, half, 0)
    input_grad = jnp.stack([jnp.where(me == 0, d_kept, d_got), jnp.where(me == 0, d_got, d_kept)])

    hs_grad = jnp.sum(delta, axis=(2, 3)).reshape(-1) / hs
    narrow_grads = jnp.concatenate([jnp.sum(grads_in, axis=1), jnp.sum(grads_narrow, axis=1)], axis=0)
    wide_grads = jnp.sum(grads_wide, axis=1)
    packed = jnp.concatenate(
        [
            narrow_grads.reshape(nn, devices, part).transpose(1, 0, 2).reshape(devices, nn * part),
            wide_grads.reshape(3, devices, wide_part).transpose(1, 0, 2).reshape(devices, 3 * wide_part),
            jnp.tile(hs_grad.reshape(2, heads_each), (devices // 2, 1)),
        ],
        axis=1,
    )
    tiles = (used + 1023) // 1024 * 8
    packed = jnp.pad(packed, ((0, 0), (0, tiles * 128 - used))).reshape(devices * tiles, 128)
    s_q, s_k, s_v, s_small = leave([g_q, g_k, g_v, packed], depth, 3)
    s_small = s_small.reshape(-1)
    nar = [s_small[k * part : (k + 1) * part] for k in range(nn)]
    base = nn * part
    wid = [s_small[base + k * wide_part : base + (k + 1) * wide_part] for k in range(3)]
    base = base + 3 * wide_part
    s_hs = s_small[base : base + heads_each]
    return (
        layer_out, input_grad, nar[0], nar[1], jnp.concatenate([s_q, s_k, s_v], axis=1), nar[2], nar[3], s_hs,
        nar[4], nar[5], s_out, nar[6], nar[7], nar[8], s_fc1, wid[0], wid[1], wid[2], s_fc2, nar[9],
    )


LONGEST = 2048


def layer_norm(values, norm_gain, norm_shift):
    center = values - jnp.mean(values, axis=-1, keepdims=True)
    spread = jnp.mean(center * center, axis=-1, keepdims=True)
    return center * lax.rsqrt(spread + EPS) * norm_gain + norm_shift


def doc_index(lengths, row_count):
    seq_ends = jnp.cumsum(lengths)
    places = jnp.arange(row_count, dtype=jnp.int32)
    return jnp.sum((places[:, None] >= seq_ends[None, :]).astype(jnp.int32), axis=1)


def block_scores(query_block, key_heads, doc_query, doc_keys, pos_query, pos_keys, score_scale):
    scores = (
        jnp.einsum("qhd,khd->hqk", query_block, key_heads, preferred_element_type=jnp.float32)
        * score_scale
    )
    allowed = (doc_query[:, None] == doc_keys[None, :]) & (pos_keys[None, :] <= pos_query[:, None])
    return jnp.where(allowed[None], scores, -1e30)


def reduce_grads(grad_set):
    return (
        lax.psum_scatter(grad_set[0], ("dp", "sp"), scatter_dimension=0, tiled=True),
        lax.psum_scatter(grad_set[1], ("dp", "sp"), scatter_dimension=0, tiled=True),
        lax.psum_scatter(grad_set[2], ("dp", "sp"), scatter_dimension=0, tiled=True),
        lax.psum_scatter(grad_set[3], ("dp", "sp"), scatter_dimension=0, tiled=True),
        lax.psum_scatter(grad_set[4], ("dp", "sp"), scatter_dimension=0, tiled=True),
        lax.psum_scatter(grad_set[5], ("dp", "sp"), scatter_dimension=0, tiled=True),
        lax.psum_scatter(grad_set[6], ("dp", "sp"), scatter_dimension=0, tiled=True),
        lax.psum_scatter(grad_set[7], ("dp", "sp"), scatter_dimension=0, tiled=True),
        lax.psum_scatter(grad_set[8], ("dp", "sp"), scatter_dimension=0, tiled=True),
        lax.psum_scatter(grad_set[9], ("dp", "sp"), scatter_dimension=0, tiled=True),
        lax.psum_scatter(grad_set[10], ("dp", "sp"), scatter_dimension=0, tiled=True),
        lax.psum_scatter(grad_set[11], ("dp", "sp"), scatter_dimension=0, tiled=True),
        lax.psum_scatter(grad_set[12], ("dp", "sp"), scatter_dimension=0, tiled=True),
        lax.psum_scatter(grad_set[13], ("dp", "sp"), scatter_dimension=0, tiled=True),
        lax.psum_scatter(grad_set[14], ("dp", "sp"), scatter_dimension=0, tiled=True),
        lax.psum_scatter(grad_set[15], ("dp", "sp"), scatter_dimension=0, tiled=True),
        lax.psum_scatter(grad_set[16], ("dp", "sp"), scatter_dimension=0, tiled=True),
    )


def shards(
    tokens,
    doc_lengths,
    out_cotangent,
    in_gain,
    in_bias,
    qkv_weight,
    q_bias,
    v_bias,
    head_scale,
    attn_gain,
    attn_bias,
    out_weight,
    out_bias,
    ffn_gain,
    ffn_bias,
    fc1_weight,
    fc1_bias,
    mid_gain,
    mid_bias,
    fc2_weight,
    fc2_bias,
):
    micro_count = tokens.shape[0]
    tok_count = tokens.shape[1]
    model_width = tokens.shape[2]
    sp_count = lax.axis_size("sp")
    group_rows = tok_count * sp_count
    local_width = model_width // sp_count
    head_local = head_scale.shape[0]
    head_dim = local_width // head_local
    score_scale = 1.0 / math.sqrt(head_dim)
    window_rows = LONGEST
    block_rows = min(512, window_rows)
    block_count = group_rows // block_rows
    head_gains = head_scale.astype(jnp.float32)
    positions = jnp.arange(group_rows, dtype=jnp.int32)
    starts = jnp.arange(block_count, dtype=jnp.int32) * block_rows

    def collect():
        return (
            lax.all_gather(in_gain, ("dp", "sp"), axis=0, tiled=True),
            lax.all_gather(in_bias, ("dp", "sp"), axis=0, tiled=True),
            lax.all_gather(qkv_weight, ("dp", "sp"), axis=0, tiled=True),
            lax.all_gather(q_bias, ("dp", "sp"), axis=0, tiled=True),
            lax.all_gather(v_bias, ("dp", "sp"), axis=0, tiled=True),
            lax.all_gather(attn_gain, ("dp", "sp"), axis=0, tiled=True),
            lax.all_gather(attn_bias, ("dp", "sp"), axis=0, tiled=True),
            lax.all_gather(out_weight, ("dp", "sp"), axis=0, tiled=True),
            lax.all_gather(out_bias, ("dp", "sp"), axis=0, tiled=True),
            lax.all_gather(ffn_gain, ("dp", "sp"), axis=0, tiled=True),
            lax.all_gather(ffn_bias, ("dp", "sp"), axis=0, tiled=True),
            lax.all_gather(fc1_weight, ("dp", "sp"), axis=0, tiled=True),
            lax.all_gather(fc1_bias, ("dp", "sp"), axis=0, tiled=True),
            lax.all_gather(mid_gain, ("dp", "sp"), axis=0, tiled=True),
            lax.all_gather(mid_bias, ("dp", "sp"), axis=0, tiled=True),
            lax.all_gather(fc2_weight, ("dp", "sp"), axis=0, tiled=True),
            lax.all_gather(fc2_bias, ("dp", "sp"), axis=0, tiled=True),
        )

    def split_heads(heads_in):
        query_heads = heads_in[:, 0].reshape(group_rows, head_local, head_dim)
        key_heads = heads_in[:, 1].reshape(group_rows, head_local, head_dim)
        value_heads = heads_in[:, 2].reshape(group_rows, head_local, head_dim)
        return (query_heads, key_heads, value_heads)

    def attend_back(heads_in, lengths, log_total, grad_mixed):
        query_heads, key_heads, value_heads = split_heads(heads_in)
        doc_ids = doc_index(lengths, group_rows)

        def one_block(block_carry, pair):
            grad_keys, grad_values = block_carry
            row_start, block_lse = pair
            query_block = lax.dynamic_slice_in_dim(query_heads, row_start, block_rows, 0)
            grad_block = lax.dynamic_slice_in_dim(grad_mixed, row_start, block_rows, 0)
            masked = block_scores(
                query_block,
                key_heads,
                lax.dynamic_slice_in_dim(doc_ids, row_start, block_rows, 0),
                doc_ids,
                lax.dynamic_slice_in_dim(positions, row_start, block_rows, 0),
                positions,
                score_scale,
            )
            prob_rows = jnp.exp(masked - block_lse[:, :, None])
            value_part = jnp.einsum(
                "hqk,qhd->khd",
                prob_rows.astype(jnp.bfloat16),
                grad_block,
                preferred_element_type=jnp.float32,
            )
            grad_probs = jnp.einsum(
                "qhd,khd->hqk", grad_block, value_heads, preferred_element_type=jnp.float32
            )
            row_inner = jnp.sum(prob_rows * grad_probs, axis=-1, keepdims=True)
            grad_scores = (prob_rows * (grad_probs - row_inner)).astype(jnp.bfloat16)
            grad_query = (
                jnp.einsum(
                    "hqk,khd->qhd", grad_scores, key_heads, preferred_element_type=jnp.float32
                )
                * score_scale
            )
            key_part = jnp.einsum(
                "hqk,qhd->khd", grad_scores, query_block, preferred_element_type=jnp.float32
            )
            grad_keys = grad_keys + key_part
            grad_values = grad_values + value_part
            return ((grad_keys, grad_values), grad_query)

        zero_heads = jnp.zeros((group_rows, head_local, head_dim), jnp.float32)
        (grad_keys, grad_values), grad_queries = lax.scan(
            one_block, (zero_heads, zero_heads), (starts, log_total)
        )
        stacked = jnp.stack(
            [
                grad_queries.reshape(group_rows, local_width),
                (grad_keys * score_scale).reshape(group_rows, local_width),
                grad_values.reshape(group_rows, local_width),
            ],
            axis=1,
        )
        return stacked.astype(jnp.bfloat16)

    outputs = []
    input_grads = []
    total_grads = None
    scale_total = jnp.zeros((head_local,), jnp.float32)
    for micro_index in range(micro_count):
        forward_set = collect()
        (
            forward_wide_in_gain,
            forward_wide_in_bias,
            forward_wide_qkv,
            forward_wide_q_bias,
            forward_wide_v_bias,
            forward_wide_attn_gain,
            forward_wide_attn_bias,
            forward_wide_out,
            forward_wide_out_bias,
            forward_wide_ffn_gain,
            forward_wide_ffn_bias,
            forward_wide_fc1,
            forward_wide_fc1_bias,
            forward_wide_mid_gain,
            forward_wide_mid_bias,
            forward_wide_fc2,
            forward_wide_fc2_bias,
        ) = forward_set
        forward_tok_rows = tokens[micro_index].astype(jnp.float32)
        forward_lengths = doc_lengths[0, micro_index]
        forward_normed = layer_norm(
            forward_tok_rows,
            forward_wide_in_gain.astype(jnp.float32),
            forward_wide_in_bias.astype(jnp.float32),
        ).astype(jnp.bfloat16)
        bias_row = jnp.concatenate(
            [forward_wide_q_bias, jnp.zeros_like(forward_wide_q_bias), forward_wide_v_bias]
        ).astype(jnp.float32)
        projected = (
            jnp.dot(forward_normed, forward_wide_qkv, preferred_element_type=jnp.float32) + bias_row
        )
        qkv_sent = projected.astype(jnp.bfloat16).reshape(tok_count, 3, model_width)
        forward_heads_in = lax.all_to_all(qkv_sent, "sp", split_axis=2, concat_axis=0, tiled=True)
        attend_query_heads, attend_key_heads, attend_value_heads = split_heads(forward_heads_in)
        attend_doc_ids = doc_index(forward_lengths, group_rows)

        def attend_one_block(row_start):
            query_block = lax.dynamic_slice_in_dim(attend_query_heads, row_start, block_rows, 0)
            masked = block_scores(
                query_block,
                attend_key_heads,
                lax.dynamic_slice_in_dim(attend_doc_ids, row_start, block_rows, 0),
                attend_doc_ids,
                lax.dynamic_slice_in_dim(positions, row_start, block_rows, 0),
                positions,
                score_scale,
            )
            row_max = jnp.max(masked, axis=-1, keepdims=True)
            raised = jnp.exp(masked - row_max)
            row_total = jnp.sum(raised, axis=-1, keepdims=True)
            prob_rows = (raised / row_total).astype(jnp.bfloat16)
            head_mixed = jnp.einsum(
                "hqk,khd->qhd", prob_rows, attend_value_heads, preferred_element_type=jnp.float32
            )
            return (head_mixed, (row_max + jnp.log(row_total))[:, :, 0])

        head_mixed, attend_log_total = lax.map(attend_one_block, starts)
        forward_head_mixed = head_mixed.reshape(group_rows, head_local, head_dim)
        scaled = (
            (forward_head_mixed * head_gains[None, :, None])
            .reshape(group_rows, local_width)
            .astype(jnp.bfloat16)
        )
        forward_attn_rows = lax.all_to_all(
            scaled, "sp", split_axis=0, concat_axis=1, tiled=True
        ).astype(jnp.float32)
        forward_post_norm = layer_norm(
            forward_attn_rows,
            forward_wide_attn_gain.astype(jnp.float32),
            forward_wide_attn_bias.astype(jnp.float32),
        ).astype(jnp.bfloat16)
        forward_hidden = (
            forward_tok_rows
            + jnp.dot(forward_post_norm, forward_wide_out, preferred_element_type=jnp.float32)
            + forward_wide_out_bias.astype(jnp.float32)
        )
        forward_ffn_in = layer_norm(
            forward_hidden,
            forward_wide_ffn_gain.astype(jnp.float32),
            forward_wide_ffn_bias.astype(jnp.float32),
        ).astype(jnp.bfloat16)
        forward_ffn_inner = jnp.dot(
            forward_ffn_in, forward_wide_fc1, preferred_element_type=jnp.float32
        ) + forward_wide_fc1_bias.astype(jnp.float32)
        forward_active = layer_norm(
            jax.nn.gelu(forward_ffn_inner),
            forward_wide_mid_gain.astype(jnp.float32),
            forward_wide_mid_bias.astype(jnp.float32),
        ).astype(jnp.bfloat16)
        output = (
            forward_hidden
            + jnp.dot(forward_active, forward_wide_fc2, preferred_element_type=jnp.float32)
            + forward_wide_fc2_bias.astype(jnp.float32)
        )
        forward_kept_values = (
            forward_normed,
            forward_heads_in,
            forward_head_mixed,
            attend_log_total,
            forward_attn_rows,
            forward_post_norm,
            forward_hidden,
            forward_ffn_in,
            forward_ffn_inner,
            forward_active,
        )
        output, kept_values = (output, forward_kept_values)
        backward_set = collect()
        (
            wide_in_gain,
            wide_in_bias,
            wide_qkv,
            wide_q_bias,
            wide_v_bias,
            wide_attn_gain,
            wide_attn_bias,
            wide_out,
            wide_out_bias,
            wide_ffn_gain,
            wide_ffn_bias,
            wide_fc1,
            wide_fc1_bias,
            wide_mid_gain,
            wide_mid_bias,
            wide_fc2,
            wide_fc2_bias,
        ) = backward_set
        (
            normed,
            backward_heads_in,
            backward_head_mixed,
            backward_log_total,
            attn_rows,
            post_norm,
            hidden,
            ffn_in,
            ffn_inner,
            active,
        ) = kept_values
        tok_rows = tokens[micro_index].astype(jnp.float32)
        backward_lengths = doc_lengths[0, micro_index]
        grad_out = out_cotangent[micro_index].astype(jnp.float32)
        fc2_bias_grad = jnp.sum(grad_out, axis=0)
        grad_low = grad_out.astype(jnp.bfloat16)
        fc2_grad = jnp.einsum("ti,tj->ij", active, grad_low, preferred_element_type=jnp.float32)
        grad_active = jnp.einsum(
            "tj,ij->ti", grad_low, wide_fc2, preferred_element_type=jnp.float32
        )
        gelu_out, gelu_back = jax.vjp(jax.nn.gelu, ffn_inner)
        _, mid_back = jax.vjp(
            layer_norm,
            gelu_out,
            wide_mid_gain.astype(jnp.float32),
            wide_mid_bias.astype(jnp.float32),
        )
        grad_gelu, mid_gain_grad, mid_bias_grad = mid_back(grad_active)
        (grad_inner,) = gelu_back(grad_gelu)
        inner_low = grad_inner.astype(jnp.bfloat16)
        fc1_bias_grad = jnp.sum(inner_low.astype(jnp.float32), axis=0)
        fc1_grad = jnp.einsum("ti,tj->ij", ffn_in, inner_low, preferred_element_type=jnp.float32)
        grad_ffn = jnp.einsum("tj,ij->ti", inner_low, wide_fc1, preferred_element_type=jnp.float32)
        _, ffn_back = jax.vjp(
            layer_norm, hidden, wide_ffn_gain.astype(jnp.float32), wide_ffn_bias.astype(jnp.float32)
        )
        grad_hid, ffn_gain_grad, ffn_bias_grad = ffn_back(grad_ffn)
        grad_hidden = grad_out + grad_hid
        out_bias_grad = jnp.sum(grad_hidden, axis=0)
        hidden_low = grad_hidden.astype(jnp.bfloat16)
        out_grad = jnp.einsum(
            "ti,tj->ij", post_norm, hidden_low, preferred_element_type=jnp.float32
        )
        grad_post = jnp.einsum(
            "tj,ij->ti", hidden_low, wide_out, preferred_element_type=jnp.float32
        )
        _, attn_back = jax.vjp(
            layer_norm,
            attn_rows,
            wide_attn_gain.astype(jnp.float32),
            wide_attn_bias.astype(jnp.float32),
        )
        grad_attn, attn_gain_grad, attn_bias_grad = attn_back(grad_post)
        grad_heads = lax.all_to_all(
            grad_attn.astype(jnp.bfloat16), "sp", split_axis=1, concat_axis=0, tiled=True
        )
        grad_scaled = grad_heads.astype(jnp.float32).reshape(group_rows, head_local, head_dim)
        scale_grad = jnp.sum(grad_scaled * backward_head_mixed, axis=(0, 2))
        backward_grad_mixed = (grad_scaled * head_gains[None, :, None]).astype(jnp.bfloat16)
        grad_qkv = attend_back(
            backward_heads_in, backward_lengths, backward_log_total, backward_grad_mixed
        )
        returned = lax.all_to_all(grad_qkv, "sp", split_axis=0, concat_axis=2, tiled=True).reshape(
            tok_count, 3 * model_width
        )
        column_sums = jnp.sum(returned.astype(jnp.float32), axis=0)
        q_bias_grad = column_sums[:model_width]
        v_bias_grad = column_sums[2 * model_width :]
        qkv_grad = jnp.einsum("ti,tj->ij", normed, returned, preferred_element_type=jnp.float32)
        grad_normed = jnp.einsum(
            "tj,ij->ti", returned, wide_qkv, preferred_element_type=jnp.float32
        )
        _, in_back = jax.vjp(
            layer_norm, tok_rows, wide_in_gain.astype(jnp.float32), wide_in_bias.astype(jnp.float32)
        )
        grad_rows, in_gain_grad, in_bias_grad = in_back(grad_normed)
        input_grad = grad_hidden + grad_rows
        grad_set = (
            in_gain_grad,
            in_bias_grad,
            qkv_grad,
            q_bias_grad,
            v_bias_grad,
            attn_gain_grad,
            attn_bias_grad,
            out_grad,
            out_bias_grad,
            ffn_gain_grad,
            ffn_bias_grad,
            fc1_grad,
            fc1_bias_grad,
            mid_gain_grad,
            mid_bias_grad,
            fc2_grad,
            fc2_bias_grad,
        )
        input_grad, grad_set, scale_grad = (input_grad, grad_set, scale_grad)
        grad_set = reduce_grads(grad_set)
        total_grads = (
            grad_set if total_grads is None else jax.tree.map(jnp.add, total_grads, grad_set)
        )
        scale_total = scale_total + scale_grad
        outputs.append(output)
        input_grads.append(input_grad)
    scale_sum = lax.psum(scale_total, "dp")
    layer_out = jnp.stack(outputs).astype(jnp.bfloat16)
    input_grad = jnp.stack(input_grads)
    return (
        layer_out,
        input_grad,
        total_grads[0],
        total_grads[1],
        total_grads[2],
        total_grads[3],
        total_grads[4],
        scale_sum,
        total_grads[5],
        total_grads[6],
        total_grads[7],
        total_grads[8],
        total_grads[9],
        total_grads[10],
        total_grads[11],
        total_grads[12],
        total_grads[13],
        total_grads[14],
        total_grads[15],
        total_grads[16],
    )


def solution(mesh):
    body = fast_shards if mesh.shape["sp"] == 2 and mesh.shape["dp"] % 4 == 0 and mesh.shape["dp"] >= 8 else shards
    return jax.shard_map(
        body,
        mesh=mesh,
        in_specs=(
            P(None, ("dp", "sp"), None),
            P("dp", None, None),
            P(None, ("dp", "sp"), None),
            P(("dp", "sp")),
            P(("dp", "sp")),
            P(("dp", "sp"), None),
            P(("dp", "sp")),
            P(("dp", "sp")),
            P("sp"),
            P(("dp", "sp")),
            P(("dp", "sp")),
            P(("dp", "sp"), None),
            P(("dp", "sp")),
            P(("dp", "sp")),
            P(("dp", "sp")),
            P(("dp", "sp"), None),
            P(("dp", "sp")),
            P(("dp", "sp")),
            P(("dp", "sp")),
            P(("dp", "sp"), None),
            P(("dp", "sp")),
        ),
        out_specs=(
            P(None, ("dp", "sp"), None),
            P(None, ("dp", "sp"), None),
            P(("dp", "sp")),
            P(("dp", "sp")),
            P(("dp", "sp"), None),
            P(("dp", "sp")),
            P(("dp", "sp")),
            P("sp"),
            P(("dp", "sp")),
            P(("dp", "sp")),
            P(("dp", "sp"), None),
            P(("dp", "sp")),
            P(("dp", "sp")),
            P(("dp", "sp")),
            P(("dp", "sp"), None),
            P(("dp", "sp")),
            P(("dp", "sp")),
            P(("dp", "sp")),
            P(("dp", "sp"), None),
            P(("dp", "sp")),
        ),
        check_vma=False,
    )
```

```python
import functools
import math

import jax
import jax.numpy as jnp
from jax import lax
from jax.experimental import pallas as pl
from jax.experimental.pallas import tpu as pltpu
from jax.sharding import PartitionSpec as P

EPS = 1e-05
BLOCK = 512
LOG2E = math.log2(math.e)
NEG = -1e30
F32 = jnp.float32
BF16 = jnp.bfloat16
VMEM_CAP = 60 * 1024 * 1024
NT = (((1,), (1,)), ((), ()))
NN = (((1,), (0,)), ((), ()))
FWD_STEPS = ((0, 0, 10, 11), (11, 12, 28, 29), (20, 21, 30, 31), (24, 25, 32, 32))
BWD_STEPS = ((1, 2, 3, 4, 5), (9, 15, 20, 26, 28), (14, 19, 24, 29, 30), (18, 23, 28, 32, 32))


def mm(a, b, dims=NN):
    return lax.dot_general(a, b, dims, preferred_element_type=F32)


def same_sequence(lengths, y):
    ends = []
    for k in range(lengths.shape[2]):
        ends.append(lengths[0, y, k] + (ends[-1] if ends else 0))

    def same(i, kb):
        between = [((e > kb * BLOCK) & (e <= i * BLOCK)).astype(jnp.int32) for e in ends]
        return sum(between) == 0

    return same


class Place:
    def __init__(self, depth):
        d = lax.axis_index("dp")
        self.depth = depth
        self.y = lax.axis_index("sp")
        self.c = d % 2
        self.x = (d // 2) % 2
        self.z = d // 4
        self.next_y = self.device(self.z, self.x, self.c, 1 - self.y)
        self.next_x = self.device(self.z, 1 - self.x, self.c, self.y)
        self.twin = self.device(self.z, self.x, 1 - self.c, self.y)

    def device(self, z, x, c, y):
        return ((z * 2 + x) * 2 + c, y)

    def along(self, step):
        return (self.z + step) % self.depth

    def column(self, step):
        return self.device(self.along(step), self.x, self.c, self.y)

    def greet(self):
        barrier = pltpu.get_barrier_semaphore()
        peers = [self.column(s) for s in range(1, self.depth)] + [self.next_x, self.next_y, self.twin]
        for peer in peers:
            pl.semaphore_signal(barrier, inc=1, device_id=peer, device_id_type=pl.DeviceIdType.MESH)
        pl.semaphore_wait(barrier, len(peers))


def remote(src, dst, send, recv, peer):
    return pltpu.make_async_remote_copy(
        src_ref=src, dst_ref=dst, send_sem=send, recv_sem=recv, device_id=peer, device_id_type=pl.DeviceIdType.MESH
    )


class Gather:
    def __init__(self, me, shard, stage, whole, at, count, local, send, recv):
        self.me, self.whole = me, whole
        if shard is not None:
            self.shard, self.stage = shard.at[pl.ds(at, count)], stage.at[pl.ds(at, count)]
        self.rows = pl.ds(at, count)
        self.local, self.send, self.recv = local, send, recv

    def own(self, z):
        me = self.me
        return self.whole.at[z, me.x, me.c, me.y, self.rows]

    def load(self):
        return pltpu.make_async_copy(self.shard, self.stage, self.local)

    def keep(self):
        return pltpu.make_async_copy(self.stage, self.own(self.me.z), self.local)

    def depth_hop(self, s, landed):
        me = self.me
        z = me.along(me.depth - s) if landed else me.z
        return remote(self.stage, self.own(z), self.send.at[6 + s], self.recv.at[6 + s], me.column(s))

    def hop(self, x, y, n, peer, c=None):
        group = self.whole.at[:, x, self.me.c if c is None else c, y, self.rows]
        return remote(group, group, self.send.at[n], self.recv.at[n], peer)

    def path(self, n, c=None):
        me = self.me
        x, y = me.x, me.y
        gx = 1 - x if n in (5, 6) else x
        gy = 1 - y if n in (2, 4, 6) else y
        peer = me.next_y if n == 0 else me.next_x if n < 3 else me.twin
        return self.hop(gx, gy, n, peer, c)

    def ready(self):
        self.load().start()

    def begin(self):
        self.load().wait()
        self.keep().start()
        for s in range(1, self.me.depth):
            self.depth_hop(s, False).start()

    def landed(self):
        self.keep().wait()
        for s in range(1, self.me.depth):
            self.depth_hop(s, True).wait()

    def launch(self):
        for n in (0, 1, 3):
            self.path(n).start()

    def spread(self):
        self.landed()
        self.launch()

    def from_y(self):
        me = self.me
        self.hop(me.x, 1 - me.y, 0, me.next_y).wait_recv()
        self.path(2).start()
        self.path(4).start()

    def from_x(self):
        me = self.me
        self.hop(1 - me.x, me.y, 1, me.next_x).wait_recv()
        self.path(5).start()

    def from_corner(self):
        me = self.me
        self.hop(1 - me.x, 1 - me.y, 2, me.next_x).wait_recv()
        self.path(6).start()

    def end(self):
        for n in range(7):
            self.path(n).wait_send()
        for n in range(3, 7):
            self.path(n, 1 - self.me.c).wait_recv()


class Swap:
    def __init__(self, me, sent, landing, kept, stage, place, local, send, recv):
        self.out = remote(sent, landing(me.y), send, recv, me.next_y)
        self.into = remote(sent, landing(1 - me.y), send, recv, me.next_y)
        self.load = pltpu.make_async_copy(kept, stage, local)
        self.keep = pltpu.make_async_copy(stage, place, local)

    def ready(self):
        self.load.start()

    def begin(self):
        self.out.start()
        self.load.wait()
        self.keep.start()

    def end(self):
        self.out.wait_send()
        self.into.wait_recv()
        self.keep.wait()


def add_group(own, x, y, taken):
    def body(s, _):
        own[s, x, y] = (own[s, x, y].astype(F32) + taken(s).astype(F32)).astype(own.dtype)
        return 0

    lax.fori_loop(0, own.shape[0], body, 0)


class Scatter:
    def __init__(self, me, part, at, count, own, got0, got1, got3, local, send, recv, total):
        self.me, self.part, self.rows = me, part, pl.ds(at, count)
        self.own, self.got0, self.got1, self.got3 = own, got0, got1, got3
        self.local, self.send, self.recv, self.total = local, send, recv, total

    def mine(self):
        return pltpu.make_async_copy(self.part.at[:, :, self.me.c, :, self.rows], self.own, self.local)

    def halves(self):
        return remote(
            self.part.at[:, :, 1 - self.me.c, :, self.rows], self.got0, self.send.at[0], self.recv.at[0], self.me.twin
        )

    def to_x(self, n):
        me = self.me
        y = me.y if n == 0 else 1 - me.y
        return remote(self.own.at[:, 1 - me.x, y], self.got1.at[n], self.send.at[1 + n], self.recv.at[1 + n], me.next_x)

    def to_y(self):
        me = self.me
        return remote(self.own.at[:, me.x, 1 - me.y], self.got1.at[2], self.send.at[3], self.recv.at[3], me.next_y)

    def to_z(self, s):
        me = self.me
        return remote(
            self.own.at[me.along(s), me.x, me.y], self.got3.at[s - 1], self.send.at[3 + s], self.recv.at[3 + s],
            me.column(s),
        )

    def begin(self):
        self.mine().start()
        self.halves().start()

    def across(self):
        me, own, got = self.me, self.own, self.got0
        self.mine().wait()
        self.halves().wait()
        for n, x, y in ((1, 1 - me.x, 1 - me.y), (0, 1 - me.x, me.y)):
            add_group(own, x, y, lambda s: got[s, x, y])
            self.to_x(n).start()
        for x, y in ((me.x, 1 - me.y), (me.x, me.y)):
            add_group(own, x, y, lambda s: got[s, x, y])

    def along_x(self):
        me, own, got = self.me, self.own, self.got1
        self.to_x(1).wait_recv()
        add_group(own, me.x, 1 - me.y, lambda s: got[1, s])
        self.to_y().start()
        self.to_x(0).wait_recv()
        add_group(own, me.x, me.y, lambda s: got[0, s])

    def along_y(self):
        me, own, got = self.me, self.own, self.got1
        self.to_y().wait_recv()
        add_group(own, me.x, me.y, lambda s: got[2, s])
        for s in range(1, me.depth):
            self.to_z(s).start()

    def end(self):
        me = self.me
        total = self.own[me.z, me.x, me.y].astype(F32)
        for s in range(1, me.depth):
            self.to_z(s).wait_recv()
            total = total + self.got3[s - 1].astype(F32)
        self.total[self.rows] = total
        self.to_x(0).wait_send()
        self.to_x(1).wait_send()
        self.to_y().wait_send()
        for s in range(1, me.depth):
            self.to_z(s).wait_send()


def scatter_scratch(pieces, depth):
    out = []
    for rows, cols, dtype in pieces:
        for lead in ((depth, 2, 2), (depth, 2, 2), (3, depth), (depth - 1,)):
            out.append(pltpu.VMEM(lead + (rows, cols), dtype))
    return out


def perform(step, plan):
    for due in sorted(plan):

        @pl.when(step == due)
        def _(actions=plan[due]):
            for action in actions:
                action()


def due(plan, step, action):
    plan.setdefault(step, []).append(action)


def head_pair_masks():
    lanes = lax.broadcasted_iota(jnp.int32, (1, 128), 1)
    return (lanes < 64, lanes >= 64)


def attend_fwd_kernel(depth, pieces, *refs):
    lengths, hs, q_ref, k_ref, v_ref = refs[:5]
    shard, cot = refs[6:8]
    o_ref, mixed_ref, lse_ref = refs[8:11]
    wholes = refs[11:13]
    cot_whole = refs[13]
    vt, local, send, recv, shard_stage, cot_stage = refs[14:]
    pair = pl.program_id(0)
    me = Place(depth)
    same = same_sequence(lengths, me.y)
    gathers = [
        Gather(me, shard if a else None, shard_stage, wholes[a], at, count, local.at[n], send.at[n], recv.at[n])
        for n, (a, at, count) in enumerate(pieces)
    ]
    n = len(pieces)
    swap = Swap(
        me, cot.at[1 - me.y], lambda y: cot_whole.at[y], cot.at[me.y], cot_stage, cot_whole.at[me.y],
        local.at[n], send.at[n, 0], recv.at[n, 0],
    )
    plan = {}
    due(plan, 0, me.greet)
    due(plan, 0, swap.ready)
    for n, g in enumerate(gathers):
        if pieces[n][0]:
            due(plan, 0, g.ready)
    for n, g in enumerate(gathers):
        due(plan, 0, g.begin if pieces[n][0] else g.launch)
        if pieces[n][0]:
            due(plan, FWD_STEPS[0][n], g.spread)
        due(plan, FWD_STEPS[1][n], g.from_y)
        due(plan, FWD_STEPS[2][n], g.from_x)
        due(plan, FWD_STEPS[3][n], g.from_corner)
        due(plan, 32, g.end)
    due(plan, 6, swap.begin)
    due(plan, 32, swap.end)
    last = plan.pop(32)
    rows = q_ref.shape[0]
    blocks = rows // BLOCK
    factor = LOG2E / 8.0
    masks = head_pair_masks()
    gains = jnp.where(masks[0], hs[0, 2 * pair], hs[0, 2 * pair + 1])
    for j in range(blocks):
        vtr = v_ref[j * BLOCK : (j + 1) * BLOCK, :].astype(F32).T.astype(BF16)
        for h in range(2):
            vt[j, h, 0:64, :] = vtr[h * 64 : (h + 1) * 64]
            vt[j, h, 64:80, :] = jnp.ones((16, BLOCK), BF16)
    key_at = lax.broadcasted_iota(jnp.int32, (BLOCK, BLOCK), 0)
    query_at = lax.broadcasted_iota(jnp.int32, (BLOCK, BLOCK), 1)

    def one_query(i):
        perform(pair, {k // blocks: plan[k] for k in plan if k % blocks == i})
        q = q_ref[pl.ds(i * BLOCK, BLOCK), :]
        qh = [jnp.where(m, q, jnp.zeros_like(q)) for m in masks]

        def step(kb, carry, diag):
            k = k_ref[pl.ds(kb * BLOCK, BLOCK), :]
            out = []
            for h in range(2):
                s = mm(k, qh[h], NT)
                if diag:
                    s = jnp.where(key_at <= query_at, s, NEG)
                    m = jnp.max(s, axis=0, keepdims=True)
                    p = jnp.exp2(s * factor - m * factor).astype(BF16)
                    out.append((m, mm(vt[kb, h], p)))
                else:
                    bias = jnp.where(same(i, kb), 0.0, NEG)
                    m_old, acc = carry[h]
                    m = jnp.maximum(m_old, jnp.max(s, axis=0, keepdims=True) + bias)
                    p = jnp.exp2(s * factor - (m - bias) * factor).astype(BF16)
                    alpha = jnp.exp2((m_old - m) * factor)
                    out.append((m, acc * alpha + mm(vt[kb, h], p)))
            return tuple(out)

        carry = step(i, None, True)
        for kb in range(i):
            carry = step(kb, carry, False)
        outs = []
        for h in range(2):
            m, acc = carry[h]
            total = acc[64:65]
            outs.append(acc[:64] / total)
            lse_ref[0, h, pl.ds(i, 1), :] = m * factor + jnp.log2(total)
        both = jnp.concatenate(outs, axis=0).T
        mixed_ref[pl.ds(i * BLOCK, BLOCK), :] = both
        o_ref[pl.ds(i * BLOCK, BLOCK), :] = (both * gains).astype(BF16)

    for i in range(blocks):
        one_query(i)
    perform(pair, {pl.num_programs(0) - 1: last})


def attend_fwd(qkv, lengths, hs, begun, shard, cot, depth, collective_id):
    rows, width3 = qkv.shape
    width = width3 // 3
    pairs = width // 128
    blocks = rows // BLOCK
    spec = lambda part: pl.BlockSpec((rows, 128), lambda p, part=part: (0, part * pairs + p))
    smem = pl.BlockSpec(memory_space=pltpu.SMEM)
    anywhere = pl.BlockSpec(memory_space=pl.ANY)
    pieces = []
    for a, count in enumerate((begun.shape[4], shard.shape[0])):
        part = count // 2
        pieces += [(a, 0, part), (a, part, part)]
    count = len(pieces) + 1
    out = pl.pallas_call(
        functools.partial(attend_fwd_kernel, depth, pieces),
        grid=(pairs,),
        in_specs=[smem, smem, spec(0), spec(1), spec(2)] + [anywhere] * 3,
        out_specs=[
            pl.BlockSpec((rows, 128), lambda p: (0, p)),
            pl.BlockSpec((rows, 128), lambda p: (0, p)),
            pl.BlockSpec((1, 2, blocks, BLOCK), lambda p: (p, 0, 0, 0)),
        ]
        + [anywhere] * 3,
        out_shape=[
            jax.ShapeDtypeStruct((rows, width), BF16),
            jax.ShapeDtypeStruct((rows, width), F32),
            jax.ShapeDtypeStruct((pairs, 2, blocks, BLOCK), F32),
            jax.ShapeDtypeStruct(begun.shape, begun.dtype),
            jax.ShapeDtypeStruct((depth, 2, 2, 2) + shard.shape, shard.dtype),
            jax.ShapeDtypeStruct(cot.shape, cot.dtype),
        ],
        input_output_aliases={5: 3},
        scratch_shapes=[
            pltpu.VMEM((blocks, 2, 80, BLOCK), BF16),
            pltpu.SemaphoreType.DMA((count,)),
            pltpu.SemaphoreType.DMA((count, 6 + depth)),
            pltpu.SemaphoreType.DMA((count, 6 + depth)),
            pltpu.VMEM(shard.shape, shard.dtype),
            pltpu.VMEM(cot.shape[1:], cot.dtype),
        ],
        compiler_params=pltpu.CompilerParams(
            vmem_limit_bytes=VMEM_CAP, collective_id=collective_id, has_side_effects=True
        ),
        name="attend_fwd",
    )(lengths, hs, qkv, qkv, qkv, begun, shard, cot)
    return out[0], out[1], out[2], out[3], out[4], out[5].reshape(rows, width)


def attend_bwd_kernel(depth, pieces, *refs):
    lengths, hs, q_ref, k_ref, v_ref, o_ref, g_ref, lse_ref = refs[:8]
    parts = refs[8:11]
    layer = refs[11]
    dq_ref, dk_ref, dv_ref, delta_ref = refs[12:16]
    sums = refs[16:19]
    layer_out = refs[19]
    kt, dk_acc, dv_acc, local, send, recv, layer_stage = refs[20:27]
    scratch = refs[27:]
    pair = pl.program_id(0)
    me = Place(depth)
    same = same_sequence(lengths, me.y)
    scatters = [
        Scatter(
            me, parts[a], at, count, *scratch[4 * n : 4 * n + 4], local.at[n], send.at[n], recv.at[n], sums[a]
        )
        for n, (a, at, count) in enumerate(pieces)
    ]
    n = len(pieces)
    half = layer_out.shape[1]
    swap = Swap(
        me, layer.at[pl.ds((1 - me.y) * half, half)], lambda y: layer_out.at[y],
        layer.at[pl.ds(me.y * half, half)], layer_stage, layer_out.at[me.y], local.at[n], send.at[n, 0], recv.at[n, 0],
    )
    plan = {}
    due(plan, 0, swap.ready)
    due(plan, 0, me.greet)
    for s in scatters:
        due(plan, 0, s.begin)
    for n, s in enumerate(scatters):
        due(plan, BWD_STEPS[0][n], s.across)
        due(plan, BWD_STEPS[1][n], s.along_x)
        due(plan, BWD_STEPS[2][n], s.along_y)
        due(plan, BWD_STEPS[3][n], s.end)
    due(plan, 0, swap.begin)
    due(plan, 32, swap.end)
    last = plan.pop(32)
    rows = q_ref.shape[0]
    blocks = rows // BLOCK
    factor = LOG2E / 8.0
    masks = head_pair_masks()
    for j in range(blocks):
        kt[j] = k_ref[j * BLOCK : (j + 1) * BLOCK, :].astype(F32).T.astype(BF16)
    key_at = lax.broadcasted_iota(jnp.int32, (BLOCK, BLOCK), 0)
    query_at = lax.broadcasted_iota(jnp.int32, (BLOCK, BLOCK), 1)
    gains = jnp.where(masks[0], hs[0, 2 * pair], hs[0, 2 * pair + 1])
    picks = jnp.concatenate([m.astype(F32) for m in masks] + [jnp.zeros((6, 128), F32)], axis=0).astype(BF16)

    def one_query(i):
        perform(pair, {k // blocks: plan[k] for k in plan if k % blocks == i})
        at = pl.ds(i * BLOCK, BLOCK)
        q = q_ref[at, :]
        g = (g_ref[at, :].astype(F32) * gains).astype(BF16)
        prod = g.astype(F32) * o_ref[at, :]
        hi = prod.astype(BF16)
        lo = (prod - hi.astype(F32)).astype(BF16)
        deltas = mm(picks, hi, NT) + mm(picks, lo, NT)
        qh = [jnp.where(m, q, jnp.zeros_like(q)) for m in masks]
        gh = [jnp.where(m, g, jnp.zeros_like(g)) for m in masks]
        delta = [deltas[h : h + 1] for h in range(2)]
        lse = [lse_ref[0, h, pl.ds(i, 1), :] for h in range(2)]
        for h in range(2):
            delta_ref[0, h, pl.ds(i, 1), :] = delta[h]

        def step(kb, carry, diag):
            ks = pl.ds(kb * BLOCK, BLOCK)
            k = k_ref[ks, :]
            v = v_ref[ks, :]
            out = []
            dk_part = None
            dv_part = None
            for h in range(2):
                s = mm(k, qh[h], NT)
                dp = mm(v, gh[h], NT)
                if diag:
                    p = jnp.exp2(s * factor - lse[h])
                    p = jnp.where(key_at <= query_at, p, 0.0)
                else:
                    bias = jnp.where(same(i, kb), 0.0, -NEG)
                    p = jnp.exp2(s * factor - (lse[h] + bias))
                ds = (p * (dp - delta[h])).astype(BF16)
                dvh = mm(p.astype(BF16), gh[h])
                dkh = mm(ds, qh[h])
                dk_part = dkh if dk_part is None else dk_part + dkh
                dv_part = dvh if dv_part is None else dv_part + dvh
                dqh = mm(kt[kb, h * 64 : (h + 1) * 64, :], ds)
                out.append(dqh if diag else carry[h] + dqh)
            if diag:
                dk_acc[ks, :] = dk_part
                dv_acc[ks, :] = dv_part
            else:
                dk_acc[ks, :] += dk_part
                dv_acc[ks, :] += dv_part
            return tuple(out)

        carry = step(i, None, True)
        for kb in range(i):
            carry = step(kb, carry, False)
        both = jnp.concatenate(carry, axis=0) * 0.125
        dq_ref[at, :] = both.T.astype(BF16)

    for i in range(blocks):
        one_query(i)
    dk_ref[...] = (dk_acc[...] * 0.125).astype(BF16)
    dv_ref[...] = dv_acc[...].astype(BF16)
    perform(pair, {pl.num_programs(0) - 1: last})


def shard_view(part, depth):
    return part.reshape((depth, 2, 2, 2, part.shape[0] // (depth * 8)) + part.shape[1:])


def attend_bwd(qkv, mixed, d_scaled, lse, lengths, hs, parts, layer, depth, collective_id):
    rows, width3 = qkv.shape
    width = width3 // 3
    pairs = width // 128
    blocks = rows // BLOCK
    spec = lambda part: pl.BlockSpec((rows, 128), lambda p, part=part: (0, part * pairs + p))
    col = pl.BlockSpec((rows, 128), lambda p: (0, p))
    stat = pl.BlockSpec((1, 2, blocks, BLOCK), lambda p: (p, 0, 0, 0))
    smem = pl.BlockSpec(memory_space=pltpu.SMEM)
    anywhere = pl.BlockSpec(memory_space=pl.ANY)
    parts = [shard_view(p, depth) for p in parts]
    pieces = []
    for a in (0, 1):
        part = parts[a].shape[4] // 2
        pieces += [(a, 0, part), (a, part, part)]
    pieces.append((2, 0, parts[2].shape[4]))
    count = len(pieces) + 1
    out = pl.pallas_call(
        functools.partial(attend_bwd_kernel, depth, pieces),
        grid=(pairs,),
        in_specs=[smem, smem, spec(0), spec(1), spec(2), col, col, stat] + [anywhere] * 4,
        out_specs=[col, col, col, stat]
        + [pl.BlockSpec(p.shape[4:], lambda p: (0, 0)) for p in parts]
        + [anywhere],
        out_shape=[jax.ShapeDtypeStruct((rows, width), BF16)] * 3
        + [jax.ShapeDtypeStruct((pairs, 2, blocks, BLOCK), F32)]
        + [jax.ShapeDtypeStruct(p.shape[4:], F32) for p in parts]
        + [jax.ShapeDtypeStruct((2, rows // 2, width), BF16)],
        scratch_shapes=[
            pltpu.VMEM((blocks, 128, BLOCK), BF16),
            pltpu.VMEM((rows, 128), F32),
            pltpu.VMEM((rows, 128), F32),
            pltpu.SemaphoreType.DMA((count,)),
            pltpu.SemaphoreType.DMA((count, 3 + depth)),
            pltpu.SemaphoreType.DMA((count, 3 + depth)),
            pltpu.VMEM((rows // 2, width), BF16),
        ]
        + scatter_scratch([(count, parts[a].shape[5], parts[a].dtype) for a, _, count in pieces], depth),
        compiler_params=pltpu.CompilerParams(
            vmem_limit_bytes=VMEM_CAP, collective_id=collective_id, has_side_effects=True
        ),
        name="attend_bwd",
    )(lengths, hs, qkv, qkv, qkv, mixed, d_scaled, lse, *parts, layer)
    return out[:4], out[4:7], out[7]


def row_norm(values):
    center = values - jnp.mean(values, axis=-1, keepdims=True)
    spread = jnp.mean(center * center, axis=-1, keepdims=True)
    rstd = lax.rsqrt(spread + EPS)
    return center * rstd, rstd


def row_norm_back(grad, hat, rstd):
    first = jnp.mean(grad, axis=-1, keepdims=True)
    second = jnp.mean(grad * hat, axis=-1, keepdims=True)
    return rstd * (grad - first - hat * second)


def fold_rows(values):
    return jnp.sum(values.reshape(values.shape[0] // 8, 8, values.shape[1]), axis=0)


def resident(shape):
    return pl.BlockSpec(shape, lambda i: (0,) * len(shape), pipeline_mode=pl.Buffered(1))


def qkv_kernel(x_ref, w_ref, p_ref, normed_ref, out_ref):
    hat, _ = row_norm(x_ref[...].astype(F32))
    normed = (hat * p_ref[0:1] + p_ref[1:2]).astype(BF16)
    normed_ref[...] = normed
    cols = out_ref.shape[1]
    width = x_ref.shape[1]
    for j in range(cols // 512):
        at = slice(j * 512, (j + 1) * 512)
        part = mm(normed, w_ref[:, at])
        third, start = j * 512 // width, j * 512 % width
        if third != 1:
            row = 2 + third // 2
            part = part + p_ref[row : row + 1, start : start + 512]
        out_ref[:, at] = part.astype(BF16)


def qkv_project(x, weight, params):
    rows, width = x.shape
    cols = weight.shape[1]
    tile = 256
    return pl.pallas_call(
        qkv_kernel,
        grid=(rows // tile,),
        in_specs=[
            pl.BlockSpec((tile, width), lambda i: (i, 0)),
            resident(weight.shape),
            resident(params.shape),
        ],
        out_specs=[
            pl.BlockSpec((tile, width), lambda i: (i, 0)),
            pl.BlockSpec((tile, cols), lambda i: (i, 0)),
        ],
        out_shape=[jax.ShapeDtypeStruct((rows, width), BF16), jax.ShapeDtypeStruct((rows, cols), BF16)],
        compiler_params=pltpu.CompilerParams(vmem_limit_bytes=VMEM_CAP),
        name="qkv_project",
    )(x, weight, params)


GELU_A = math.sqrt(2.0 / math.pi)
GELU_B = 0.044715
CHUNK = 512


def middle_kernel(
    sc_ref, x_ref, dy_ref, wout, w1, w2, nar, wide,
    lay_ref, post_ref, fin_ref, act_ref, din_ref, dhid_ref, dlow_ref, dsc_ref, gn_ref, gw_ref,
    n_s, gp_s, dn_s,
):
    @pl.when(pl.program_id(0) == 0)
    def _():
        gn_ref[...] = jnp.zeros_like(gn_ref)
        gw_ref[...] = jnp.zeros_like(gw_ref)

    tile, width = x_ref.shape
    ff = w1.shape[1]
    chunks = ff // CHUNK
    ahat, arstd = row_norm(sc_ref[...].astype(F32))
    post = (ahat * nar[4:5] + nar[5:6]).astype(BF16)
    post_ref[...] = post
    hidden = x_ref[...].astype(F32) + mm(post, wout[...]) + nar[6:7]
    hhat, hrstd = row_norm(hidden)
    fin = (hhat * nar[7:8] + nar[8:9]).astype(BF16)
    fin_ref[...] = fin

    def lanes(values):
        return jnp.sum(values.reshape(tile, CHUNK // 128, 128), axis=1)

    def inner(j, total):
        at = pl.ds(pl.multiple_of(j * CHUNK, CHUNK), CHUNK)
        u = mm(fin, w1[:, at]) + wide[0:1, at]
        u2 = u * u
        t = jnp.tanh(u * (GELU_A + GELU_A * GELU_B * u2))
        half = 0.5 * (1.0 + t)
        n = u * half
        gp_s[:, at] = (half + n * (1.0 - t) * (GELU_A + 3.0 * GELU_A * GELU_B * u2)).astype(BF16)
        n_s[:, at] = n
        for q in range(CHUNK // 128):
            total = total + n[:, q * 128 : (q + 1) * 128]
        return total

    zero = jnp.zeros((tile, 128), F32)
    total = lax.fori_loop(0, chunks, inner, zero, unroll=8)
    nmean = jnp.sum(total, axis=-1, keepdims=True) / ff

    def square(j, total):
        at = pl.ds(pl.multiple_of(j * 128, 128), 128)
        c = n_s[:, at] - nmean
        return total + c * c

    total = lax.fori_loop(0, ff // 128, square, zero, unroll=4)
    nrstd = lax.rsqrt(jnp.sum(total, axis=-1, keepdims=True) / ff + EPS)
    dyl = dy_ref[...]

    def outer(j, carry):
        acc, s1, s2 = carry
        at = pl.ds(pl.multiple_of(j * CHUNK, CHUNK), CHUNK)
        nh = (n_s[:, at] - nmean) * nrstd
        n_s[:, at] = nh
        act = (nh * wide[1:2, at] + wide[2:3, at]).astype(BF16)
        act_ref[:, at] = act
        acc = acc + mm(act, w2[at, :])
        da = mm(dyl, w2[at, :], NT)
        danh = da * nh
        gw_ref[1, :, at] += fold_rows(danh)
        gw_ref[2, :, at] += fold_rows(da)
        gain = wide[1:2, at]
        dg = da * gain
        dgn = danh * gain
        dn_s[:, at] = dg
        for q in range(CHUNK // 128):
            s1 = s1 + dg[:, q * 128 : (q + 1) * 128]
            s2 = s2 + dgn[:, q * 128 : (q + 1) * 128]
        return acc, s1, s2

    acc, s1, s2 = lax.fori_loop(0, chunks, outer, (jnp.zeros((tile, width), F32), zero, zero), unroll=8)
    lay_ref[...] = (hidden + acc + nar[9:10]).astype(BF16)
    s1 = jnp.sum(s1, axis=-1, keepdims=True) / ff
    s2 = jnp.sum(s2, axis=-1, keepdims=True) / ff

    def inner_back(j, acc):
        at = pl.ds(pl.multiple_of(j * CHUNK, CHUNK), CHUNK)
        dn = nrstd * (dn_s[:, at] - s1 - n_s[:, at] * s2)
        din = (dn * gp_s[:, at].astype(F32)).astype(BF16)
        din_ref[:, at] = din
        gw_ref[0, :, at] += fold_rows(din.astype(F32))
        return acc + mm(din, w1[:, at], NT)

    dffn = lax.fori_loop(0, chunks, inner_back, jnp.zeros((tile, width), F32), unroll=8)
    dy = dyl.astype(F32)
    gn_ref[5] += fold_rows(dy)
    gn_ref[3] += fold_rows(dffn * hhat)
    gn_ref[4] += fold_rows(dffn)
    dhid = dy + row_norm_back(dffn * nar[7:8], hhat, hrstd)
    dhid_ref[...] = dhid
    gn_ref[2] += fold_rows(dhid)
    dlow = dhid.astype(BF16)
    dlow_ref[...] = dlow
    dpost = mm(dlow, wout[...], NT)
    gn_ref[0] += fold_rows(dpost * ahat)
    gn_ref[1] += fold_rows(dpost)
    dsc_ref[...] = row_norm_back(dpost * nar[4:5], ahat, arstd).astype(BF16)


def middle(scaled, x, dy, wout, w1, w2, narrow, wide):
    rows, width = x.shape
    ff = w1.shape[1]
    tile = 256
    thin = pl.BlockSpec((tile, width), lambda i: (i, 0))
    fat = pl.BlockSpec((tile, ff), lambda i: (i, 0))
    keep = lambda shape: pl.BlockSpec(shape, lambda i: (0,) * len(shape))
    return pl.pallas_call(
        middle_kernel,
        grid=(rows // tile,),
        in_specs=[
            thin, thin, thin,
            resident(wout.shape), resident(w1.shape), resident(w2.shape),
            resident(narrow.shape), resident(wide.shape),
        ],
        out_specs=[thin, thin, thin, fat, fat, thin, thin, thin, keep((6, 8, width)), keep((3, 8, ff))],
        out_shape=[
            jax.ShapeDtypeStruct((rows, width), BF16),
            jax.ShapeDtypeStruct((rows, width), BF16),
            jax.ShapeDtypeStruct((rows, width), BF16),
            jax.ShapeDtypeStruct((rows, ff), BF16),
            jax.ShapeDtypeStruct((rows, ff), BF16),
            jax.ShapeDtypeStruct((rows, width), F32),
            jax.ShapeDtypeStruct((rows, width), BF16),
            jax.ShapeDtypeStruct((rows, width), BF16),
            jax.ShapeDtypeStruct((6, 8, width), F32),
            jax.ShapeDtypeStruct((3, 8, ff), F32),
        ],
        scratch_shapes=[
            pltpu.VMEM((tile, ff), F32),
            pltpu.VMEM((tile, ff), BF16),
            pltpu.VMEM((tile, ff), F32),
        ],
        compiler_params=pltpu.CompilerParams(vmem_limit_bytes=VMEM_CAP),
        name="middle",
    )(scaled, x, dy, wout, w1, w2, narrow, wide)


def enter_kernel(depth, pieces, counts, *refs):
    me = Place(depth)
    smalls = refs[: len(counts)]
    shards = [None] + list(refs[len(counts) : len(counts) + 3])
    tok = refs[len(counts) + 3]
    wholes = list(refs[len(counts) + 4 : len(counts) + 7])
    tok_whole, narrow, wide, hs = refs[len(counts) + 7 : len(counts) + 11]
    small, small_whole, local, send, recv, small_sem, tok_stage = refs[len(counts) + 11 : len(counts) + 18]
    stages = list(refs[len(counts) + 18 : len(counts) + 22])
    smalls_here = refs[len(counts) + 22 :]
    copies = [pltpu.make_async_copy(s, h, small_sem.at[n]) for n, (s, h) in enumerate(zip(smalls, smalls_here))]
    for copy in copies:
        copy.start()
    for copy in copies:
        copy.wait()
    shards[0] = small
    wholes = [small_whole] + wholes
    rows = []
    for ref, count in zip(smalls_here, counts):
        row = ref[...].astype(F32).reshape(1, count)
        rows.append(row if count == 128 else jnp.concatenate([row, jnp.zeros((1, 128 - count), F32)], axis=1))
    rows.append(jnp.zeros((16 - len(counts), 128), F32))
    small[...] = jnp.concatenate(rows, axis=0).astype(BF16)
    gathers = [
        Gather(me, shards[a], stages[a], wholes[a], at, count, local.at[n], send.at[n], recv.at[n])
        for n, (a, at, count) in enumerate(pieces)
    ]
    first, later, begun = gathers[:3], gathers[3], gathers[4:]
    half = tok.shape[1]
    cut = half * 3 // 8
    swaps = []
    for n, (at, count) in enumerate(((0, cut), (cut, half - cut))):
        span = pl.ds(at, count)
        n = len(pieces) + n
        swaps.append(
            Swap(
                me, tok.at[1 - me.y, span], lambda y, span=span: tok_whole.at[y, span], tok.at[me.y, span],
                tok_stage.at[span], tok_whole.at[me.y, span], local.at[n], send.at[n, 0], recv.at[n, 0],
            )
        )
    for g in gathers + swaps:
        g.ready()
    me.greet()
    swaps[0].begin()
    for g in first:
        g.begin()
    for g in first:
        g.spread()
    swaps[1].begin()
    for g in [later] + begun:
        g.begin()
    for g in first:
        g.from_y()
    later.spread()
    for g in first:
        g.from_x()
    for g in first:
        g.from_corner()
    first[0].end()
    part = counts[0]
    each = 128 // part
    for d in range(depth * 8 // each):
        tiles = []
        for k in range(d * each, (d + 1) * each):
            tile = small_whole[k // 8, k // 4 % 2, k // 2 % 2, k % 2].astype(F32)
            tiles.append(tile[:, 0:part])
            wide[0:3, k * 128 : (k + 1) * 128] = tile[10:13]
        narrow[:, d * 128 : (d + 1) * 128] = jnp.concatenate(tiles, axis=1)
    hs[...] = jnp.concatenate(
        [small_whole[0, 0, 0, y].astype(F32)[13:14, 0 : counts[13]] for y in range(2)], axis=1
    )
    later.from_y()
    later.from_x()
    later.from_corner()
    for g in begun:
        g.landed()
    for g in first[1:]:
        g.end()
    later.end()
    for swap in swaps:
        swap.end()


def enter(smalls, qkv_weight, out_weight, fc1_weight, tokens, depth, collective_id):
    shards = [qkv_weight, out_weight, fc1_weight]
    counts = [s.shape[0] for s in smalls]
    pieces = [(0, 0, 16)]
    for a in (1, 2, 3):
        rows = shards[a - 1].shape[0]
        pieces += [(a, 0, rows)] if a == 2 else [(a, 0, rows // 2), (a, rows // 2, rows // 2)]
    count = len(pieces) + 2
    anywhere = pl.BlockSpec(memory_space=pl.ANY)
    vmem = pl.BlockSpec(memory_space=pltpu.VMEM)
    out = pl.pallas_call(
        functools.partial(enter_kernel, depth, pieces, counts),
        in_specs=[anywhere] * (len(counts) + 4),
        out_specs=[anywhere] * 4 + [vmem] * 3,
        out_shape=[jax.ShapeDtypeStruct((depth, 2, 2, 2) + s.shape, s.dtype) for s in shards]
        + [
            jax.ShapeDtypeStruct(tokens.shape, tokens.dtype),
            jax.ShapeDtypeStruct((16, depth * 8 * counts[0]), F32),
            jax.ShapeDtypeStruct((8, depth * 8 * counts[10]), F32),
            jax.ShapeDtypeStruct((1, 2 * counts[13]), F32),
        ],
        scratch_shapes=[
            pltpu.VMEM((16, 128), BF16),
            pltpu.VMEM((depth, 2, 2, 2, 16, 128), BF16),
            pltpu.SemaphoreType.DMA((count,)),
            pltpu.SemaphoreType.DMA((count, 6 + depth)),
            pltpu.SemaphoreType.DMA((count, 6 + depth)),
            pltpu.SemaphoreType.DMA((len(counts),)),
            pltpu.VMEM(tokens.shape[1:], tokens.dtype),
        ]
        + [pltpu.VMEM((16, 128), BF16)]
        + [pltpu.VMEM(s.shape, s.dtype) for s in shards]
        + [pltpu.VMEM((n,), BF16) for n in counts],
        compiler_params=pltpu.CompilerParams(
            collective_id=collective_id, has_side_effects=True, vmem_limit_bytes=VMEM_CAP
        ),
        name="enter",
    )(*smalls, *shards, tokens)
    return flat(out[0]), flat(out[1]), out[2], out[3].reshape(-1, tokens.shape[2]), out[4], out[5], out[6]


def flat(whole):
    return whole.reshape((-1,) + whole.shape[5:])


def leave_kernel(depth, part, heads, *refs):
    dq_ref, dk_ref, dv_ref, x_ref, dhid_ref, w_ref, p_ref = refs[:7]
    parts = refs[7:10]
    thin_ref, fat_ref, delta_ref, hs_ref = refs[10:14]
    out, qkv_sum, small_sum = refs[14:17]
    local, send, recv, go, come, store, g_acc, thin, fat, small, leaving, landing, stage = refs[17:30]
    scratch = refs[30:]
    me = Place(depth)
    step = pl.program_id(0)
    half_tiles = leaving.shape[0]
    tile, width = x_ref.shape
    rows = parts[0].shape[4]
    scatters = [
        Scatter(
            me, parts[n], 0, rows, *scratch[4 * n : 4 * n + 4], local.at[n], send.at[n], recv.at[n],
            qkv_sum.at[:, pl.ds(n * width, width)],
        )
        for n in range(3)
    ]
    smalls = Scatter(me, small, 0, 16, *scratch[12:16], local.at[3], send.at[3], recv.at[3], small_sum)

    def trade(j):
        return remote(leaving.at[j], landing.at[j], go.at[j], come.at[j], me.next_y)

    def put(y, j):
        return pltpu.make_async_copy(stage.at[j], out.at[y, pl.ds(j * tile, tile)], store.at[j])

    @pl.when(step == 0)
    def _():
        g_acc[...] = jnp.zeros_like(g_acc)
        me.greet()
        for s in scatters:
            s.begin()

    @pl.when(step == 2)
    def _():
        for s in scatters:
            s.across()

    hat, rstd = row_norm(x_ref[...].astype(F32))
    dnormed = mm(dq_ref[...], w_ref[:, 0:width], NT)
    dnormed = dnormed + mm(dk_ref[...], w_ref[:, width : 2 * width], NT)
    dnormed = dnormed + mm(dv_ref[...], w_ref[:, 2 * width : 3 * width], NT)
    g_acc[0] += fold_rows(dnormed * hat)
    g_acc[1] += fold_rows(dnormed)
    g_acc[2] += fold_rows(dq_ref[...].astype(F32))
    g_acc[3] += fold_rows(dv_ref[...].astype(F32))
    grad = dhid_ref[...] + row_norm_back(dnormed * p_ref[0:1], hat, rstd)

    @pl.when(step < half_tiles)
    def _():
        leaving[step] = grad.astype(BF16)
        trade(step).start()

    @pl.when(step >= half_tiles)
    def _():
        stage[step - half_tiles] = grad
        put(me.y, step - half_tiles).start()

    @pl.when(step == pl.num_programs(0) - 1)
    def _():
        thin[...] = jnp.zeros_like(thin)
        fat[...] = jnp.zeros_like(fat)
        for k in range(4):
            thin[k : k + 1, :] = jnp.sum(g_acc[k], axis=0, keepdims=True)
        for k in range(6):
            thin[4 + k : 5 + k, :] = jnp.sum(thin_ref[k], axis=0, keepdims=True)
        for k in range(3):
            fat[10 + k : 11 + k, :] = jnp.sum(fat_ref[k], axis=0, keepdims=True)
        lanes = lax.broadcasted_iota(jnp.int32, (1, 128), 1)
        scale = jnp.zeros((1, 128), F32)
        for p in range(delta_ref.shape[0]):
            for h in range(2):
                scale = jnp.where(lanes == 2 * p + h, jnp.sum(delta_ref[p, h]), scale)
        scale = scale / jnp.concatenate([hs_ref[...], jnp.ones((1, 128 - 2 * heads), F32)], axis=1)
        each = 128 // part
        is_scale = lax.broadcasted_iota(jnp.int32, (16, 128), 0) == 13
        for d in range(depth * 8):
            block = thin[:, d // each * 128 : (d // each + 1) * 128]
            turn = d % each * part
            block = pltpu.roll(block, 128 - turn, 1) if turn else block
            block = block + fat[:, d * 128 : (d + 1) * 128]
            row = pltpu.roll(scale, 128 - heads, 1) if d % 2 else scale
            small[d // 8, d // 4 % 2, d // 2 % 2, d % 2] = jnp.where(is_scale, row, block)
        smalls.begin()
        v, k, q = scatters[2], scatters[1], scatters[0]
        v.along_x()
        smalls.across()
        k.along_x()
        v.along_y()
        smalls.along_x()
        q.along_x()
        k.along_y()
        smalls.along_y()
        v.end()
        q.along_y()
        for j in range(half_tiles):
            trade(j).wait()
            put(me.y, j).wait()
            stage[j] = landing[j].astype(F32)
            put(1 - me.y, j).start()
        k.end()
        smalls.end()
        q.end()
        for j in range(half_tiles):
            put(1 - me.y, j).wait()


def leave(dq, dk, dv, x, dhid, weight, params, parts, thin, fat, delta, hs, depth, collective_id):
    rows, width = x.shape
    tile = 256
    tiles = rows // tile
    parts = [shard_view(p, depth) for p in parts]
    part = width // (depth * 8)
    heads = hs.shape[1] // 2

    def at(i):
        return ((i + tiles // 2 * (1 - lax.axis_index("sp"))) % tiles, 0)

    block = pl.BlockSpec((tile, width), at)
    anywhere = pl.BlockSpec(memory_space=pl.ANY)
    pieces = [(p.shape[4], p.shape[5], p.dtype) for p in parts] + [(16, 128, F32)]
    keep = lambda shape: pl.BlockSpec(shape, lambda i: (0,) * len(shape))
    out_shape = [
        jax.ShapeDtypeStruct((2, rows // 2, width), F32),
        jax.ShapeDtypeStruct((parts[0].shape[4], 3 * width), F32),
        jax.ShapeDtypeStruct((16, 128), F32),
    ]
    return pl.pallas_call(
        functools.partial(leave_kernel, depth, part, heads),
        grid=(tiles,),
        in_specs=[block] * 5
        + [resident(weight.shape), resident(params.shape)]
        + [anywhere] * 3
        + [resident(a.shape) for a in (thin, fat, delta, hs)],
        out_specs=[anywhere, keep(out_shape[1].shape), keep(out_shape[2].shape)],
        out_shape=out_shape,
        scratch_shapes=[
            pltpu.SemaphoreType.DMA((4,)),
            pltpu.SemaphoreType.DMA((4, 3 + depth)),
            pltpu.SemaphoreType.DMA((4, 3 + depth)),
            pltpu.SemaphoreType.DMA((tiles // 2,)),
            pltpu.SemaphoreType.DMA((tiles // 2,)),
            pltpu.SemaphoreType.DMA((tiles // 2,)),
            pltpu.VMEM((4, 8, width), F32),
            pltpu.VMEM((16, width), F32),
            pltpu.VMEM((16, fat.shape[2]), F32),
            pltpu.VMEM((depth, 2, 2, 2, 16, 128), F32),
            pltpu.VMEM((tiles // 2, tile, width), BF16),
            pltpu.VMEM((tiles // 2, tile, width), BF16),
            pltpu.VMEM((tiles // 2, tile, width), F32),
        ]
        + scatter_scratch(pieces, depth),
        compiler_params=pltpu.CompilerParams(
            collective_id=collective_id, has_side_effects=True, vmem_limit_bytes=VMEM_CAP
        ),
        name="leave",
    )(dq, dk, dv, x, dhid, weight, params, *parts, thin, fat, delta, hs)


def fast_shards(
    tokens, doc_lengths, out_cotangent, in_gain, in_bias, qkv_weight, q_bias, v_bias, head_scale, attn_gain,
    attn_bias, out_weight, out_bias, ffn_gain, ffn_bias, fc1_weight, fc1_bias, mid_gain, mid_bias, fc2_weight,
    fc2_bias,
):
    depth = lax.axis_size("dp") // 4
    devices = depth * 8
    half = tokens.shape[1]
    rows = 2 * half
    width = tokens.shape[2]
    me = lax.axis_index("sp")

    narrow_in = [in_gain, in_bias, q_bias, v_bias, attn_gain, attn_bias, out_bias, ffn_gain, ffn_bias, fc2_bias]
    wide_in = [fc1_bias, mid_gain, mid_bias]
    part = width // devices
    heads_each = head_scale.shape[0]
    wqkv, wout, begun, x, narrow, wide, hs = enter(
        narrow_in + wide_in + [head_scale], qkv_weight, out_weight, fc1_weight, tokens, depth, 0
    )
    normed, qkv = qkv_project(x, wqkv, narrow)
    scaled, mixed, lse, w1, w2, dy = attend_fwd(qkv, doc_lengths, hs, begun, fc2_weight, out_cotangent, depth, 1)
    w1, w2 = flat(w1), flat(w2)
    layer, post, ffn_in, active, d_inner, d_hidden, d_low, d_scaled, grads_narrow, grads_wide = middle(
        scaled, x, dy, wout, w1, w2, narrow, wide
    )

    def weight_grad(left, right):
        return jnp.einsum("ti,tj->ij", left, right, preferred_element_type=F32).astype(BF16)

    g_fc2 = weight_grad(active, dy)
    g_fc1 = weight_grad(ffn_in, d_inner)
    g_out = weight_grad(post, d_low)
    (dq, dk, dv, delta), (s_fc2, s_fc1, s_out), layer_out = attend_bwd(
        qkv, mixed, d_scaled, lse, doc_lengths, hs, [g_fc2, g_fc1, g_out], layer, depth, 2
    )
    g_q = weight_grad(normed, dq)
    g_k = weight_grad(normed, dk)
    g_v = weight_grad(normed, dv)
    input_grad, s_qkv, s_small = leave(
        dq, dk, dv, x, d_hidden, wqkv, narrow, [g_q, g_k, g_v], grads_narrow, grads_wide, delta, hs, depth, 3
    )
    nar = [s_small[k, :part] for k in range(10)]
    wid = [s_small[10 + k] for k in range(3)]
    s_hs = s_small[13, :heads_each]
    return (
        layer_out, input_grad, nar[0], nar[1], s_qkv, nar[2], nar[3], s_hs, nar[4], nar[5], s_out, nar[6], nar[7],
        nar[8], s_fc1, wid[0], wid[1], wid[2], s_fc2, nar[9],
    )


LONGEST = 2048


def layer_norm(values, norm_gain, norm_shift):
    center = values - jnp.mean(values, axis=-1, keepdims=True)
    spread = jnp.mean(center * center, axis=-1, keepdims=True)
    return center * lax.rsqrt(spread + EPS) * norm_gain + norm_shift


def doc_index(lengths, row_count):
    seq_ends = jnp.cumsum(lengths)
    places = jnp.arange(row_count, dtype=jnp.int32)
    return jnp.sum((places[:, None] >= seq_ends[None, :]).astype(jnp.int32), axis=1)


def block_scores(query_block, key_heads, doc_query, doc_keys, pos_query, pos_keys, score_scale):
    scores = (
        jnp.einsum("qhd,khd->hqk", query_block, key_heads, preferred_element_type=jnp.float32)
        * score_scale
    )
    allowed = (doc_query[:, None] == doc_keys[None, :]) & (pos_keys[None, :] <= pos_query[:, None])
    return jnp.where(allowed[None], scores, -1e30)


def reduce_grads(grad_set):
    return (
        lax.psum_scatter(grad_set[0], ("dp", "sp"), scatter_dimension=0, tiled=True),
        lax.psum_scatter(grad_set[1], ("dp", "sp"), scatter_dimension=0, tiled=True),
        lax.psum_scatter(grad_set[2], ("dp", "sp"), scatter_dimension=0, tiled=True),
        lax.psum_scatter(grad_set[3], ("dp", "sp"), scatter_dimension=0, tiled=True),
        lax.psum_scatter(grad_set[4], ("dp", "sp"), scatter_dimension=0, tiled=True),
        lax.psum_scatter(grad_set[5], ("dp", "sp"), scatter_dimension=0, tiled=True),
        lax.psum_scatter(grad_set[6], ("dp", "sp"), scatter_dimension=0, tiled=True),
        lax.psum_scatter(grad_set[7], ("dp", "sp"), scatter_dimension=0, tiled=True),
        lax.psum_scatter(grad_set[8], ("dp", "sp"), scatter_dimension=0, tiled=True),
        lax.psum_scatter(grad_set[9], ("dp", "sp"), scatter_dimension=0, tiled=True),
        lax.psum_scatter(grad_set[10], ("dp", "sp"), scatter_dimension=0, tiled=True),
        lax.psum_scatter(grad_set[11], ("dp", "sp"), scatter_dimension=0, tiled=True),
        lax.psum_scatter(grad_set[12], ("dp", "sp"), scatter_dimension=0, tiled=True),
        lax.psum_scatter(grad_set[13], ("dp", "sp"), scatter_dimension=0, tiled=True),
        lax.psum_scatter(grad_set[14], ("dp", "sp"), scatter_dimension=0, tiled=True),
        lax.psum_scatter(grad_set[15], ("dp", "sp"), scatter_dimension=0, tiled=True),
        lax.psum_scatter(grad_set[16], ("dp", "sp"), scatter_dimension=0, tiled=True),
    )


def shards(
    tokens,
    doc_lengths,
    out_cotangent,
    in_gain,
    in_bias,
    qkv_weight,
    q_bias,
    v_bias,
    head_scale,
    attn_gain,
    attn_bias,
    out_weight,
    out_bias,
    ffn_gain,
    ffn_bias,
    fc1_weight,
    fc1_bias,
    mid_gain,
    mid_bias,
    fc2_weight,
    fc2_bias,
):
    micro_count = tokens.shape[0]
    tok_count = tokens.shape[1]
    model_width = tokens.shape[2]
    sp_count = lax.axis_size("sp")
    group_rows = tok_count * sp_count
    local_width = model_width // sp_count
    head_local = head_scale.shape[0]
    head_dim = local_width // head_local
    score_scale = 1.0 / math.sqrt(head_dim)
    window_rows = LONGEST
    block_rows = min(512, window_rows)
    block_count = group_rows // block_rows
    head_gains = head_scale.astype(jnp.float32)
    positions = jnp.arange(group_rows, dtype=jnp.int32)
    starts = jnp.arange(block_count, dtype=jnp.int32) * block_rows

    def collect():
        return (
            lax.all_gather(in_gain, ("dp", "sp"), axis=0, tiled=True),
            lax.all_gather(in_bias, ("dp", "sp"), axis=0, tiled=True),
            lax.all_gather(qkv_weight, ("dp", "sp"), axis=0, tiled=True),
            lax.all_gather(q_bias, ("dp", "sp"), axis=0, tiled=True),
            lax.all_gather(v_bias, ("dp", "sp"), axis=0, tiled=True),
            lax.all_gather(attn_gain, ("dp", "sp"), axis=0, tiled=True),
            lax.all_gather(attn_bias, ("dp", "sp"), axis=0, tiled=True),
            lax.all_gather(out_weight, ("dp", "sp"), axis=0, tiled=True),
            lax.all_gather(out_bias, ("dp", "sp"), axis=0, tiled=True),
            lax.all_gather(ffn_gain, ("dp", "sp"), axis=0, tiled=True),
            lax.all_gather(ffn_bias, ("dp", "sp"), axis=0, tiled=True),
            lax.all_gather(fc1_weight, ("dp", "sp"), axis=0, tiled=True),
            lax.all_gather(fc1_bias, ("dp", "sp"), axis=0, tiled=True),
            lax.all_gather(mid_gain, ("dp", "sp"), axis=0, tiled=True),
            lax.all_gather(mid_bias, ("dp", "sp"), axis=0, tiled=True),
            lax.all_gather(fc2_weight, ("dp", "sp"), axis=0, tiled=True),
            lax.all_gather(fc2_bias, ("dp", "sp"), axis=0, tiled=True),
        )

    def split_heads(heads_in):
        query_heads = heads_in[:, 0].reshape(group_rows, head_local, head_dim)
        key_heads = heads_in[:, 1].reshape(group_rows, head_local, head_dim)
        value_heads = heads_in[:, 2].reshape(group_rows, head_local, head_dim)
        return (query_heads, key_heads, value_heads)

    def attend_back(heads_in, lengths, log_total, grad_mixed):
        query_heads, key_heads, value_heads = split_heads(heads_in)
        doc_ids = doc_index(lengths, group_rows)

        def one_block(block_carry, pair):
            grad_keys, grad_values = block_carry
            row_start, block_lse = pair
            query_block = lax.dynamic_slice_in_dim(query_heads, row_start, block_rows, 0)
            grad_block = lax.dynamic_slice_in_dim(grad_mixed, row_start, block_rows, 0)
            masked = block_scores(
                query_block,
                key_heads,
                lax.dynamic_slice_in_dim(doc_ids, row_start, block_rows, 0),
                doc_ids,
                lax.dynamic_slice_in_dim(positions, row_start, block_rows, 0),
                positions,
                score_scale,
            )
            prob_rows = jnp.exp(masked - block_lse[:, :, None])
            value_part = jnp.einsum(
                "hqk,qhd->khd",
                prob_rows.astype(jnp.bfloat16),
                grad_block,
                preferred_element_type=jnp.float32,
            )
            grad_probs = jnp.einsum(
                "qhd,khd->hqk", grad_block, value_heads, preferred_element_type=jnp.float32
            )
            row_inner = jnp.sum(prob_rows * grad_probs, axis=-1, keepdims=True)
            grad_scores = (prob_rows * (grad_probs - row_inner)).astype(jnp.bfloat16)
            grad_query = (
                jnp.einsum(
                    "hqk,khd->qhd", grad_scores, key_heads, preferred_element_type=jnp.float32
                )
                * score_scale
            )
            key_part = jnp.einsum(
                "hqk,qhd->khd", grad_scores, query_block, preferred_element_type=jnp.float32
            )
            grad_keys = grad_keys + key_part
            grad_values = grad_values + value_part
            return ((grad_keys, grad_values), grad_query)

        zero_heads = jnp.zeros((group_rows, head_local, head_dim), jnp.float32)
        (grad_keys, grad_values), grad_queries = lax.scan(
            one_block, (zero_heads, zero_heads), (starts, log_total)
        )
        stacked = jnp.stack(
            [
                grad_queries.reshape(group_rows, local_width),
                (grad_keys * score_scale).reshape(group_rows, local_width),
                grad_values.reshape(group_rows, local_width),
            ],
            axis=1,
        )
        return stacked.astype(jnp.bfloat16)

    outputs = []
    input_grads = []
    total_grads = None
    scale_total = jnp.zeros((head_local,), jnp.float32)
    for micro_index in range(micro_count):
        forward_set = collect()
        (
            forward_wide_in_gain,
            forward_wide_in_bias,
            forward_wide_qkv,
            forward_wide_q_bias,
            forward_wide_v_bias,
            forward_wide_attn_gain,
            forward_wide_attn_bias,
            forward_wide_out,
            forward_wide_out_bias,
            forward_wide_ffn_gain,
            forward_wide_ffn_bias,
            forward_wide_fc1,
            forward_wide_fc1_bias,
            forward_wide_mid_gain,
            forward_wide_mid_bias,
            forward_wide_fc2,
            forward_wide_fc2_bias,
        ) = forward_set
        forward_tok_rows = tokens[micro_index].astype(jnp.float32)
        forward_lengths = doc_lengths[0, micro_index]
        forward_normed = layer_norm(
            forward_tok_rows,
            forward_wide_in_gain.astype(jnp.float32),
            forward_wide_in_bias.astype(jnp.float32),
        ).astype(jnp.bfloat16)
        bias_row = jnp.concatenate(
            [forward_wide_q_bias, jnp.zeros_like(forward_wide_q_bias), forward_wide_v_bias]
        ).astype(jnp.float32)
        projected = (
            jnp.dot(forward_normed, forward_wide_qkv, preferred_element_type=jnp.float32) + bias_row
        )
        qkv_sent = projected.astype(jnp.bfloat16).reshape(tok_count, 3, model_width)
        forward_heads_in = lax.all_to_all(qkv_sent, "sp", split_axis=2, concat_axis=0, tiled=True)
        attend_query_heads, attend_key_heads, attend_value_heads = split_heads(forward_heads_in)
        attend_doc_ids = doc_index(forward_lengths, group_rows)

        def attend_one_block(row_start):
            query_block = lax.dynamic_slice_in_dim(attend_query_heads, row_start, block_rows, 0)
            masked = block_scores(
                query_block,
                attend_key_heads,
                lax.dynamic_slice_in_dim(attend_doc_ids, row_start, block_rows, 0),
                attend_doc_ids,
                lax.dynamic_slice_in_dim(positions, row_start, block_rows, 0),
                positions,
                score_scale,
            )
            row_max = jnp.max(masked, axis=-1, keepdims=True)
            raised = jnp.exp(masked - row_max)
            row_total = jnp.sum(raised, axis=-1, keepdims=True)
            prob_rows = (raised / row_total).astype(jnp.bfloat16)
            head_mixed = jnp.einsum(
                "hqk,khd->qhd", prob_rows, attend_value_heads, preferred_element_type=jnp.float32
            )
            return (head_mixed, (row_max + jnp.log(row_total))[:, :, 0])

        head_mixed, attend_log_total = lax.map(attend_one_block, starts)
        forward_head_mixed = head_mixed.reshape(group_rows, head_local, head_dim)
        scaled = (
            (forward_head_mixed * head_gains[None, :, None])
            .reshape(group_rows, local_width)
            .astype(jnp.bfloat16)
        )
        forward_attn_rows = lax.all_to_all(
            scaled, "sp", split_axis=0, concat_axis=1, tiled=True
        ).astype(jnp.float32)
        forward_post_norm = layer_norm(
            forward_attn_rows,
            forward_wide_attn_gain.astype(jnp.float32),
            forward_wide_attn_bias.astype(jnp.float32),
        ).astype(jnp.bfloat16)
        forward_hidden = (
            forward_tok_rows
            + jnp.dot(forward_post_norm, forward_wide_out, preferred_element_type=jnp.float32)
            + forward_wide_out_bias.astype(jnp.float32)
        )
        forward_ffn_in = layer_norm(
            forward_hidden,
            forward_wide_ffn_gain.astype(jnp.float32),
            forward_wide_ffn_bias.astype(jnp.float32),
        ).astype(jnp.bfloat16)
        forward_ffn_inner = jnp.dot(
            forward_ffn_in, forward_wide_fc1, preferred_element_type=jnp.float32
        ) + forward_wide_fc1_bias.astype(jnp.float32)
        forward_active = layer_norm(
            jax.nn.gelu(forward_ffn_inner),
            forward_wide_mid_gain.astype(jnp.float32),
            forward_wide_mid_bias.astype(jnp.float32),
        ).astype(jnp.bfloat16)
        output = (
            forward_hidden
            + jnp.dot(forward_active, forward_wide_fc2, preferred_element_type=jnp.float32)
            + forward_wide_fc2_bias.astype(jnp.float32)
        )
        forward_kept_values = (
            forward_normed,
            forward_heads_in,
            forward_head_mixed,
            attend_log_total,
            forward_attn_rows,
            forward_post_norm,
            forward_hidden,
            forward_ffn_in,
            forward_ffn_inner,
            forward_active,
        )
        output, kept_values = (output, forward_kept_values)
        backward_set = collect()
        (
            wide_in_gain,
            wide_in_bias,
            wide_qkv,
            wide_q_bias,
            wide_v_bias,
            wide_attn_gain,
            wide_attn_bias,
            wide_out,
            wide_out_bias,
            wide_ffn_gain,
            wide_ffn_bias,
            wide_fc1,
            wide_fc1_bias,
            wide_mid_gain,
            wide_mid_bias,
            wide_fc2,
            wide_fc2_bias,
        ) = backward_set
        (
            normed,
            backward_heads_in,
            backward_head_mixed,
            backward_log_total,
            attn_rows,
            post_norm,
            hidden,
            ffn_in,
            ffn_inner,
            active,
        ) = kept_values
        tok_rows = tokens[micro_index].astype(jnp.float32)
        backward_lengths = doc_lengths[0, micro_index]
        grad_out = out_cotangent[micro_index].astype(jnp.float32)
        fc2_bias_grad = jnp.sum(grad_out, axis=0)
        grad_low = grad_out.astype(jnp.bfloat16)
        fc2_grad = jnp.einsum("ti,tj->ij", active, grad_low, preferred_element_type=jnp.float32)
        grad_active = jnp.einsum(
            "tj,ij->ti", grad_low, wide_fc2, preferred_element_type=jnp.float32
        )
        gelu_out, gelu_back = jax.vjp(jax.nn.gelu, ffn_inner)
        _, mid_back = jax.vjp(
            layer_norm,
            gelu_out,
            wide_mid_gain.astype(jnp.float32),
            wide_mid_bias.astype(jnp.float32),
        )
        grad_gelu, mid_gain_grad, mid_bias_grad = mid_back(grad_active)
        (grad_inner,) = gelu_back(grad_gelu)
        inner_low = grad_inner.astype(jnp.bfloat16)
        fc1_bias_grad = jnp.sum(inner_low.astype(jnp.float32), axis=0)
        fc1_grad = jnp.einsum("ti,tj->ij", ffn_in, inner_low, preferred_element_type=jnp.float32)
        grad_ffn = jnp.einsum("tj,ij->ti", inner_low, wide_fc1, preferred_element_type=jnp.float32)
        _, ffn_back = jax.vjp(
            layer_norm, hidden, wide_ffn_gain.astype(jnp.float32), wide_ffn_bias.astype(jnp.float32)
        )
        grad_hid, ffn_gain_grad, ffn_bias_grad = ffn_back(grad_ffn)
        grad_hidden = grad_out + grad_hid
        out_bias_grad = jnp.sum(grad_hidden, axis=0)
        hidden_low = grad_hidden.astype(jnp.bfloat16)
        out_grad = jnp.einsum(
            "ti,tj->ij", post_norm, hidden_low, preferred_element_type=jnp.float32
        )
        grad_post = jnp.einsum(
            "tj,ij->ti", hidden_low, wide_out, preferred_element_type=jnp.float32
        )
        _, attn_back = jax.vjp(
            layer_norm,
            attn_rows,
            wide_attn_gain.astype(jnp.float32),
            wide_attn_bias.astype(jnp.float32),
        )
        grad_attn, attn_gain_grad, attn_bias_grad = attn_back(grad_post)
        grad_heads = lax.all_to_all(
            grad_attn.astype(jnp.bfloat16), "sp", split_axis=1, concat_axis=0, tiled=True
        )
        grad_scaled = grad_heads.astype(jnp.float32).reshape(group_rows, head_local, head_dim)
        scale_grad = jnp.sum(grad_scaled * backward_head_mixed, axis=(0, 2))
        backward_grad_mixed = (grad_scaled * head_gains[None, :, None]).astype(jnp.bfloat16)
        grad_qkv = attend_back(
            backward_heads_in, backward_lengths, backward_log_total, backward_grad_mixed
        )
        returned = lax.all_to_all(grad_qkv, "sp", split_axis=0, concat_axis=2, tiled=True).reshape(
            tok_count, 3 * model_width
        )
        column_sums = jnp.sum(returned.astype(jnp.float32), axis=0)
        q_bias_grad = column_sums[:model_width]
        v_bias_grad = column_sums[2 * model_width :]
        qkv_grad = jnp.einsum("ti,tj->ij", normed, returned, preferred_element_type=jnp.float32)
        grad_normed = jnp.einsum(
            "tj,ij->ti", returned, wide_qkv, preferred_element_type=jnp.float32
        )
        _, in_back = jax.vjp(
            layer_norm, tok_rows, wide_in_gain.astype(jnp.float32), wide_in_bias.astype(jnp.float32)
        )
        grad_rows, in_gain_grad, in_bias_grad = in_back(grad_normed)
        input_grad = grad_hidden + grad_rows
        grad_set = (
            in_gain_grad,
            in_bias_grad,
            qkv_grad,
            q_bias_grad,
            v_bias_grad,
            attn_gain_grad,
            attn_bias_grad,
            out_grad,
            out_bias_grad,
            ffn_gain_grad,
            ffn_bias_grad,
            fc1_grad,
            fc1_bias_grad,
            mid_gain_grad,
            mid_bias_grad,
            fc2_grad,
            fc2_bias_grad,
        )
        input_grad, grad_set, scale_grad = (input_grad, grad_set, scale_grad)
        grad_set = reduce_grads(grad_set)
        total_grads = (
            grad_set if total_grads is None else jax.tree.map(jnp.add, total_grads, grad_set)
        )
        scale_total = scale_total + scale_grad
        outputs.append(output)
        input_grads.append(input_grad)
    scale_sum = lax.psum(scale_total, "dp")
    layer_out = jnp.stack(outputs).astype(jnp.bfloat16)
    input_grad = jnp.stack(input_grads)
    return (
        layer_out,
        input_grad,
        total_grads[0],
        total_grads[1],
        total_grads[2],
        total_grads[3],
        total_grads[4],
        scale_sum,
        total_grads[5],
        total_grads[6],
        total_grads[7],
        total_grads[8],
        total_grads[9],
        total_grads[10],
        total_grads[11],
        total_grads[12],
        total_grads[13],
        total_grads[14],
        total_grads[15],
        total_grads[16],
    )


def fits(args):
    dp, sp = lax.axis_size("dp"), lax.axis_size("sp")
    tokens, lengths, in_gain, fc1_bias = args[0], args[1], args[3], args[16]
    return (
        sp == 2
        and tokens.shape[0] == 2
        and dp % 4 == 0
        and dp >= 8
        and 2 * tokens.shape[1] == LONGEST
        and lengths.shape[2] * BLOCK == LONGEST
        and 128 % in_gain.shape[0] == 0
        and fc1_bias.shape[0] == 128
        and tokens.shape[2] == 128 * args[8].shape[0]
    )


def body(*args):
    return fast_shards(*args) if fits(args) else shards(*args)


def solution(mesh):
    return jax.shard_map(
        body,
        mesh=mesh,
        in_specs=(
            P(None, ("dp", "sp"), None),
            P("dp", None, None),
            P(None, ("dp", "sp"), None),
            P(("dp", "sp")),
            P(("dp", "sp")),
            P(("dp", "sp"), None),
            P(("dp", "sp")),
            P(("dp", "sp")),
            P("sp"),
            P(("dp", "sp")),
            P(("dp", "sp")),
            P(("dp", "sp"), None),
            P(("dp", "sp")),
            P(("dp", "sp")),
            P(("dp", "sp")),
            P(("dp", "sp"), None),
            P(("dp", "sp")),
            P(("dp", "sp")),
            P(("dp", "sp")),
            P(("dp", "sp"), None),
            P(("dp", "sp")),
        ),
        out_specs=(
            P(None, ("dp", "sp"), None),
            P(None, ("dp", "sp"), None),
            P(("dp", "sp")),
            P(("dp", "sp")),
            P(("dp", "sp"), None),
            P(("dp", "sp")),
            P(("dp", "sp")),
            P("sp"),
            P(("dp", "sp")),
            P(("dp", "sp")),
            P(("dp", "sp"), None),
            P(("dp", "sp")),
            P(("dp", "sp")),
            P(("dp", "sp")),
            P(("dp", "sp"), None),
            P(("dp", "sp")),
            P(("dp", "sp")),
            P(("dp", "sp")),
            P(("dp", "sp"), None),
            P(("dp", "sp")),
        ),
        check_vma=False,
    )
```

```python
import functools
import math

import jax
import jax.numpy as jnp
from jax import lax
from jax.experimental import pallas as pl
from jax.experimental.pallas import tpu as pltpu
from jax.sharding import PartitionSpec as P

EPS = 1e-05
BLOCK = 512
LOG2E = math.log2(math.e)
NEG = -1e30
F32 = jnp.float32
BF16 = jnp.bfloat16
VMEM_CAP = 60 * 1024 * 1024
NT = (((1,), (1,)), ((), ()))
NN = (((1,), (0,)), ((), ()))
FWD_STEPS = ((0, 0, 10, 11), (11, 12, 28, 29), (20, 21, 30, 31), (24, 25, 32, 32))
BWD_STEPS = ((1, 2, 3, 4, 5), (9, 15, 20, 26, 28), (14, 19, 24, 29, 30), (18, 23, 28, 32, 32))


def mm(a, b, dims=NN):
    return lax.dot_general(a, b, dims, preferred_element_type=F32)


def same_sequence(lengths, y):
    ends = []
    for k in range(lengths.shape[2]):
        ends.append(lengths[0, y, k] + (ends[-1] if ends else 0))

    def same(i, kb):
        between = [((e > kb * BLOCK) & (e <= i * BLOCK)).astype(jnp.int32) for e in ends]
        return sum(between) == 0

    return same


class Place:
    def __init__(self, depth):
        d = lax.axis_index("dp")
        self.depth = depth
        self.y = lax.axis_index("sp")
        self.c = d % 2
        self.x = (d // 2) % 2
        self.z = d // 4
        self.next_y = self.device(self.z, self.x, self.c, 1 - self.y)
        self.next_x = self.device(self.z, 1 - self.x, self.c, self.y)
        self.twin = self.device(self.z, self.x, 1 - self.c, self.y)

    def device(self, z, x, c, y):
        return ((z * 2 + x) * 2 + c, y)

    def along(self, step):
        return (self.z + step) % self.depth

    def column(self, step):
        return self.device(self.along(step), self.x, self.c, self.y)

    def greet(self):
        barrier = pltpu.get_barrier_semaphore()
        peers = [self.column(s) for s in range(1, self.depth)] + [self.next_x, self.next_y, self.twin]
        for peer in peers:
            pl.semaphore_signal(barrier, inc=1, device_id=peer, device_id_type=pl.DeviceIdType.MESH)
        pl.semaphore_wait(barrier, len(peers))


def remote(src, dst, send, recv, peer):
    return pltpu.make_async_remote_copy(
        src_ref=src, dst_ref=dst, send_sem=send, recv_sem=recv, device_id=peer, device_id_type=pl.DeviceIdType.MESH
    )


class Gather:
    def __init__(self, me, shard, stage, whole, at, count, local, send, recv):
        self.me, self.whole = me, whole
        if shard is not None:
            self.shard, self.stage = shard.at[pl.ds(at, count)], stage.at[pl.ds(at, count)]
        self.rows = pl.ds(at, count)
        self.local, self.send, self.recv = local, send, recv

    def own(self, z):
        me = self.me
        return self.whole.at[z, me.x, me.c, me.y, self.rows]

    def load(self):
        return pltpu.make_async_copy(self.shard, self.stage, self.local)

    def keep(self):
        return pltpu.make_async_copy(self.stage, self.own(self.me.z), self.local)

    def depth_hop(self, s, landed):
        me = self.me
        z = me.along(me.depth - s) if landed else me.z
        return remote(self.stage, self.own(z), self.send.at[6 + s], self.recv.at[6 + s], me.column(s))

    def hop(self, x, y, n, peer, c=None):
        group = self.whole.at[:, x, self.me.c if c is None else c, y, self.rows]
        return remote(group, group, self.send.at[n], self.recv.at[n], peer)

    def path(self, n, c=None):
        me = self.me
        x, y = me.x, me.y
        gx = 1 - x if n in (5, 6) else x
        gy = 1 - y if n in (2, 4, 6) else y
        peer = me.next_y if n == 0 else me.next_x if n < 3 else me.twin
        return self.hop(gx, gy, n, peer, c)

    def ready(self):
        self.load().start()

    def begin(self):
        self.load().wait()
        self.keep().start()
        for s in range(1, self.me.depth):
            self.depth_hop(s, False).start()

    def landed(self):
        self.keep().wait()
        for s in range(1, self.me.depth):
            self.depth_hop(s, True).wait()

    def launch(self):
        for n in (0, 1, 3):
            self.path(n).start()

    def spread(self):
        self.landed()
        self.launch()

    def from_y(self):
        me = self.me
        self.hop(me.x, 1 - me.y, 0, me.next_y).wait_recv()
        self.path(2).start()
        self.path(4).start()

    def from_x(self):
        me = self.me
        self.hop(1 - me.x, me.y, 1, me.next_x).wait_recv()
        self.path(5).start()

    def from_corner(self):
        me = self.me
        self.hop(1 - me.x, 1 - me.y, 2, me.next_x).wait_recv()
        self.path(6).start()

    def end(self):
        for n in range(7):
            self.path(n).wait_send()
        for n in range(3, 7):
            self.path(n, 1 - self.me.c).wait_recv()


class Gather2:
    def __init__(self, me, shard, stage, whole, at, count, local, send, recv):
        self.me, self.whole = me, whole
        self.rows = pl.ds(at, count)
        if shard is not None:
            self.shard, self.stage = shard.at[self.rows], stage.at[self.rows]
        self.local, self.send, self.recv = local, send, recv

    def one(self, z, y):
        me = self.me
        return self.whole.at[z, me.x, me.c, y, self.rows]

    def load(self):
        return pltpu.make_async_copy(self.shard, self.stage, self.local)

    def keep(self):
        return pltpu.make_async_copy(self.stage, self.one(self.me.z, self.me.y), self.local)

    def y_hop(self, y):
        me = self.me
        return remote(self.stage, self.one(me.z, y), self.send.at[0], self.recv.at[0], me.next_y)

    def z_hop(self, s, n, landed):
        me = self.me
        z = me.along(me.depth - s) if landed else me.z
        y = 1 - me.y if n else me.y
        src = self.one(me.z, y) if n else self.stage
        k = 1 + n * (me.depth - 1) + s
        return remote(src, self.one(z, y), self.send.at[k], self.recv.at[k], me.column(s))

    def plane(self, x, n, peer, c):
        k = 2 * self.me.depth + n
        plane = self.whole.at[:, x, c, :, self.rows]
        return remote(plane, plane, self.send.at[k], self.recv.at[k], peer)

    def x_hop(self, landed):
        me = self.me
        return self.plane(1 - me.x if landed else me.x, 0, me.next_x, me.c)

    def twin_hop(self, n, landed):
        me = self.me
        return self.plane(1 - me.x if n else me.x, 1 + n, me.twin, 1 - me.c if landed else me.c)

    def ready(self):
        self.load().start()

    def begin(self):
        self.load().wait()
        self.keep().start()
        self.y_hop(self.me.y).start()
        for s in range(1, self.me.depth):
            self.z_hop(s, 0, False).start()

    def pass_z(self):
        self.y_hop(self.me.y).wait_send()
        self.y_hop(1 - self.me.y).wait_recv()
        for s in range(1, self.me.depth):
            self.z_hop(s, 1, False).start()

    def landed(self):
        self.keep().wait()
        for n in range(2):
            for s in range(1, self.me.depth):
                self.z_hop(s, n, True).wait()

    def pass_x(self):
        self.landed()
        self.x_hop(False).start()

    def pass_twin(self):
        self.twin_hop(0, False).start()

    def arrived(self):
        self.x_hop(False).wait_send()
        self.x_hop(True).wait_recv()

    def pass_twin_far(self):
        self.twin_hop(1, False).start()

    def end(self):
        for n in range(2):
            self.twin_hop(n, False).wait_send()
            self.twin_hop(n, True).wait_recv()


class Swap:
    def __init__(self, me, sent, landing, kept, stage, place, local, send, recv):
        self.out = remote(sent, landing(me.y), send, recv, me.next_y)
        self.into = remote(sent, landing(1 - me.y), send, recv, me.next_y)
        self.load = pltpu.make_async_copy(kept, stage, local)
        self.keep = pltpu.make_async_copy(stage, place, local)

    def ready(self):
        self.load.start()

    def begin(self):
        self.out.start()
        self.load.wait()
        self.keep.start()

    def end(self):
        self.out.wait_send()
        self.into.wait_recv()
        self.keep.wait()


def add_group(own, x, y, taken):
    def body(s, _):
        own[s, x, y] = (own[s, x, y].astype(F32) + taken(s).astype(F32)).astype(own.dtype)
        return 0

    lax.fori_loop(0, own.shape[0], body, 0)


class Scatter:
    def __init__(self, me, part, at, count, own, got0, got1, got3, local, send, recv, total):
        self.me, self.part, self.rows = me, part, pl.ds(at, count)
        self.own, self.got0, self.got1, self.got3 = own, got0, got1, got3
        self.local, self.send, self.recv, self.total = local, send, recv, total

    def mine(self):
        return pltpu.make_async_copy(self.part.at[:, :, self.me.c, :, self.rows], self.own, self.local)

    def halves(self):
        return remote(
            self.part.at[:, :, 1 - self.me.c, :, self.rows], self.got0, self.send.at[0], self.recv.at[0], self.me.twin
        )

    def to_x(self, n):
        me = self.me
        y = me.y if n == 0 else 1 - me.y
        return remote(self.own.at[:, 1 - me.x, y], self.got1.at[n], self.send.at[1 + n], self.recv.at[1 + n], me.next_x)

    def to_y(self):
        me = self.me
        return remote(self.own.at[:, me.x, 1 - me.y], self.got1.at[2], self.send.at[3], self.recv.at[3], me.next_y)

    def to_z(self, s):
        me = self.me
        return remote(
            self.own.at[me.along(s), me.x, me.y], self.got3.at[s - 1], self.send.at[3 + s], self.recv.at[3 + s],
            me.column(s),
        )

    def begin(self):
        self.mine().start()
        self.halves().start()

    def across(self):
        me, own, got = self.me, self.own, self.got0
        self.mine().wait()
        self.halves().wait()
        for n, x, y in ((1, 1 - me.x, 1 - me.y), (0, 1 - me.x, me.y)):
            add_group(own, x, y, lambda s: got[s, x, y])
            self.to_x(n).start()
        for x, y in ((me.x, 1 - me.y), (me.x, me.y)):
            add_group(own, x, y, lambda s: got[s, x, y])

    def along_x(self):
        me, own, got = self.me, self.own, self.got1
        self.to_x(1).wait_recv()
        add_group(own, me.x, 1 - me.y, lambda s: got[1, s])
        self.to_y().start()
        self.to_x(0).wait_recv()
        add_group(own, me.x, me.y, lambda s: got[0, s])

    def along_y(self):
        me, own, got = self.me, self.own, self.got1
        self.to_y().wait_recv()
        add_group(own, me.x, me.y, lambda s: got[2, s])
        for s in range(1, me.depth):
            self.to_z(s).start()

    def end(self):
        me = self.me
        total = self.own[me.z, me.x, me.y].astype(F32)
        for s in range(1, me.depth):
            self.to_z(s).wait_recv()
            total = total + self.got3[s - 1].astype(F32)
        self.total[self.rows] = total
        self.to_x(0).wait_send()
        self.to_x(1).wait_send()
        self.to_y().wait_send()
        for s in range(1, me.depth):
            self.to_z(s).wait_send()


def scatter_scratch(pieces, depth):
    out = []
    for rows, cols, dtype in pieces:
        for lead in ((depth, 2, 2), (depth, 2, 2), (3, depth), (depth - 1,)):
            out.append(pltpu.VMEM(lead + (rows, cols), dtype))
    return out


def perform(step, plan):
    for due in sorted(plan):

        @pl.when(step == due)
        def _(actions=plan[due]):
            for action in actions:
                action()


def due(plan, step, action):
    plan.setdefault(step, []).append(action)


def head_pair_masks():
    lanes = lax.broadcasted_iota(jnp.int32, (1, 128), 1)
    return (lanes < 64, lanes >= 64)


def attend_fwd_kernel(depth, pieces, *refs):
    lengths, hs, q_ref, k_ref, v_ref = refs[:5]
    shard, cot = refs[6:8]
    o_ref, mixed_ref, lse_ref = refs[8:11]
    wholes = refs[11:13]
    cot_whole = refs[13]
    vt, local, send, recv, shard_stage, cot_stage = refs[14:]
    pair = pl.program_id(0)
    me = Place(depth)
    same = same_sequence(lengths, me.y)
    gathers = [
        Gather(me, shard if a else None, shard_stage, wholes[a], at, count, local.at[n], send.at[n], recv.at[n])
        for n, (a, at, count) in enumerate(pieces)
    ]
    n = len(pieces)
    swap = Swap(
        me, cot.at[1 - me.y], lambda y: cot_whole.at[y], cot.at[me.y], cot_stage, cot_whole.at[me.y],
        local.at[n], send.at[n, 0], recv.at[n, 0],
    )
    plan = {}
    due(plan, 0, me.greet)
    due(plan, 0, swap.ready)
    for n, g in enumerate(gathers):
        if pieces[n][0]:
            due(plan, 0, g.ready)
    for n, g in enumerate(gathers):
        due(plan, 0, g.begin if pieces[n][0] else g.launch)
        if pieces[n][0]:
            due(plan, FWD_STEPS[0][n], g.spread)
        due(plan, FWD_STEPS[1][n], g.from_y)
        due(plan, FWD_STEPS[2][n], g.from_x)
        due(plan, FWD_STEPS[3][n], g.from_corner)
        due(plan, 32, g.end)
    due(plan, 6, swap.begin)
    due(plan, 32, swap.end)
    last = plan.pop(32)
    rows = q_ref.shape[0]
    blocks = rows // BLOCK
    factor = LOG2E / 8.0
    masks = head_pair_masks()
    gains = jnp.where(masks[0], hs[0, 2 * pair], hs[0, 2 * pair + 1])
    for j in range(blocks):
        vtr = v_ref[j * BLOCK : (j + 1) * BLOCK, :].astype(F32).T.astype(BF16)
        for h in range(2):
            vt[j, h, 0:64, :] = vtr[h * 64 : (h + 1) * 64]
            vt[j, h, 64:80, :] = jnp.ones((16, BLOCK), BF16)
    key_at = lax.broadcasted_iota(jnp.int32, (BLOCK, BLOCK), 0)
    query_at = lax.broadcasted_iota(jnp.int32, (BLOCK, BLOCK), 1)

    def one_query(i):
        perform(pair, {k // blocks: plan[k] for k in plan if k % blocks == i})
        q = q_ref[pl.ds(i * BLOCK, BLOCK), :]
        qh = [jnp.where(m, q, jnp.zeros_like(q)) for m in masks]

        def step(kb, carry, diag):
            k = k_ref[pl.ds(kb * BLOCK, BLOCK), :]
            out = []
            for h in range(2):
                s = mm(k, qh[h], NT)
                if diag:
                    s = jnp.where(key_at <= query_at, s, NEG)
                    m = jnp.max(s, axis=0, keepdims=True)
                    p = jnp.exp2(s * factor - m * factor).astype(BF16)
                    out.append((m, mm(vt[kb, h], p)))
                else:
                    bias = jnp.where(same(i, kb), 0.0, NEG)
                    m_old, acc = carry[h]
                    m = jnp.maximum(m_old, jnp.max(s, axis=0, keepdims=True) + bias)
                    p = jnp.exp2(s * factor - (m - bias) * factor).astype(BF16)
                    alpha = jnp.exp2((m_old - m) * factor)
                    out.append((m, acc * alpha + mm(vt[kb, h], p)))
            return tuple(out)

        carry = step(i, None, True)
        for kb in range(i):
            carry = step(kb, carry, False)
        outs = []
        for h in range(2):
            m, acc = carry[h]
            total = acc[64:65]
            outs.append(acc[:64] / total)
            lse_ref[0, h, pl.ds(i, 1), :] = m * factor + jnp.log2(total)
        both = jnp.concatenate(outs, axis=0).T
        mixed_ref[pl.ds(i * BLOCK, BLOCK), :] = both
        o_ref[pl.ds(i * BLOCK, BLOCK), :] = (both * gains).astype(BF16)

    for i in range(blocks):
        one_query(i)
    perform(pair, {pl.num_programs(0) - 1: last})


def attend_fwd(qkv, lengths, hs, begun, shard, cot, depth, collective_id):
    rows, width3 = qkv.shape
    width = width3 // 3
    pairs = width // 128
    blocks = rows // BLOCK
    spec = lambda part: pl.BlockSpec((rows, 128), lambda p, part=part: (0, part * pairs + p))
    smem = pl.BlockSpec(memory_space=pltpu.SMEM)
    anywhere = pl.BlockSpec(memory_space=pl.ANY)
    pieces = []
    for a, count in enumerate((begun.shape[4], shard.shape[0])):
        part = count // 2
        pieces += [(a, 0, part), (a, part, part)]
    count = len(pieces) + 1
    out = pl.pallas_call(
        functools.partial(attend_fwd_kernel, depth, pieces),
        grid=(pairs,),
        in_specs=[smem, smem, spec(0), spec(1), spec(2)] + [anywhere] * 3,
        out_specs=[
            pl.BlockSpec((rows, 128), lambda p: (0, p)),
            pl.BlockSpec((rows, 128), lambda p: (0, p)),
            pl.BlockSpec((1, 2, blocks, BLOCK), lambda p: (p, 0, 0, 0)),
        ]
        + [anywhere] * 3,
        out_shape=[
            jax.ShapeDtypeStruct((rows, width), BF16),
            jax.ShapeDtypeStruct((rows, width), F32),
            jax.ShapeDtypeStruct((pairs, 2, blocks, BLOCK), F32),
            jax.ShapeDtypeStruct(begun.shape, begun.dtype),
            jax.ShapeDtypeStruct((depth, 2, 2, 2) + shard.shape, shard.dtype),
            jax.ShapeDtypeStruct(cot.shape, cot.dtype),
        ],
        input_output_aliases={5: 3},
        scratch_shapes=[
            pltpu.VMEM((blocks, 2, 80, BLOCK), BF16),
            pltpu.SemaphoreType.DMA((count,)),
            pltpu.SemaphoreType.DMA((count, 6 + depth)),
            pltpu.SemaphoreType.DMA((count, 6 + depth)),
            pltpu.VMEM(shard.shape, shard.dtype),
            pltpu.VMEM(cot.shape[1:], cot.dtype),
        ],
        compiler_params=pltpu.CompilerParams(
            vmem_limit_bytes=VMEM_CAP, collective_id=collective_id, has_side_effects=True
        ),
        name="attend_fwd",
    )(lengths, hs, qkv, qkv, qkv, begun, shard, cot)
    return out[0], out[1], out[2], out[3], out[4], out[5].reshape(rows, width)


def attend_bwd_kernel(depth, pieces, *refs):
    lengths, hs, q_ref, k_ref, v_ref, o_ref, g_ref, lse_ref = refs[:8]
    parts = refs[8:11]
    layer = refs[11]
    dq_ref, dk_ref, dv_ref, delta_ref = refs[12:16]
    sums = refs[16:19]
    layer_out = refs[19]
    kt, dk_acc, dv_acc, local, send, recv, layer_stage = refs[20:27]
    scratch = refs[27:]
    pair = pl.program_id(0)
    me = Place(depth)
    same = same_sequence(lengths, me.y)
    scatters = [
        Scatter(
            me, parts[a], at, count, *scratch[4 * n : 4 * n + 4], local.at[n], send.at[n], recv.at[n], sums[a]
        )
        for n, (a, at, count) in enumerate(pieces)
    ]
    n = len(pieces)
    half = layer_out.shape[1]
    swap = Swap(
        me, layer.at[pl.ds((1 - me.y) * half, half)], lambda y: layer_out.at[y],
        layer.at[pl.ds(me.y * half, half)], layer_stage, layer_out.at[me.y], local.at[n], send.at[n, 0], recv.at[n, 0],
    )
    plan = {}
    due(plan, 0, swap.ready)
    due(plan, 0, me.greet)
    for s in scatters:
        due(plan, 0, s.begin)
    for n, s in enumerate(scatters):
        due(plan, BWD_STEPS[0][n], s.across)
        due(plan, BWD_STEPS[1][n], s.along_x)
        due(plan, BWD_STEPS[2][n], s.along_y)
        due(plan, BWD_STEPS[3][n], s.end)
    due(plan, 0, swap.begin)
    due(plan, 32, swap.end)
    last = plan.pop(32)
    rows = q_ref.shape[0]
    blocks = rows // BLOCK
    factor = LOG2E / 8.0
    masks = head_pair_masks()
    for j in range(blocks):
        kt[j] = k_ref[j * BLOCK : (j + 1) * BLOCK, :].astype(F32).T.astype(BF16)
    key_at = lax.broadcasted_iota(jnp.int32, (BLOCK, BLOCK), 0)
    query_at = lax.broadcasted_iota(jnp.int32, (BLOCK, BLOCK), 1)
    gains = jnp.where(masks[0], hs[0, 2 * pair], hs[0, 2 * pair + 1])
    picks = jnp.concatenate([m.astype(F32) for m in masks] + [jnp.zeros((6, 128), F32)], axis=0).astype(BF16)

    def one_query(i):
        perform(pair, {k // blocks: plan[k] for k in plan if k % blocks == i})
        at = pl.ds(i * BLOCK, BLOCK)
        q = q_ref[at, :]
        g = (g_ref[at, :].astype(F32) * gains).astype(BF16)
        prod = g.astype(F32) * o_ref[at, :]
        hi = prod.astype(BF16)
        lo = (prod - hi.astype(F32)).astype(BF16)
        deltas = mm(picks, hi, NT) + mm(picks, lo, NT)
        qh = [jnp.where(m, q, jnp.zeros_like(q)) for m in masks]
        gh = [jnp.where(m, g, jnp.zeros_like(g)) for m in masks]
        delta = [deltas[h : h + 1] for h in range(2)]
        lse = [lse_ref[0, h, pl.ds(i, 1), :] for h in range(2)]
        for h in range(2):
            delta_ref[0, h, pl.ds(i, 1), :] = delta[h]

        def step(kb, carry, diag):
            ks = pl.ds(kb * BLOCK, BLOCK)
            k = k_ref[ks, :]
            v = v_ref[ks, :]
            out = []
            dk_part = None
            dv_part = None
            for h in range(2):
                s = mm(k, qh[h], NT)
                dp = mm(v, gh[h], NT)
                if diag:
                    p = jnp.exp2(s * factor - lse[h])
                    p = jnp.where(key_at <= query_at, p, 0.0)
                else:
                    bias = jnp.where(same(i, kb), 0.0, -NEG)
                    p = jnp.exp2(s * factor - (lse[h] + bias))
                ds = (p * (dp - delta[h])).astype(BF16)
                dvh = mm(p.astype(BF16), gh[h])
                dkh = mm(ds, qh[h])
                dk_part = dkh if dk_part is None else dk_part + dkh
                dv_part = dvh if dv_part is None else dv_part + dvh
                dqh = mm(kt[kb, h * 64 : (h + 1) * 64, :], ds)
                out.append(dqh if diag else carry[h] + dqh)
            if diag:
                dk_acc[ks, :] = dk_part
                dv_acc[ks, :] = dv_part
            else:
                dk_acc[ks, :] += dk_part
                dv_acc[ks, :] += dv_part
            return tuple(out)

        carry = step(i, None, True)
        for kb in range(i):
            carry = step(kb, carry, False)
        both = jnp.concatenate(carry, axis=0) * 0.125
        dq_ref[at, :] = both.T.astype(BF16)

    for i in range(blocks):
        one_query(i)
    dk_ref[...] = (dk_acc[...] * 0.125).astype(BF16)
    dv_ref[...] = dv_acc[...].astype(BF16)
    perform(pair, {pl.num_programs(0) - 1: last})


def shard_view(part, depth):
    return part.reshape((depth, 2, 2, 2, part.shape[0] // (depth * 8)) + part.shape[1:])


def attend_bwd(qkv, mixed, d_scaled, lse, lengths, hs, parts, layer, depth, collective_id):
    rows, width3 = qkv.shape
    width = width3 // 3
    pairs = width // 128
    blocks = rows // BLOCK
    spec = lambda part: pl.BlockSpec((rows, 128), lambda p, part=part: (0, part * pairs + p))
    col = pl.BlockSpec((rows, 128), lambda p: (0, p))
    stat = pl.BlockSpec((1, 2, blocks, BLOCK), lambda p: (p, 0, 0, 0))
    smem = pl.BlockSpec(memory_space=pltpu.SMEM)
    anywhere = pl.BlockSpec(memory_space=pl.ANY)
    parts = [shard_view(p, depth) for p in parts]
    pieces = []
    for a in (0, 1):
        part = parts[a].shape[4] // 2
        pieces += [(a, 0, part), (a, part, part)]
    pieces.append((2, 0, parts[2].shape[4]))
    count = len(pieces) + 1
    out = pl.pallas_call(
        functools.partial(attend_bwd_kernel, depth, pieces),
        grid=(pairs,),
        in_specs=[smem, smem, spec(0), spec(1), spec(2), col, col, stat] + [anywhere] * 4,
        out_specs=[col, col, col, stat]
        + [pl.BlockSpec(p.shape[4:], lambda p: (0, 0)) for p in parts]
        + [anywhere],
        out_shape=[jax.ShapeDtypeStruct((rows, width), BF16)] * 3
        + [jax.ShapeDtypeStruct((pairs, 2, blocks, BLOCK), F32)]
        + [jax.ShapeDtypeStruct(p.shape[4:], F32) for p in parts]
        + [jax.ShapeDtypeStruct((2, rows // 2, width), BF16)],
        scratch_shapes=[
            pltpu.VMEM((blocks, 128, BLOCK), BF16),
            pltpu.VMEM((rows, 128), F32),
            pltpu.VMEM((rows, 128), F32),
            pltpu.SemaphoreType.DMA((count,)),
            pltpu.SemaphoreType.DMA((count, 3 + depth)),
            pltpu.SemaphoreType.DMA((count, 3 + depth)),
            pltpu.VMEM((rows // 2, width), BF16),
        ]
        + scatter_scratch([(count, parts[a].shape[5], parts[a].dtype) for a, _, count in pieces], depth),
        compiler_params=pltpu.CompilerParams(
            vmem_limit_bytes=VMEM_CAP, collective_id=collective_id, has_side_effects=True
        ),
        name="attend_bwd",
    )(lengths, hs, qkv, qkv, qkv, mixed, d_scaled, lse, *parts, layer)
    return out[:4], out[4:7], out[7]


def row_norm(values):
    center = values - jnp.mean(values, axis=-1, keepdims=True)
    spread = jnp.mean(center * center, axis=-1, keepdims=True)
    rstd = lax.rsqrt(spread + EPS)
    return center * rstd, rstd


def row_norm_back(grad, hat, rstd):
    first = jnp.mean(grad, axis=-1, keepdims=True)
    second = jnp.mean(grad * hat, axis=-1, keepdims=True)
    return rstd * (grad - first - hat * second)


def fold_rows(values):
    return jnp.sum(values.reshape(values.shape[0] // 8, 8, values.shape[1]), axis=0)


def resident(shape):
    return pl.BlockSpec(shape, lambda i: (0,) * len(shape), pipeline_mode=pl.Buffered(1))


GELU_A = math.sqrt(2.0 / math.pi)
GELU_B = 0.044715
CHUNK = 512


def middle_kernel(
    sc_ref, x_ref, dy_ref, wout, w1, w2, nar, wide,
    lay_ref, post_ref, fin_ref, act_ref, din_ref, dhid_ref, dlow_ref, dsc_ref, gn_ref, gw_ref,
    n_s, gp_s, dn_s,
):
    @pl.when(pl.program_id(0) == 0)
    def _():
        gn_ref[...] = jnp.zeros_like(gn_ref)
        gw_ref[...] = jnp.zeros_like(gw_ref)

    tile, width = x_ref.shape
    ff = w1.shape[1]
    chunks = ff // CHUNK
    ahat, arstd = row_norm(sc_ref[...].astype(F32))
    post = (ahat * nar[4:5] + nar[5:6]).astype(BF16)
    post_ref[...] = post
    hidden = x_ref[...].astype(F32) + mm(post, wout[...]) + nar[6:7]
    hhat, hrstd = row_norm(hidden)
    fin = (hhat * nar[7:8] + nar[8:9]).astype(BF16)
    fin_ref[...] = fin

    def lanes(values):
        return jnp.sum(values.reshape(tile, CHUNK // 128, 128), axis=1)

    def inner(j, total):
        at = pl.ds(pl.multiple_of(j * CHUNK, CHUNK), CHUNK)
        u = mm(fin, w1[:, at]) + wide[0:1, at]
        u2 = u * u
        t = jnp.tanh(u * (GELU_A + GELU_A * GELU_B * u2))
        half = 0.5 * (1.0 + t)
        n = u * half
        gp_s[:, at] = (half + n * (1.0 - t) * (GELU_A + 3.0 * GELU_A * GELU_B * u2)).astype(BF16)
        n_s[:, at] = n
        for q in range(CHUNK // 128):
            total = total + n[:, q * 128 : (q + 1) * 128]
        return total

    zero = jnp.zeros((tile, 128), F32)
    total = lax.fori_loop(0, chunks, inner, zero, unroll=8)
    nmean = jnp.sum(total, axis=-1, keepdims=True) / ff

    def square(j, total):
        at = pl.ds(pl.multiple_of(j * 128, 128), 128)
        c = n_s[:, at] - nmean
        return total + c * c

    total = lax.fori_loop(0, ff // 128, square, zero, unroll=4)
    nrstd = lax.rsqrt(jnp.sum(total, axis=-1, keepdims=True) / ff + EPS)
    dyl = dy_ref[...]

    def outer(j, carry):
        acc, s1, s2 = carry
        at = pl.ds(pl.multiple_of(j * CHUNK, CHUNK), CHUNK)
        nh = (n_s[:, at] - nmean) * nrstd
        n_s[:, at] = nh
        act = (nh * wide[1:2, at] + wide[2:3, at]).astype(BF16)
        act_ref[:, at] = act
        acc = acc + mm(act, w2[at, :])
        da = mm(dyl, w2[at, :], NT)
        danh = da * nh
        gw_ref[1, :, at] += fold_rows(danh)
        gw_ref[2, :, at] += fold_rows(da)
        gain = wide[1:2, at]
        dg = da * gain
        dgn = danh * gain
        dn_s[:, at] = dg
        for q in range(CHUNK // 128):
            s1 = s1 + dg[:, q * 128 : (q + 1) * 128]
            s2 = s2 + dgn[:, q * 128 : (q + 1) * 128]
        return acc, s1, s2

    acc, s1, s2 = lax.fori_loop(0, chunks, outer, (jnp.zeros((tile, width), F32), zero, zero), unroll=8)
    lay_ref[...] = (hidden + acc + nar[9:10]).astype(BF16)
    s1 = jnp.sum(s1, axis=-1, keepdims=True) / ff
    s2 = jnp.sum(s2, axis=-1, keepdims=True) / ff

    def inner_back(j, acc):
        at = pl.ds(pl.multiple_of(j * CHUNK, CHUNK), CHUNK)
        dn = nrstd * (dn_s[:, at] - s1 - n_s[:, at] * s2)
        din = (dn * gp_s[:, at].astype(F32)).astype(BF16)
        din_ref[:, at] = din
        gw_ref[0, :, at] += fold_rows(din.astype(F32))
        return acc + mm(din, w1[:, at], NT)

    dffn = lax.fori_loop(0, chunks, inner_back, jnp.zeros((tile, width), F32), unroll=8)
    dy = dyl.astype(F32)
    gn_ref[5] += fold_rows(dy)
    gn_ref[3] += fold_rows(dffn * hhat)
    gn_ref[4] += fold_rows(dffn)
    dhid = dy + row_norm_back(dffn * nar[7:8], hhat, hrstd)
    dhid_ref[...] = dhid
    gn_ref[2] += fold_rows(dhid)
    dlow = dhid.astype(BF16)
    dlow_ref[...] = dlow
    dpost = mm(dlow, wout[...], NT)
    gn_ref[0] += fold_rows(dpost * ahat)
    gn_ref[1] += fold_rows(dpost)
    dsc_ref[...] = row_norm_back(dpost * nar[4:5], ahat, arstd).astype(BF16)


def middle(scaled, x, dy, wout, w1, w2, narrow, wide):
    rows, width = x.shape
    ff = w1.shape[1]
    tile = 256
    thin = pl.BlockSpec((tile, width), lambda i: (i, 0))
    fat = pl.BlockSpec((tile, ff), lambda i: (i, 0))
    keep = lambda shape: pl.BlockSpec(shape, lambda i: (0,) * len(shape))
    return pl.pallas_call(
        middle_kernel,
        grid=(rows // tile,),
        in_specs=[
            thin, thin, thin,
            resident(wout.shape), resident(w1.shape), resident(w2.shape),
            resident(narrow.shape), resident(wide.shape),
        ],
        out_specs=[thin, thin, thin, fat, fat, thin, thin, thin, keep((6, 8, width)), keep((3, 8, ff))],
        out_shape=[
            jax.ShapeDtypeStruct((rows, width), BF16),
            jax.ShapeDtypeStruct((rows, width), BF16),
            jax.ShapeDtypeStruct((rows, width), BF16),
            jax.ShapeDtypeStruct((rows, ff), BF16),
            jax.ShapeDtypeStruct((rows, ff), BF16),
            jax.ShapeDtypeStruct((rows, width), F32),
            jax.ShapeDtypeStruct((rows, width), BF16),
            jax.ShapeDtypeStruct((rows, width), BF16),
            jax.ShapeDtypeStruct((6, 8, width), F32),
            jax.ShapeDtypeStruct((3, 8, ff), F32),
        ],
        scratch_shapes=[
            pltpu.VMEM((tile, ff), F32),
            pltpu.VMEM((tile, ff), BF16),
            pltpu.VMEM((tile, ff), F32),
        ],
        compiler_params=pltpu.CompilerParams(vmem_limit_bytes=VMEM_CAP),
        name="middle",
    )(scaled, x, dy, wout, w1, w2, narrow, wide)


def enter_kernel(depth, counts, *refs):
    me = Place(depth)
    base = len(counts)
    smalls = refs[:base]
    qkv_shard, out_shard, fc1_shard, tok = refs[base : base + 4]
    qkv_whole, out_whole, fc1_whole, x_out, normed_out, qkv_out, narrow, wide, hs = refs[base + 4 : base + 13]
    small, small_stage, small_whole, qkv_stage, out_stage, fc1_stage, weight = refs[base + 13 : base + 20]
    tok_own, tok_got, normed_tiles, qkv_tiles = refs[base + 20 : base + 24]
    local, send, recv, small_sem, tok_sem, go, come, put_sem, tile_sem = refs[base + 24 : base + 33]
    smalls_here = refs[base + 33 :]
    y = me.y
    qrows, frows = qkv_shard.shape[0] // 2, fc1_shard.shape[0] // 2
    sems = lambda n: (local.at[n], send.at[n], recv.at[n])
    tiny = Gather(me, small, small_stage, small_whole, 0, 16, *sems(0))
    q_a = Gather(me, qkv_shard, qkv_stage, weight, 0, qrows, *sems(1))
    q_b = Gather2(me, qkv_shard, qkv_stage, weight, qrows, qrows, *sems(2))
    w_out = Gather2(me, out_shard, out_stage, out_whole, 0, out_shard.shape[0], *sems(3))
    f_a = Gather(me, fc1_shard, fc1_stage, fc1_whole, 0, frows, *sems(4))
    f_b = Gather(me, fc1_shard, fc1_stage, fc1_whole, frows, frows, *sems(5))
    copies = [pltpu.make_async_copy(s, h, small_sem.at[n]) for n, (s, h) in enumerate(zip(smalls, smalls_here))]
    own = pltpu.make_async_copy(tok.at[y], tok_own, tok_sem)
    for copy in copies + [own]:
        copy.start()
    for g in (q_a, q_b, w_out, f_a, f_b):
        g.ready()
    for copy in copies:
        copy.wait()
    rows = []
    for ref, count in zip(smalls_here, counts):
        row = ref[...].astype(F32).reshape(1, count)
        rows.append(row if count == 128 else jnp.concatenate([row, jnp.zeros((1, 128 - count), F32)], axis=1))
    rows.append(jnp.zeros((16 - len(counts), 128), F32))
    small[...] = jnp.concatenate(rows, axis=0).astype(BF16)
    tiny.ready()
    half, width = tok_own.shape
    cut = half // 4

    def trade(n):
        span = pl.ds(n * cut, cut if n == 0 else half - cut)
        return remote(tok.at[1 - y, span], tok_got.at[span], go.at[n], come.at[n], me.next_y)

    me.greet()
    tiny.begin()
    q_a.begin()
    q_b.begin()
    trade(0).start()
    tiny.spread()
    q_b.pass_z()
    q_a.spread()
    tiny.from_y()
    tiny.from_x()
    w_out.begin()
    tiny.from_corner()
    q_a.from_y()
    trade(1).start()
    q_b.pass_x()
    q_b.pass_twin()
    w_out.pass_z()
    tiny.end()
    part = counts[0]
    each = 128 // part
    for d in range(depth * 8 // each):
        tiles = []
        for k in range(d * each, (d + 1) * each):
            tile = small_whole[k // 8, k // 4 % 2, k // 2 % 2, k % 2].astype(F32)
            tiles.append(tile[:, 0:part])
            wide[0:3, k * 128 : (k + 1) * 128] = tile[10:13]
        narrow[:, d * 128 : (d + 1) * 128] = jnp.concatenate(tiles, axis=1)
    hs[...] = jnp.concatenate(
        [small_whole[0, 0, 0, k].astype(F32)[13:14, 0 : counts[13]] for k in range(2)], axis=1
    )
    q_a.from_x()
    q_a.from_corner()
    f_a.begin()
    f_b.begin()
    w_out.pass_x()
    w_out.pass_twin()
    q_b.arrived()
    q_b.pass_twin_far()
    q_a.end()
    q_b.end()
    put_weight = pltpu.make_async_copy(weight, qkv_whole, put_sem.at[0])
    put_weight.start()
    own.wait()
    put_own = pltpu.make_async_copy(tok_own, x_out.at[y], put_sem.at[1])
    put_own.start()
    tile_rows = normed_tiles.shape[1]
    tiles = normed_tiles.shape[0]

    def puts(i, at):
        span = pl.ds(at * half + i * tile_rows, tile_rows)
        return (
            pltpu.make_async_copy(normed_tiles.at[i], normed_out.at[span], tile_sem.at[0, i]),
            pltpu.make_async_copy(qkv_tiles.at[i], qkv_out.at[span], tile_sem.at[1, i]),
        )

    def project(source, at):
        def body(i, _):
            hat, _ = row_norm(source[pl.ds(i * tile_rows, tile_rows), :].astype(F32))
            normed = (hat * narrow[0:1] + narrow[1:2]).astype(BF16)
            normed_tiles[i] = normed
            for j in range(3 * width // 512):
                span = slice(j * 512, (j + 1) * 512)
                piece = mm(normed, weight[:, :, :, :, :, span].reshape(width, 512))
                third, start = j * 512 // width, j * 512 % width
                if third != 1:
                    row = 2 + third // 2
                    piece = piece + narrow[row : row + 1, start : start + 512]
                qkv_tiles[i, :, span] = piece.astype(BF16)
            for put in puts(i, at):
                put.start()
            return 0

        lax.fori_loop(0, tiles, body, 0)

    project(tok_own, y)
    w_out.arrived()
    w_out.pass_twin_far()
    for n in range(2):
        trade(n).wait()
    put_got = pltpu.make_async_copy(tok_got, x_out.at[1 - y], put_sem.at[2])
    put_got.start()
    for i in range(tiles):
        for put in puts(i, y):
            put.wait()
    project(tok_got, 1 - y)
    f_a.landed()
    f_b.landed()
    w_out.end()
    for i in range(tiles):
        for put in puts(i, 1 - y):
            put.wait()
    put_weight.wait()
    put_own.wait()
    put_got.wait()


def enter(smalls, qkv_weight, out_weight, fc1_weight, tokens, depth, collective_id):
    shards = [qkv_weight, out_weight, fc1_weight]
    counts = [s.shape[0] for s in smalls]
    _, half, width = tokens.shape
    tile = 256
    anywhere = pl.BlockSpec(memory_space=pl.ANY)
    vmem = pl.BlockSpec(memory_space=pltpu.VMEM)
    whole = lambda s: (depth, 2, 2, 2) + s.shape
    out = pl.pallas_call(
        functools.partial(enter_kernel, depth, counts),
        in_specs=[anywhere] * (len(counts) + 4),
        out_specs=[anywhere] * 6 + [vmem] * 3,
        out_shape=[jax.ShapeDtypeStruct(whole(s), s.dtype) for s in shards]
        + [
            jax.ShapeDtypeStruct(tokens.shape, tokens.dtype),
            jax.ShapeDtypeStruct((2 * half, width), BF16),
            jax.ShapeDtypeStruct((2 * half, 3 * width), BF16),
            jax.ShapeDtypeStruct((16, depth * 8 * counts[0]), F32),
            jax.ShapeDtypeStruct((8, depth * 8 * counts[10]), F32),
            jax.ShapeDtypeStruct((1, 2 * counts[13]), F32),
        ],
        scratch_shapes=[
            pltpu.VMEM((16, 128), BF16),
            pltpu.VMEM((16, 128), BF16),
            pltpu.VMEM((depth, 2, 2, 2, 16, 128), BF16),
        ]
        + [pltpu.VMEM(s.shape, s.dtype) for s in shards]
        + [
            pltpu.VMEM(whole(qkv_weight), BF16),
            pltpu.VMEM((half, width), BF16),
            pltpu.VMEM((half, width), BF16),
            pltpu.VMEM((half // tile, tile, width), BF16),
            pltpu.VMEM((half // tile, tile, 3 * width), BF16),
            pltpu.SemaphoreType.DMA((6,)),
            pltpu.SemaphoreType.DMA((6, 2 * depth + 3)),
            pltpu.SemaphoreType.DMA((6, 2 * depth + 3)),
            pltpu.SemaphoreType.DMA((len(counts),)),
            pltpu.SemaphoreType.DMA,
            pltpu.SemaphoreType.DMA((2,)),
            pltpu.SemaphoreType.DMA((2,)),
            pltpu.SemaphoreType.DMA((3,)),
            pltpu.SemaphoreType.DMA((2, half // tile)),
        ]
        + [pltpu.VMEM((n,), BF16) for n in counts],
        compiler_params=pltpu.CompilerParams(
            collective_id=collective_id, has_side_effects=True, vmem_limit_bytes=VMEM_CAP
        ),
        name="enter",
    )(*smalls, *shards, tokens)
    return flat(out[0]), flat(out[1]), out[2], out[3].reshape(-1, width), *out[4:]


def flat(whole):
    return whole.reshape((-1,) + whole.shape[5:])


def leave_kernel(depth, part, heads, *refs):
    dq_ref, dk_ref, dv_ref, x_ref, dhid_ref, w_ref, p_ref = refs[:7]
    parts = refs[7:10]
    thin_ref, fat_ref, delta_ref, hs_ref = refs[10:14]
    out, qkv_sum, small_sum = refs[14:17]
    local, send, recv, go, come, store, g_acc, thin, fat, small, leaving, landing, stage = refs[17:30]
    scratch = refs[30:]
    me = Place(depth)
    step = pl.program_id(0)
    half_tiles = leaving.shape[0]
    tile, width = x_ref.shape
    rows = parts[0].shape[4]
    scatters = [
        Scatter(
            me, parts[n], 0, rows, *scratch[4 * n : 4 * n + 4], local.at[n], send.at[n], recv.at[n],
            qkv_sum.at[:, pl.ds(n * width, width)],
        )
        for n in range(3)
    ]
    smalls = Scatter(me, small, 0, 16, *scratch[12:16], local.at[3], send.at[3], recv.at[3], small_sum)

    def trade(j):
        return remote(leaving.at[j], landing.at[j], go.at[j], come.at[j], me.next_y)

    def put(y, j):
        return pltpu.make_async_copy(stage.at[j], out.at[y, pl.ds(j * tile, tile)], store.at[j])

    @pl.when(step == 0)
    def _():
        g_acc[...] = jnp.zeros_like(g_acc)
        me.greet()
        for s in scatters:
            s.begin()

    @pl.when(step == 2)
    def _():
        for s in scatters:
            s.across()

    hat, rstd = row_norm(x_ref[...].astype(F32))
    dnormed = mm(dq_ref[...], w_ref[:, 0:width], NT)
    dnormed = dnormed + mm(dk_ref[...], w_ref[:, width : 2 * width], NT)
    dnormed = dnormed + mm(dv_ref[...], w_ref[:, 2 * width : 3 * width], NT)
    g_acc[0] += fold_rows(dnormed * hat)
    g_acc[1] += fold_rows(dnormed)
    g_acc[2] += fold_rows(dq_ref[...].astype(F32))
    g_acc[3] += fold_rows(dv_ref[...].astype(F32))
    grad = dhid_ref[...] + row_norm_back(dnormed * p_ref[0:1], hat, rstd)

    @pl.when(step < half_tiles)
    def _():
        leaving[step] = grad.astype(BF16)
        trade(step).start()

    @pl.when(step >= half_tiles)
    def _():
        stage[step - half_tiles] = grad
        put(me.y, step - half_tiles).start()

    @pl.when(step == pl.num_programs(0) - 1)
    def _():
        thin[...] = jnp.zeros_like(thin)
        fat[...] = jnp.zeros_like(fat)
        for k in range(4):
            thin[k : k + 1, :] = jnp.sum(g_acc[k], axis=0, keepdims=True)
        for k in range(6):
            thin[4 + k : 5 + k, :] = jnp.sum(thin_ref[k], axis=0, keepdims=True)
        for k in range(3):
            fat[10 + k : 11 + k, :] = jnp.sum(fat_ref[k], axis=0, keepdims=True)
        lanes = lax.broadcasted_iota(jnp.int32, (1, 128), 1)
        scale = jnp.zeros((1, 128), F32)
        for p in range(delta_ref.shape[0]):
            for h in range(2):
                scale = jnp.where(lanes == 2 * p + h, jnp.sum(delta_ref[p, h]), scale)
        scale = scale / jnp.concatenate([hs_ref[...], jnp.ones((1, 128 - 2 * heads), F32)], axis=1)
        each = 128 // part
        is_scale = lax.broadcasted_iota(jnp.int32, (16, 128), 0) == 13
        for d in range(depth * 8):
            block = thin[:, d // each * 128 : (d // each + 1) * 128]
            turn = d % each * part
            block = pltpu.roll(block, 128 - turn, 1) if turn else block
            block = block + fat[:, d * 128 : (d + 1) * 128]
            row = pltpu.roll(scale, 128 - heads, 1) if d % 2 else scale
            small[d // 8, d // 4 % 2, d // 2 % 2, d % 2] = jnp.where(is_scale, row, block)
        smalls.begin()
        v, k, q = scatters[2], scatters[1], scatters[0]
        v.along_x()
        smalls.across()
        k.along_x()
        v.along_y()
        smalls.along_x()
        q.along_x()
        k.along_y()
        smalls.along_y()
        v.end()
        q.along_y()
        for j in range(half_tiles):
            trade(j).wait()
            put(me.y, j).wait()
            stage[j] = landing[j].astype(F32)
            put(1 - me.y, j).start()
        k.end()
        smalls.end()
        q.end()
        for j in range(half_tiles):
            put(1 - me.y, j).wait()


def leave(dq, dk, dv, x, dhid, weight, params, parts, thin, fat, delta, hs, depth, collective_id):
    rows, width = x.shape
    tile = 256
    tiles = rows // tile
    parts = [shard_view(p, depth) for p in parts]
    part = width // (depth * 8)
    heads = hs.shape[1] // 2

    def at(i):
        return ((i + tiles // 2 * (1 - lax.axis_index("sp"))) % tiles, 0)

    block = pl.BlockSpec((tile, width), at)
    anywhere = pl.BlockSpec(memory_space=pl.ANY)
    pieces = [(p.shape[4], p.shape[5], p.dtype) for p in parts] + [(16, 128, F32)]
    keep = lambda shape: pl.BlockSpec(shape, lambda i: (0,) * len(shape))
    out_shape = [
        jax.ShapeDtypeStruct((2, rows // 2, width), F32),
        jax.ShapeDtypeStruct((parts[0].shape[4], 3 * width), F32),
        jax.ShapeDtypeStruct((16, 128), F32),
    ]
    return pl.pallas_call(
        functools.partial(leave_kernel, depth, part, heads),
        grid=(tiles,),
        in_specs=[block] * 5
        + [resident(weight.shape), resident(params.shape)]
        + [anywhere] * 3
        + [resident(a.shape) for a in (thin, fat, delta, hs)],
        out_specs=[anywhere, keep(out_shape[1].shape), keep(out_shape[2].shape)],
        out_shape=out_shape,
        scratch_shapes=[
            pltpu.SemaphoreType.DMA((4,)),
            pltpu.SemaphoreType.DMA((4, 3 + depth)),
            pltpu.SemaphoreType.DMA((4, 3 + depth)),
            pltpu.SemaphoreType.DMA((tiles // 2,)),
            pltpu.SemaphoreType.DMA((tiles // 2,)),
            pltpu.SemaphoreType.DMA((tiles // 2,)),
            pltpu.VMEM((4, 8, width), F32),
            pltpu.VMEM((16, width), F32),
            pltpu.VMEM((16, fat.shape[2]), F32),
            pltpu.VMEM((depth, 2, 2, 2, 16, 128), F32),
            pltpu.VMEM((tiles // 2, tile, width), BF16),
            pltpu.VMEM((tiles // 2, tile, width), BF16),
            pltpu.VMEM((tiles // 2, tile, width), F32),
        ]
        + scatter_scratch(pieces, depth),
        compiler_params=pltpu.CompilerParams(
            collective_id=collective_id, has_side_effects=True, vmem_limit_bytes=VMEM_CAP
        ),
        name="leave",
    )(dq, dk, dv, x, dhid, weight, params, *parts, thin, fat, delta, hs)


def fast_shards(
    tokens, doc_lengths, out_cotangent, in_gain, in_bias, qkv_weight, q_bias, v_bias, head_scale, attn_gain,
    attn_bias, out_weight, out_bias, ffn_gain, ffn_bias, fc1_weight, fc1_bias, mid_gain, mid_bias, fc2_weight,
    fc2_bias,
):
    depth = lax.axis_size("dp") // 4
    devices = depth * 8
    half = tokens.shape[1]
    rows = 2 * half
    width = tokens.shape[2]
    me = lax.axis_index("sp")

    narrow_in = [in_gain, in_bias, q_bias, v_bias, attn_gain, attn_bias, out_bias, ffn_gain, ffn_bias, fc2_bias]
    wide_in = [fc1_bias, mid_gain, mid_bias]
    part = width // devices
    heads_each = head_scale.shape[0]
    wqkv, wout, begun, x, normed, qkv, narrow, wide, hs = enter(
        narrow_in + wide_in + [head_scale], qkv_weight, out_weight, fc1_weight, tokens, depth, 0
    )
    scaled, mixed, lse, w1, w2, dy = attend_fwd(qkv, doc_lengths, hs, begun, fc2_weight, out_cotangent, depth, 1)
    w1, w2 = flat(w1), flat(w2)
    layer, post, ffn_in, active, d_inner, d_hidden, d_low, d_scaled, grads_narrow, grads_wide = middle(
        scaled, x, dy, wout, w1, w2, narrow, wide
    )

    def weight_grad(left, right):
        return jnp.einsum("ti,tj->ij", left, right, preferred_element_type=F32).astype(BF16)

    g_fc2 = weight_grad(active, dy)
    g_fc1 = weight_grad(ffn_in, d_inner)
    g_out = weight_grad(post, d_low)
    (dq, dk, dv, delta), (s_fc2, s_fc1, s_out), layer_out = attend_bwd(
        qkv, mixed, d_scaled, lse, doc_lengths, hs, [g_fc2, g_fc1, g_out], layer, depth, 2
    )
    g_q = weight_grad(normed, dq)
    g_k = weight_grad(normed, dk)
    g_v = weight_grad(normed, dv)
    input_grad, s_qkv, s_small = leave(
        dq, dk, dv, x, d_hidden, wqkv, narrow, [g_q, g_k, g_v], grads_narrow, grads_wide, delta, hs, depth, 3
    )
    nar = [s_small[k, :part] for k in range(10)]
    wid = [s_small[10 + k] for k in range(3)]
    s_hs = s_small[13, :heads_each]
    return (
        layer_out, input_grad, nar[0], nar[1], s_qkv, nar[2], nar[3], s_hs, nar[4], nar[5], s_out, nar[6], nar[7],
        nar[8], s_fc1, wid[0], wid[1], wid[2], s_fc2, nar[9],
    )


LONGEST = 2048


def layer_norm(values, norm_gain, norm_shift):
    center = values - jnp.mean(values, axis=-1, keepdims=True)
    spread = jnp.mean(center * center, axis=-1, keepdims=True)
    return center * lax.rsqrt(spread + EPS) * norm_gain + norm_shift


def doc_index(lengths, row_count):
    seq_ends = jnp.cumsum(lengths)
    places = jnp.arange(row_count, dtype=jnp.int32)
    return jnp.sum((places[:, None] >= seq_ends[None, :]).astype(jnp.int32), axis=1)


def block_scores(query_block, key_heads, doc_query, doc_keys, pos_query, pos_keys, score_scale):
    scores = (
        jnp.einsum("qhd,khd->hqk", query_block, key_heads, preferred_element_type=jnp.float32)
        * score_scale
    )
    allowed = (doc_query[:, None] == doc_keys[None, :]) & (pos_keys[None, :] <= pos_query[:, None])
    return jnp.where(allowed[None], scores, -1e30)


def reduce_grads(grad_set):
    return (
        lax.psum_scatter(grad_set[0], ("dp", "sp"), scatter_dimension=0, tiled=True),
        lax.psum_scatter(grad_set[1], ("dp", "sp"), scatter_dimension=0, tiled=True),
        lax.psum_scatter(grad_set[2], ("dp", "sp"), scatter_dimension=0, tiled=True),
        lax.psum_scatter(grad_set[3], ("dp", "sp"), scatter_dimension=0, tiled=True),
        lax.psum_scatter(grad_set[4], ("dp", "sp"), scatter_dimension=0, tiled=True),
        lax.psum_scatter(grad_set[5], ("dp", "sp"), scatter_dimension=0, tiled=True),
        lax.psum_scatter(grad_set[6], ("dp", "sp"), scatter_dimension=0, tiled=True),
        lax.psum_scatter(grad_set[7], ("dp", "sp"), scatter_dimension=0, tiled=True),
        lax.psum_scatter(grad_set[8], ("dp", "sp"), scatter_dimension=0, tiled=True),
        lax.psum_scatter(grad_set[9], ("dp", "sp"), scatter_dimension=0, tiled=True),
        lax.psum_scatter(grad_set[10], ("dp", "sp"), scatter_dimension=0, tiled=True),
        lax.psum_scatter(grad_set[11], ("dp", "sp"), scatter_dimension=0, tiled=True),
        lax.psum_scatter(grad_set[12], ("dp", "sp"), scatter_dimension=0, tiled=True),
        lax.psum_scatter(grad_set[13], ("dp", "sp"), scatter_dimension=0, tiled=True),
        lax.psum_scatter(grad_set[14], ("dp", "sp"), scatter_dimension=0, tiled=True),
        lax.psum_scatter(grad_set[15], ("dp", "sp"), scatter_dimension=0, tiled=True),
        lax.psum_scatter(grad_set[16], ("dp", "sp"), scatter_dimension=0, tiled=True),
    )


def shards(
    tokens,
    doc_lengths,
    out_cotangent,
    in_gain,
    in_bias,
    qkv_weight,
    q_bias,
    v_bias,
    head_scale,
    attn_gain,
    attn_bias,
    out_weight,
    out_bias,
    ffn_gain,
    ffn_bias,
    fc1_weight,
    fc1_bias,
    mid_gain,
    mid_bias,
    fc2_weight,
    fc2_bias,
):
    micro_count = tokens.shape[0]
    tok_count = tokens.shape[1]
    model_width = tokens.shape[2]
    sp_count = lax.axis_size("sp")
    group_rows = tok_count * sp_count
    local_width = model_width // sp_count
    head_local = head_scale.shape[0]
    head_dim = local_width // head_local
    score_scale = 1.0 / math.sqrt(head_dim)
    window_rows = LONGEST
    block_rows = min(512, window_rows)
    block_count = group_rows // block_rows
    head_gains = head_scale.astype(jnp.float32)
    positions = jnp.arange(group_rows, dtype=jnp.int32)
    starts = jnp.arange(block_count, dtype=jnp.int32) * block_rows

    def collect():
        return (
            lax.all_gather(in_gain, ("dp", "sp"), axis=0, tiled=True),
            lax.all_gather(in_bias, ("dp", "sp"), axis=0, tiled=True),
            lax.all_gather(qkv_weight, ("dp", "sp"), axis=0, tiled=True),
            lax.all_gather(q_bias, ("dp", "sp"), axis=0, tiled=True),
            lax.all_gather(v_bias, ("dp", "sp"), axis=0, tiled=True),
            lax.all_gather(attn_gain, ("dp", "sp"), axis=0, tiled=True),
            lax.all_gather(attn_bias, ("dp", "sp"), axis=0, tiled=True),
            lax.all_gather(out_weight, ("dp", "sp"), axis=0, tiled=True),
            lax.all_gather(out_bias, ("dp", "sp"), axis=0, tiled=True),
            lax.all_gather(ffn_gain, ("dp", "sp"), axis=0, tiled=True),
            lax.all_gather(ffn_bias, ("dp", "sp"), axis=0, tiled=True),
            lax.all_gather(fc1_weight, ("dp", "sp"), axis=0, tiled=True),
            lax.all_gather(fc1_bias, ("dp", "sp"), axis=0, tiled=True),
            lax.all_gather(mid_gain, ("dp", "sp"), axis=0, tiled=True),
            lax.all_gather(mid_bias, ("dp", "sp"), axis=0, tiled=True),
            lax.all_gather(fc2_weight, ("dp", "sp"), axis=0, tiled=True),
            lax.all_gather(fc2_bias, ("dp", "sp"), axis=0, tiled=True),
        )

    def split_heads(heads_in):
        query_heads = heads_in[:, 0].reshape(group_rows, head_local, head_dim)
        key_heads = heads_in[:, 1].reshape(group_rows, head_local, head_dim)
        value_heads = heads_in[:, 2].reshape(group_rows, head_local, head_dim)
        return (query_heads, key_heads, value_heads)

    def attend_back(heads_in, lengths, log_total, grad_mixed):
        query_heads, key_heads, value_heads = split_heads(heads_in)
        doc_ids = doc_index(lengths, group_rows)

        def one_block(block_carry, pair):
            grad_keys, grad_values = block_carry
            row_start, block_lse = pair
            query_block = lax.dynamic_slice_in_dim(query_heads, row_start, block_rows, 0)
            grad_block = lax.dynamic_slice_in_dim(grad_mixed, row_start, block_rows, 0)
            masked = block_scores(
                query_block,
                key_heads,
                lax.dynamic_slice_in_dim(doc_ids, row_start, block_rows, 0),
                doc_ids,
                lax.dynamic_slice_in_dim(positions, row_start, block_rows, 0),
                positions,
                score_scale,
            )
            prob_rows = jnp.exp(masked - block_lse[:, :, None])
            value_part = jnp.einsum(
                "hqk,qhd->khd",
                prob_rows.astype(jnp.bfloat16),
                grad_block,
                preferred_element_type=jnp.float32,
            )
            grad_probs = jnp.einsum(
                "qhd,khd->hqk", grad_block, value_heads, preferred_element_type=jnp.float32
            )
            row_inner = jnp.sum(prob_rows * grad_probs, axis=-1, keepdims=True)
            grad_scores = (prob_rows * (grad_probs - row_inner)).astype(jnp.bfloat16)
            grad_query = (
                jnp.einsum(
                    "hqk,khd->qhd", grad_scores, key_heads, preferred_element_type=jnp.float32
                )
                * score_scale
            )
            key_part = jnp.einsum(
                "hqk,qhd->khd", grad_scores, query_block, preferred_element_type=jnp.float32
            )
            grad_keys = grad_keys + key_part
            grad_values = grad_values + value_part
            return ((grad_keys, grad_values), grad_query)

        zero_heads = jnp.zeros((group_rows, head_local, head_dim), jnp.float32)
        (grad_keys, grad_values), grad_queries = lax.scan(
            one_block, (zero_heads, zero_heads), (starts, log_total)
        )
        stacked = jnp.stack(
            [
                grad_queries.reshape(group_rows, local_width),
                (grad_keys * score_scale).reshape(group_rows, local_width),
                grad_values.reshape(group_rows, local_width),
            ],
            axis=1,
        )
        return stacked.astype(jnp.bfloat16)

    outputs = []
    input_grads = []
    total_grads = None
    scale_total = jnp.zeros((head_local,), jnp.float32)
    for micro_index in range(micro_count):
        forward_set = collect()
        (
            forward_wide_in_gain,
            forward_wide_in_bias,
            forward_wide_qkv,
            forward_wide_q_bias,
            forward_wide_v_bias,
            forward_wide_attn_gain,
            forward_wide_attn_bias,
            forward_wide_out,
            forward_wide_out_bias,
            forward_wide_ffn_gain,
            forward_wide_ffn_bias,
            forward_wide_fc1,
            forward_wide_fc1_bias,
            forward_wide_mid_gain,
            forward_wide_mid_bias,
            forward_wide_fc2,
            forward_wide_fc2_bias,
        ) = forward_set
        forward_tok_rows = tokens[micro_index].astype(jnp.float32)
        forward_lengths = doc_lengths[0, micro_index]
        forward_normed = layer_norm(
            forward_tok_rows,
            forward_wide_in_gain.astype(jnp.float32),
            forward_wide_in_bias.astype(jnp.float32),
        ).astype(jnp.bfloat16)
        bias_row = jnp.concatenate(
            [forward_wide_q_bias, jnp.zeros_like(forward_wide_q_bias), forward_wide_v_bias]
        ).astype(jnp.float32)
        projected = (
            jnp.dot(forward_normed, forward_wide_qkv, preferred_element_type=jnp.float32) + bias_row
        )
        qkv_sent = projected.astype(jnp.bfloat16).reshape(tok_count, 3, model_width)
        forward_heads_in = lax.all_to_all(qkv_sent, "sp", split_axis=2, concat_axis=0, tiled=True)
        attend_query_heads, attend_key_heads, attend_value_heads = split_heads(forward_heads_in)
        attend_doc_ids = doc_index(forward_lengths, group_rows)

        def attend_one_block(row_start):
            query_block = lax.dynamic_slice_in_dim(attend_query_heads, row_start, block_rows, 0)
            masked = block_scores(
                query_block,
                attend_key_heads,
                lax.dynamic_slice_in_dim(attend_doc_ids, row_start, block_rows, 0),
                attend_doc_ids,
                lax.dynamic_slice_in_dim(positions, row_start, block_rows, 0),
                positions,
                score_scale,
            )
            row_max = jnp.max(masked, axis=-1, keepdims=True)
            raised = jnp.exp(masked - row_max)
            row_total = jnp.sum(raised, axis=-1, keepdims=True)
            prob_rows = (raised / row_total).astype(jnp.bfloat16)
            head_mixed = jnp.einsum(
                "hqk,khd->qhd", prob_rows, attend_value_heads, preferred_element_type=jnp.float32
            )
            return (head_mixed, (row_max + jnp.log(row_total))[:, :, 0])

        head_mixed, attend_log_total = lax.map(attend_one_block, starts)
        forward_head_mixed = head_mixed.reshape(group_rows, head_local, head_dim)
        scaled = (
            (forward_head_mixed * head_gains[None, :, None])
            .reshape(group_rows, local_width)
            .astype(jnp.bfloat16)
        )
        forward_attn_rows = lax.all_to_all(
            scaled, "sp", split_axis=0, concat_axis=1, tiled=True
        ).astype(jnp.float32)
        forward_post_norm = layer_norm(
            forward_attn_rows,
            forward_wide_attn_gain.astype(jnp.float32),
            forward_wide_attn_bias.astype(jnp.float32),
        ).astype(jnp.bfloat16)
        forward_hidden = (
            forward_tok_rows
            + jnp.dot(forward_post_norm, forward_wide_out, preferred_element_type=jnp.float32)
            + forward_wide_out_bias.astype(jnp.float32)
        )
        forward_ffn_in = layer_norm(
            forward_hidden,
            forward_wide_ffn_gain.astype(jnp.float32),
            forward_wide_ffn_bias.astype(jnp.float32),
        ).astype(jnp.bfloat16)
        forward_ffn_inner = jnp.dot(
            forward_ffn_in, forward_wide_fc1, preferred_element_type=jnp.float32
        ) + forward_wide_fc1_bias.astype(jnp.float32)
        forward_active = layer_norm(
            jax.nn.gelu(forward_ffn_inner),
            forward_wide_mid_gain.astype(jnp.float32),
            forward_wide_mid_bias.astype(jnp.float32),
        ).astype(jnp.bfloat16)
        output = (
            forward_hidden
            + jnp.dot(forward_active, forward_wide_fc2, preferred_element_type=jnp.float32)
            + forward_wide_fc2_bias.astype(jnp.float32)
        )
        forward_kept_values = (
            forward_normed,
            forward_heads_in,
            forward_head_mixed,
            attend_log_total,
            forward_attn_rows,
            forward_post_norm,
            forward_hidden,
            forward_ffn_in,
            forward_ffn_inner,
            forward_active,
        )
        output, kept_values = (output, forward_kept_values)
        backward_set = collect()
        (
            wide_in_gain,
            wide_in_bias,
            wide_qkv,
            wide_q_bias,
            wide_v_bias,
            wide_attn_gain,
            wide_attn_bias,
            wide_out,
            wide_out_bias,
            wide_ffn_gain,
            wide_ffn_bias,
            wide_fc1,
            wide_fc1_bias,
            wide_mid_gain,
            wide_mid_bias,
            wide_fc2,
            wide_fc2_bias,
        ) = backward_set
        (
            normed,
            backward_heads_in,
            backward_head_mixed,
            backward_log_total,
            attn_rows,
            post_norm,
            hidden,
            ffn_in,
            ffn_inner,
            active,
        ) = kept_values
        tok_rows = tokens[micro_index].astype(jnp.float32)
        backward_lengths = doc_lengths[0, micro_index]
        grad_out = out_cotangent[micro_index].astype(jnp.float32)
        fc2_bias_grad = jnp.sum(grad_out, axis=0)
        grad_low = grad_out.astype(jnp.bfloat16)
        fc2_grad = jnp.einsum("ti,tj->ij", active, grad_low, preferred_element_type=jnp.float32)
        grad_active = jnp.einsum(
            "tj,ij->ti", grad_low, wide_fc2, preferred_element_type=jnp.float32
        )
        gelu_out, gelu_back = jax.vjp(jax.nn.gelu, ffn_inner)
        _, mid_back = jax.vjp(
            layer_norm,
            gelu_out,
            wide_mid_gain.astype(jnp.float32),
            wide_mid_bias.astype(jnp.float32),
        )
        grad_gelu, mid_gain_grad, mid_bias_grad = mid_back(grad_active)
        (grad_inner,) = gelu_back(grad_gelu)
        inner_low = grad_inner.astype(jnp.bfloat16)
        fc1_bias_grad = jnp.sum(inner_low.astype(jnp.float32), axis=0)
        fc1_grad = jnp.einsum("ti,tj->ij", ffn_in, inner_low, preferred_element_type=jnp.float32)
        grad_ffn = jnp.einsum("tj,ij->ti", inner_low, wide_fc1, preferred_element_type=jnp.float32)
        _, ffn_back = jax.vjp(
            layer_norm, hidden, wide_ffn_gain.astype(jnp.float32), wide_ffn_bias.astype(jnp.float32)
        )
        grad_hid, ffn_gain_grad, ffn_bias_grad = ffn_back(grad_ffn)
        grad_hidden = grad_out + grad_hid
        out_bias_grad = jnp.sum(grad_hidden, axis=0)
        hidden_low = grad_hidden.astype(jnp.bfloat16)
        out_grad = jnp.einsum(
            "ti,tj->ij", post_norm, hidden_low, preferred_element_type=jnp.float32
        )
        grad_post = jnp.einsum(
            "tj,ij->ti", hidden_low, wide_out, preferred_element_type=jnp.float32
        )
        _, attn_back = jax.vjp(
            layer_norm,
            attn_rows,
            wide_attn_gain.astype(jnp.float32),
            wide_attn_bias.astype(jnp.float32),
        )
        grad_attn, attn_gain_grad, attn_bias_grad = attn_back(grad_post)
        grad_heads = lax.all_to_all(
            grad_attn.astype(jnp.bfloat16), "sp", split_axis=1, concat_axis=0, tiled=True
        )
        grad_scaled = grad_heads.astype(jnp.float32).reshape(group_rows, head_local, head_dim)
        scale_grad = jnp.sum(grad_scaled * backward_head_mixed, axis=(0, 2))
        backward_grad_mixed = (grad_scaled * head_gains[None, :, None]).astype(jnp.bfloat16)
        grad_qkv = attend_back(
            backward_heads_in, backward_lengths, backward_log_total, backward_grad_mixed
        )
        returned = lax.all_to_all(grad_qkv, "sp", split_axis=0, concat_axis=2, tiled=True).reshape(
            tok_count, 3 * model_width
        )
        column_sums = jnp.sum(returned.astype(jnp.float32), axis=0)
        q_bias_grad = column_sums[:model_width]
        v_bias_grad = column_sums[2 * model_width :]
        qkv_grad = jnp.einsum("ti,tj->ij", normed, returned, preferred_element_type=jnp.float32)
        grad_normed = jnp.einsum(
            "tj,ij->ti", returned, wide_qkv, preferred_element_type=jnp.float32
        )
        _, in_back = jax.vjp(
            layer_norm, tok_rows, wide_in_gain.astype(jnp.float32), wide_in_bias.astype(jnp.float32)
        )
        grad_rows, in_gain_grad, in_bias_grad = in_back(grad_normed)
        input_grad = grad_hidden + grad_rows
        grad_set = (
            in_gain_grad,
            in_bias_grad,
            qkv_grad,
            q_bias_grad,
            v_bias_grad,
            attn_gain_grad,
            attn_bias_grad,
            out_grad,
            out_bias_grad,
            ffn_gain_grad,
            ffn_bias_grad,
            fc1_grad,
            fc1_bias_grad,
            mid_gain_grad,
            mid_bias_grad,
            fc2_grad,
            fc2_bias_grad,
        )
        input_grad, grad_set, scale_grad = (input_grad, grad_set, scale_grad)
        grad_set = reduce_grads(grad_set)
        total_grads = (
            grad_set if total_grads is None else jax.tree.map(jnp.add, total_grads, grad_set)
        )
        scale_total = scale_total + scale_grad
        outputs.append(output)
        input_grads.append(input_grad)
    scale_sum = lax.psum(scale_total, "dp")
    layer_out = jnp.stack(outputs).astype(jnp.bfloat16)
    input_grad = jnp.stack(input_grads)
    return (
        layer_out,
        input_grad,
        total_grads[0],
        total_grads[1],
        total_grads[2],
        total_grads[3],
        total_grads[4],
        scale_sum,
        total_grads[5],
        total_grads[6],
        total_grads[7],
        total_grads[8],
        total_grads[9],
        total_grads[10],
        total_grads[11],
        total_grads[12],
        total_grads[13],
        total_grads[14],
        total_grads[15],
        total_grads[16],
    )


def fits(args):
    dp, sp = lax.axis_size("dp"), lax.axis_size("sp")
    tokens, lengths, in_gain, fc1_bias = args[0], args[1], args[3], args[16]
    return (
        sp == 2
        and tokens.shape[0] == 2
        and dp % 4 == 0
        and dp >= 8
        and 2 * tokens.shape[1] == LONGEST
        and lengths.shape[2] * BLOCK == LONGEST
        and 128 % in_gain.shape[0] == 0
        and fc1_bias.shape[0] == 128
        and tokens.shape[2] == 128 * args[8].shape[0]
    )


def body(*args):
    return fast_shards(*args) if fits(args) else shards(*args)


def solution(mesh):
    return jax.shard_map(
        body,
        mesh=mesh,
        in_specs=(
            P(None, ("dp", "sp"), None),
            P("dp", None, None),
            P(None, ("dp", "sp"), None),
            P(("dp", "sp")),
            P(("dp", "sp")),
            P(("dp", "sp"), None),
            P(("dp", "sp")),
            P(("dp", "sp")),
            P("sp"),
            P(("dp", "sp")),
            P(("dp", "sp")),
            P(("dp", "sp"), None),
            P(("dp", "sp")),
            P(("dp", "sp")),
            P(("dp", "sp")),
            P(("dp", "sp"), None),
            P(("dp", "sp")),
            P(("dp", "sp")),
            P(("dp", "sp")),
            P(("dp", "sp"), None),
            P(("dp", "sp")),
        ),
        out_specs=(
            P(None, ("dp", "sp"), None),
            P(None, ("dp", "sp"), None),
            P(("dp", "sp")),
            P(("dp", "sp")),
            P(("dp", "sp"), None),
            P(("dp", "sp")),
            P(("dp", "sp")),
            P("sp"),
            P(("dp", "sp")),
            P(("dp", "sp")),
            P(("dp", "sp"), None),
            P(("dp", "sp")),
            P(("dp", "sp")),
            P(("dp", "sp")),
            P(("dp", "sp"), None),
            P(("dp", "sp")),
            P(("dp", "sp")),
            P(("dp", "sp")),
            P(("dp", "sp"), None),
            P(("dp", "sp")),
        ),
        check_vma=False,
    )
```

```python
import functools
import math

import jax
import jax.numpy as jnp
from jax import lax
from jax.experimental import pallas as pl
from jax.experimental.pallas import tpu as pltpu
from jax.sharding import PartitionSpec as P

EPS = 1e-05
BLOCK = 512
LOG2E = math.log2(math.e)
NEG = -1e30
F32 = jnp.float32
BF16 = jnp.bfloat16
VMEM_CAP = 60 * 1024 * 1024
NT = (((1,), (1,)), ((), ()))
NN = (((1,), (0,)), ((), ()))
FWD_STEPS = ((0, 0, 10, 11), (9, 12, 25, 26), (20, 21, 30, 31), (24, 25, 32, 32))
BWD_STEPS = ((1, 2, 3, 4, 5), (9, 15, 20, 26, 28), (14, 19, 24, 29, 30), (18, 23, 28, 32, 32))


def mm(a, b, dims=NN):
    return lax.dot_general(a, b, dims, preferred_element_type=F32)


def same_sequence(lengths, y):
    ends = []
    for k in range(lengths.shape[2]):
        ends.append(lengths[0, y, k] + (ends[-1] if ends else 0))

    def same(i, kb):
        between = [((e > kb * BLOCK) & (e <= i * BLOCK)).astype(jnp.int32) for e in ends]
        return sum(between) == 0

    return same


class Place:
    def __init__(self, depth):
        d = lax.axis_index("dp")
        self.depth = depth
        self.y = lax.axis_index("sp")
        self.c = d % 2
        self.x = (d // 2) % 2
        self.z = d // 4
        self.next_y = self.device(self.z, self.x, self.c, 1 - self.y)
        self.next_x = self.device(self.z, 1 - self.x, self.c, self.y)
        self.twin = self.device(self.z, self.x, 1 - self.c, self.y)

    def device(self, z, x, c, y):
        return ((z * 2 + x) * 2 + c, y)

    def along(self, step):
        return (self.z + step) % self.depth

    def column(self, step):
        return self.device(self.along(step), self.x, self.c, self.y)

    def greet(self):
        barrier = pltpu.get_barrier_semaphore()
        peers = [self.column(s) for s in range(1, self.depth)] + [self.next_x, self.next_y, self.twin]
        for peer in peers:
            pl.semaphore_signal(barrier, inc=1, device_id=peer, device_id_type=pl.DeviceIdType.MESH)
        pl.semaphore_wait(barrier, len(peers))


def remote(src, dst, send, recv, peer):
    return pltpu.make_async_remote_copy(
        src_ref=src, dst_ref=dst, send_sem=send, recv_sem=recv, device_id=peer, device_id_type=pl.DeviceIdType.MESH
    )


class Gather:
    def __init__(self, me, shard, stage, whole, at, count, local, send, recv, early=False):
        self.me, self.whole, self.early = me, whole, early
        if shard is not None:
            self.shard, self.stage = shard.at[pl.ds(at, count)], stage.at[pl.ds(at, count)]
        self.rows = pl.ds(at, count)
        self.local, self.send, self.recv = local, send, recv

    def own(self, z):
        me = self.me
        return self.whole.at[z, me.x, me.c, me.y, self.rows]

    def load(self):
        return pltpu.make_async_copy(self.shard, self.stage, self.local)

    def keep(self):
        return pltpu.make_async_copy(self.stage, self.own(self.me.z), self.local)

    def depth_hop(self, s, landed):
        me = self.me
        z = me.along(me.depth - s) if landed else me.z
        return remote(self.stage, self.own(z), self.send.at[6 + s], self.recv.at[6 + s], me.column(s))

    def hop(self, x, y, n, peer, c=None):
        group = self.whole.at[:, x, self.me.c if c is None else c, y, self.rows]
        return remote(group, group, self.send.at[n], self.recv.at[n], peer)

    def path(self, n, c=None):
        me = self.me
        x, y = me.x, me.y
        gx = 1 - x if n in (5, 6) else x
        gy = 1 - y if n in (2, 4, 6) else y
        peer = me.next_y if n == 0 else me.next_x if n < 3 else me.twin
        return self.hop(gx, gy, n, peer, c)

    def ready(self):
        self.load().start()

    def begin(self):
        self.load().wait()
        self.keep().start()
        for s in range(1, self.me.depth):
            self.depth_hop(s, False).start()

    def landed(self):
        self.keep().wait()
        for s in range(1, self.me.depth):
            self.depth_hop(s, True).wait()

    def launch(self):
        for n in (0, 3) if self.early else (0, 1, 3):
            self.path(n).start()

    def x_begin(self):
        self.path(1).start()

    def x_end(self):
        self.path(1).wait_send()
        self.hop(1 - self.me.x, self.me.y, 1, self.me.next_x).wait_recv()

    def spread(self):
        self.landed()
        self.launch()

    def from_y(self):
        me = self.me
        self.hop(me.x, 1 - me.y, 0, me.next_y).wait_recv()
        self.path(2).start()
        self.path(4).start()

    def from_x(self):
        me = self.me
        if not self.early:
            self.hop(1 - me.x, me.y, 1, me.next_x).wait_recv()
        self.path(5).start()

    def from_corner(self):
        me = self.me
        self.hop(1 - me.x, 1 - me.y, 2, me.next_x).wait_recv()
        self.path(6).start()

    def end(self):
        for n in range(7):
            if n != 1 or not self.early:
                self.path(n).wait_send()
        for n in range(3, 7):
            self.path(n, 1 - self.me.c).wait_recv()


class Gather2:
    def __init__(self, me, shard, stage, whole, at, count, local, send, recv):
        self.me, self.whole = me, whole
        self.rows = pl.ds(at, count)
        if shard is not None:
            self.shard, self.stage = shard.at[self.rows], stage.at[self.rows]
        self.local, self.send, self.recv = local, send, recv

    def one(self, z, y):
        me = self.me
        return self.whole.at[z, me.x, me.c, y, self.rows]

    def load(self):
        return pltpu.make_async_copy(self.shard, self.stage, self.local)

    def keep(self):
        return pltpu.make_async_copy(self.stage, self.one(self.me.z, self.me.y), self.local)

    def y_hop(self, y):
        me = self.me
        return remote(self.stage, self.one(me.z, y), self.send.at[0], self.recv.at[0], me.next_y)

    def z_hop(self, s, n, landed):
        me = self.me
        z = me.along(me.depth - s) if landed else me.z
        y = 1 - me.y if n else me.y
        src = self.one(me.z, y) if n else self.stage
        k = 1 + n * (me.depth - 1) + s
        return remote(src, self.one(z, y), self.send.at[k], self.recv.at[k], me.column(s))

    def plane(self, x, n, peer, c):
        k = 2 * self.me.depth + n
        plane = self.whole.at[:, x, c, :, self.rows]
        return remote(plane, plane, self.send.at[k], self.recv.at[k], peer)

    def x_hop(self, landed):
        me = self.me
        return self.plane(1 - me.x if landed else me.x, 0, me.next_x, me.c)

    def twin_hop(self, n, landed):
        me = self.me
        return self.plane(1 - me.x if n else me.x, 1 + n, me.twin, 1 - me.c if landed else me.c)

    def ready(self):
        self.load().start()

    def begin(self):
        self.load().wait()
        self.keep().start()
        self.y_hop(self.me.y).start()
        for s in range(1, self.me.depth):
            self.z_hop(s, 0, False).start()

    def pass_z(self):
        self.y_hop(self.me.y).wait_send()
        self.y_hop(1 - self.me.y).wait_recv()
        for s in range(1, self.me.depth):
            self.z_hop(s, 1, False).start()

    def landed(self):
        self.keep().wait()
        for n in range(2):
            for s in range(1, self.me.depth):
                self.z_hop(s, n, True).wait()

    def pass_x(self):
        self.landed()
        self.x_hop(False).start()

    def pass_twin(self):
        self.twin_hop(0, False).start()

    def arrived(self):
        self.x_hop(False).wait_send()
        self.x_hop(True).wait_recv()

    def pass_twin_far(self):
        self.twin_hop(1, False).start()

    def end(self):
        for n in range(2):
            self.twin_hop(n, False).wait_send()
            self.twin_hop(n, True).wait_recv()


class Swap:
    def __init__(self, me, sent, landing, kept, stage, place, local, send, recv):
        self.out = remote(sent, landing(me.y), send, recv, me.next_y)
        self.into = remote(sent, landing(1 - me.y), send, recv, me.next_y)
        self.load = pltpu.make_async_copy(kept, stage, local)
        self.keep = pltpu.make_async_copy(stage, place, local)

    def ready(self):
        self.load.start()

    def begin(self):
        self.out.start()
        self.load.wait()
        self.keep.start()

    def end(self):
        self.out.wait_send()
        self.into.wait_recv()
        self.keep.wait()


def add_group(own, x, y, taken):
    def body(s, _):
        own[s, x, y] = (own[s, x, y].astype(F32) + taken(s).astype(F32)).astype(own.dtype)
        return 0

    lax.fori_loop(0, own.shape[0], body, 0)


class Scatter:
    def __init__(self, me, part, at, count, own, got0, got1, got3, local, send, recv, total):
        self.me, self.part, self.rows = me, part, pl.ds(at, count)
        self.own, self.got0, self.got1, self.got3 = own, got0, got1, got3
        self.local, self.send, self.recv, self.total = local, send, recv, total

    def mine(self):
        return pltpu.make_async_copy(self.part.at[:, :, self.me.c, :, self.rows], self.own, self.local)

    def halves(self):
        return remote(
            self.part.at[:, :, 1 - self.me.c, :, self.rows], self.got0, self.send.at[0], self.recv.at[0], self.me.twin
        )

    def to_x(self, n):
        me = self.me
        y = me.y if n == 0 else 1 - me.y
        return remote(self.own.at[:, 1 - me.x, y], self.got1.at[n], self.send.at[1 + n], self.recv.at[1 + n], me.next_x)

    def to_y(self):
        me = self.me
        return remote(self.own.at[:, me.x, 1 - me.y], self.got1.at[2], self.send.at[3], self.recv.at[3], me.next_y)

    def to_z(self, s):
        me = self.me
        return remote(
            self.own.at[me.along(s), me.x, me.y], self.got3.at[s - 1], self.send.at[3 + s], self.recv.at[3 + s],
            me.column(s),
        )

    def begin(self):
        self.mine().start()
        self.halves().start()

    def across(self):
        me, own, got = self.me, self.own, self.got0
        self.mine().wait()
        self.halves().wait()
        for n, x, y in ((1, 1 - me.x, 1 - me.y), (0, 1 - me.x, me.y)):
            add_group(own, x, y, lambda s: got[s, x, y])
            self.to_x(n).start()
        for x, y in ((me.x, 1 - me.y), (me.x, me.y)):
            add_group(own, x, y, lambda s: got[s, x, y])

    def along_x(self):
        me, own, got = self.me, self.own, self.got1
        self.to_x(1).wait_recv()
        add_group(own, me.x, 1 - me.y, lambda s: got[1, s])
        self.to_y().start()
        self.to_x(0).wait_recv()
        add_group(own, me.x, me.y, lambda s: got[0, s])

    def along_y(self):
        me, own, got = self.me, self.own, self.got1
        self.to_y().wait_recv()
        add_group(own, me.x, me.y, lambda s: got[2, s])
        for s in range(1, me.depth):
            self.to_z(s).start()

    def end(self):
        me = self.me
        total = self.own[me.z, me.x, me.y].astype(F32)
        for s in range(1, me.depth):
            self.to_z(s).wait_recv()
            total = total + self.got3[s - 1].astype(F32)
        self.total[self.rows] = total
        self.to_x(0).wait_send()
        self.to_x(1).wait_send()
        self.to_y().wait_send()
        for s in range(1, me.depth):
            self.to_z(s).wait_send()


def scatter_scratch(pieces, depth):
    out = []
    for rows, cols, dtype in pieces:
        for lead in ((depth, 2, 2), (depth, 2, 2), (3, depth), (depth - 1,)):
            out.append(pltpu.VMEM(lead + (rows, cols), dtype))
    return out


def perform(step, plan):
    for due in sorted(plan):

        @pl.when(step == due)
        def _(actions=plan[due]):
            for action in actions:
                action()


def due(plan, step, action):
    plan.setdefault(step, []).append(action)


def head_pair_masks():
    lanes = lax.broadcasted_iota(jnp.int32, (1, 128), 1)
    return (lanes < 64, lanes >= 64)


def attend_fwd_kernel(depth, pieces, *refs):
    lengths, hs, q_ref, k_ref, v_ref = refs[:5]
    shard = refs[6]
    o_ref, mixed_ref, lse_ref = refs[7:10]
    wholes = refs[10:12]
    vt, local, send, recv, shard_stage = refs[12:]
    pair = pl.program_id(0)
    me = Place(depth)
    same = same_sequence(lengths, me.y)
    gathers = [
        Gather(
            me, shard if a else None, shard_stage, wholes[a], at, count, local.at[n], send.at[n], recv.at[n], n == 0
        )
        for n, (a, at, count) in enumerate(pieces)
    ]
    plan = {}
    due(plan, 0, me.greet)
    for n, g in enumerate(gathers):
        if pieces[n][0]:
            due(plan, 0, g.ready)
    for n, g in enumerate(gathers):
        due(plan, 0, g.begin if pieces[n][0] else g.launch)
        if pieces[n][0]:
            due(plan, FWD_STEPS[0][n], g.spread)
        due(plan, FWD_STEPS[1][n], g.from_y)
        due(plan, FWD_STEPS[2][n], g.from_x)
        due(plan, FWD_STEPS[3][n], g.from_corner)
        due(plan, 32, g.end)
    last = plan.pop(32)
    rows = q_ref.shape[0]
    blocks = rows // BLOCK
    factor = LOG2E / 8.0
    masks = head_pair_masks()
    gains = jnp.where(masks[0], hs[0, 2 * pair], hs[0, 2 * pair + 1])
    for j in range(blocks):
        vtr = v_ref[j * BLOCK : (j + 1) * BLOCK, :].astype(F32).T.astype(BF16)
        for h in range(2):
            vt[j, h, 0:64, :] = vtr[h * 64 : (h + 1) * 64]
            vt[j, h, 64:80, :] = jnp.ones((16, BLOCK), BF16)
    key_at = lax.broadcasted_iota(jnp.int32, (BLOCK, BLOCK), 0)
    query_at = lax.broadcasted_iota(jnp.int32, (BLOCK, BLOCK), 1)

    def one_query(i):
        perform(pair, {k // blocks: plan[k] for k in plan if k % blocks == i})
        q = q_ref[pl.ds(i * BLOCK, BLOCK), :]
        qh = [jnp.where(m, q, jnp.zeros_like(q)) for m in masks]

        def step(kb, carry, diag):
            k = k_ref[pl.ds(kb * BLOCK, BLOCK), :]
            out = []
            for h in range(2):
                s = mm(k, qh[h], NT)
                if diag:
                    s = jnp.where(key_at <= query_at, s, NEG)
                    m = jnp.max(s, axis=0, keepdims=True)
                    p = jnp.exp2(s * factor - m * factor).astype(BF16)
                    out.append((m, mm(vt[kb, h], p)))
                else:
                    bias = jnp.where(same(i, kb), 0.0, NEG)
                    m_old, acc = carry[h]
                    m = jnp.maximum(m_old, jnp.max(s, axis=0, keepdims=True) + bias)
                    p = jnp.exp2(s * factor - (m - bias) * factor).astype(BF16)
                    alpha = jnp.exp2((m_old - m) * factor)
                    out.append((m, acc * alpha + mm(vt[kb, h], p)))
            return tuple(out)

        carry = step(i, None, True)
        for kb in range(i):
            carry = step(kb, carry, False)
        outs = []
        for h in range(2):
            m, acc = carry[h]
            total = acc[64:65]
            outs.append(acc[:64] / total)
            lse_ref[0, h, pl.ds(i, 1), :] = m * factor + jnp.log2(total)
        both = jnp.concatenate(outs, axis=0).T
        mixed_ref[pl.ds(i * BLOCK, BLOCK), :] = both
        o_ref[pl.ds(i * BLOCK, BLOCK), :] = (both * gains).astype(BF16)

    for i in range(blocks):
        one_query(i)
    perform(pair, {pl.num_programs(0) - 1: last})


def attend_fwd(qkv, lengths, hs, begun, shard, depth, collective_id):
    rows, width3 = qkv.shape
    width = width3 // 3
    pairs = width // 128
    blocks = rows // BLOCK
    spec = lambda part: pl.BlockSpec((rows, 128), lambda p, part=part: (0, part * pairs + p))
    smem = pl.BlockSpec(memory_space=pltpu.SMEM)
    anywhere = pl.BlockSpec(memory_space=pl.ANY)
    pieces = []
    for a, count in enumerate((begun.shape[4], shard.shape[0])):
        part = count // 2
        pieces += [(a, 0, part), (a, part, part)]
    count = len(pieces)
    out = pl.pallas_call(
        functools.partial(attend_fwd_kernel, depth, pieces),
        grid=(pairs,),
        in_specs=[smem, smem, spec(0), spec(1), spec(2)] + [anywhere] * 2,
        out_specs=[
            pl.BlockSpec((rows, 128), lambda p: (0, p)),
            pl.BlockSpec((rows, 128), lambda p: (0, p)),
            pl.BlockSpec((1, 2, blocks, BLOCK), lambda p: (p, 0, 0, 0)),
        ]
        + [anywhere] * 2,
        out_shape=[
            jax.ShapeDtypeStruct((rows, width), BF16),
            jax.ShapeDtypeStruct((rows, width), F32),
            jax.ShapeDtypeStruct((pairs, 2, blocks, BLOCK), F32),
            jax.ShapeDtypeStruct(begun.shape, begun.dtype),
            jax.ShapeDtypeStruct((depth, 2, 2, 2) + shard.shape, shard.dtype),
        ],
        input_output_aliases={5: 3},
        scratch_shapes=[
            pltpu.VMEM((blocks, 2, 80, BLOCK), BF16),
            pltpu.SemaphoreType.DMA((count,)),
            pltpu.SemaphoreType.DMA((count, 6 + depth)),
            pltpu.SemaphoreType.DMA((count, 6 + depth)),
            pltpu.VMEM(shard.shape, shard.dtype),
        ],
        compiler_params=pltpu.CompilerParams(
            vmem_limit_bytes=VMEM_CAP, collective_id=collective_id, has_side_effects=True
        ),
        name="attend_fwd",
    )(lengths, hs, qkv, qkv, qkv, begun, shard)
    return out[0], out[1], out[2], out[3], out[4]


def attend_bwd_kernel(depth, pieces, *refs):
    lengths, hs, q_ref, k_ref, v_ref, o_ref, g_ref, lse_ref = refs[:8]
    parts = refs[8:11]
    layer = refs[11]
    dq_ref, dk_ref, dv_ref, delta_ref = refs[12:16]
    sums = refs[16:19]
    layer_out = refs[19]
    kt, dk_acc, dv_acc, local, send, recv, layer_stage = refs[20:27]
    scratch = refs[27:]
    pair = pl.program_id(0)
    me = Place(depth)
    same = same_sequence(lengths, me.y)
    scatters = [
        Scatter(
            me, parts[a], at, count, *scratch[4 * n : 4 * n + 4], local.at[n], send.at[n], recv.at[n], sums[a]
        )
        for n, (a, at, count) in enumerate(pieces)
    ]
    n = len(pieces)
    half = layer_out.shape[1]
    swap = Swap(
        me, layer.at[pl.ds((1 - me.y) * half, half)], lambda y: layer_out.at[y],
        layer.at[pl.ds(me.y * half, half)], layer_stage, layer_out.at[me.y], local.at[n], send.at[n, 0], recv.at[n, 0],
    )
    plan = {}
    due(plan, 0, swap.ready)
    due(plan, 0, me.greet)
    for s in scatters:
        due(plan, 0, s.begin)
    for n, s in enumerate(scatters):
        due(plan, BWD_STEPS[0][n], s.across)
        due(plan, BWD_STEPS[1][n], s.along_x)
        due(plan, BWD_STEPS[2][n], s.along_y)
        due(plan, BWD_STEPS[3][n], s.end)
    due(plan, 0, swap.begin)
    due(plan, 32, swap.end)
    last = plan.pop(32)
    rows = q_ref.shape[0]
    blocks = rows // BLOCK
    factor = LOG2E / 8.0
    masks = head_pair_masks()
    for j in range(blocks):
        kt[j] = k_ref[j * BLOCK : (j + 1) * BLOCK, :].astype(F32).T.astype(BF16)
    key_at = lax.broadcasted_iota(jnp.int32, (BLOCK, BLOCK), 0)
    query_at = lax.broadcasted_iota(jnp.int32, (BLOCK, BLOCK), 1)
    gains = jnp.where(masks[0], hs[0, 2 * pair], hs[0, 2 * pair + 1])
    picks = jnp.concatenate([m.astype(F32) for m in masks] + [jnp.zeros((6, 128), F32)], axis=0).astype(BF16)

    def one_query(i):
        perform(pair, {k // blocks: plan[k] for k in plan if k % blocks == i})
        at = pl.ds(i * BLOCK, BLOCK)
        q = q_ref[at, :]
        g = (g_ref[at, :].astype(F32) * gains).astype(BF16)
        prod = g.astype(F32) * o_ref[at, :]
        hi = prod.astype(BF16)
        lo = (prod - hi.astype(F32)).astype(BF16)
        deltas = mm(picks, hi, NT) + mm(picks, lo, NT)
        qh = [jnp.where(m, q, jnp.zeros_like(q)) for m in masks]
        gh = [jnp.where(m, g, jnp.zeros_like(g)) for m in masks]
        delta = [deltas[h : h + 1] for h in range(2)]
        lse = [lse_ref[0, h, pl.ds(i, 1), :] for h in range(2)]
        for h in range(2):
            delta_ref[0, h, pl.ds(i, 1), :] = delta[h]

        def step(kb, carry, diag):
            ks = pl.ds(kb * BLOCK, BLOCK)
            k = k_ref[ks, :]
            v = v_ref[ks, :]
            out = []
            dk_part = None
            dv_part = None
            for h in range(2):
                s = mm(k, qh[h], NT)
                dp = mm(v, gh[h], NT)
                if diag:
                    p = jnp.exp2(s * factor - lse[h])
                    p = jnp.where(key_at <= query_at, p, 0.0)
                else:
                    bias = jnp.where(same(i, kb), 0.0, -NEG)
                    p = jnp.exp2(s * factor - (lse[h] + bias))
                ds = (p * (dp - delta[h])).astype(BF16)
                dvh = mm(p.astype(BF16), gh[h])
                dkh = mm(ds, qh[h])
                dk_part = dkh if dk_part is None else dk_part + dkh
                dv_part = dvh if dv_part is None else dv_part + dvh
                dqh = mm(kt[kb, h * 64 : (h + 1) * 64, :], ds)
                out.append(dqh if diag else carry[h] + dqh)
            if diag:
                dk_acc[ks, :] = dk_part
                dv_acc[ks, :] = dv_part
            else:
                dk_acc[ks, :] += dk_part
                dv_acc[ks, :] += dv_part
            return tuple(out)

        carry = step(i, None, True)
        for kb in range(i):
            carry = step(kb, carry, False)
        both = jnp.concatenate(carry, axis=0) * 0.125
        dq_ref[at, :] = both.T.astype(BF16)

    for i in range(blocks):
        one_query(i)
    dk_ref[...] = (dk_acc[...] * 0.125).astype(BF16)
    dv_ref[...] = dv_acc[...].astype(BF16)
    perform(pair, {pl.num_programs(0) - 1: last})


def shard_view(part, depth):
    return part.reshape((depth, 2, 2, 2, part.shape[0] // (depth * 8)) + part.shape[1:])


def attend_bwd(qkv, mixed, d_scaled, lse, lengths, hs, parts, layer, depth, collective_id):
    rows, width3 = qkv.shape
    width = width3 // 3
    pairs = width // 128
    blocks = rows // BLOCK
    spec = lambda part: pl.BlockSpec((rows, 128), lambda p, part=part: (0, part * pairs + p))
    col = pl.BlockSpec((rows, 128), lambda p: (0, p))
    stat = pl.BlockSpec((1, 2, blocks, BLOCK), lambda p: (p, 0, 0, 0))
    smem = pl.BlockSpec(memory_space=pltpu.SMEM)
    anywhere = pl.BlockSpec(memory_space=pl.ANY)
    parts = [shard_view(p, depth) for p in parts]
    pieces = []
    for a in (0, 1):
        part = parts[a].shape[4] // 2
        pieces += [(a, 0, part), (a, part, part)]
    pieces.append((2, 0, parts[2].shape[4]))
    count = len(pieces) + 1
    out = pl.pallas_call(
        functools.partial(attend_bwd_kernel, depth, pieces),
        grid=(pairs,),
        in_specs=[smem, smem, spec(0), spec(1), spec(2), col, col, stat] + [anywhere] * 4,
        out_specs=[col, col, col, stat]
        + [pl.BlockSpec(p.shape[4:], lambda p: (0, 0)) for p in parts]
        + [anywhere],
        out_shape=[jax.ShapeDtypeStruct((rows, width), BF16)] * 3
        + [jax.ShapeDtypeStruct((pairs, 2, blocks, BLOCK), F32)]
        + [jax.ShapeDtypeStruct(p.shape[4:], F32) for p in parts]
        + [jax.ShapeDtypeStruct((2, rows // 2, width), BF16)],
        scratch_shapes=[
            pltpu.VMEM((blocks, 128, BLOCK), BF16),
            pltpu.VMEM((rows, 128), F32),
            pltpu.VMEM((rows, 128), F32),
            pltpu.SemaphoreType.DMA((count,)),
            pltpu.SemaphoreType.DMA((count, 3 + depth)),
            pltpu.SemaphoreType.DMA((count, 3 + depth)),
            pltpu.VMEM((rows // 2, width), BF16),
        ]
        + scatter_scratch([(count, parts[a].shape[5], parts[a].dtype) for a, _, count in pieces], depth),
        compiler_params=pltpu.CompilerParams(
            vmem_limit_bytes=VMEM_CAP, collective_id=collective_id, has_side_effects=True
        ),
        name="attend_bwd",
    )(lengths, hs, qkv, qkv, qkv, mixed, d_scaled, lse, *parts, layer)
    return out[:4], out[4:7], out[7]


def row_norm(values):
    center = values - jnp.mean(values, axis=-1, keepdims=True)
    spread = jnp.mean(center * center, axis=-1, keepdims=True)
    rstd = lax.rsqrt(spread + EPS)
    return center * rstd, rstd


def row_norm_back(grad, hat, rstd):
    first = jnp.mean(grad, axis=-1, keepdims=True)
    second = jnp.mean(grad * hat, axis=-1, keepdims=True)
    return rstd * (grad - first - hat * second)


def fold_rows(values):
    return jnp.sum(values.reshape(values.shape[0] // 8, 8, values.shape[1]), axis=0)


def resident(shape):
    return pl.BlockSpec(shape, lambda i: (0,) * len(shape), pipeline_mode=pl.Buffered(1))


GELU_A = math.sqrt(2.0 / math.pi)
GELU_B = 0.044715
CHUNK = 512


def middle_kernel(
    depth, sc_ref, x_ref, cot, wout, w1, w2, nar, wide,
    lay_ref, post_ref, fin_ref, act_ref, din_ref, dhid_ref, dlow_ref, dsc_ref, gn_ref, gw_ref, dy_out,
    n_s, gp_s, dn_s, dy_s, local, go, come,
):
    me = Place(depth)
    step = pl.program_id(0)
    half_tiles = dy_s.shape[1] // x_ref.shape[0]
    load = pltpu.make_async_copy(cot.at[me.y], dy_s.at[0], local.at[0])
    trade = remote(cot.at[1 - me.y], dy_s.at[1], go, come, me.next_y)
    puts = [
        pltpu.make_async_copy(dy_s.at[n], dy_out.at[1 - me.y if n else me.y], local.at[1 + n]) for n in range(2)
    ]

    @pl.when(step == 0)
    def _():
        load.start()
        me.greet()
        trade.start()
        load.wait()
        puts[0].start()

    @pl.when(step == half_tiles)
    def _():
        trade.wait()
        puts[1].start()

    @pl.when(step == pl.num_programs(0) - 1)
    def _():
        for put in puts:
            put.wait()

    @pl.when(step == 0)
    def _():
        gn_ref[...] = jnp.zeros_like(gn_ref)
        gw_ref[...] = jnp.zeros_like(gw_ref)

    tile, width = x_ref.shape
    ff = w1.shape[1]
    chunks = ff // CHUNK
    ahat, arstd = row_norm(sc_ref[...].astype(F32))
    post = (ahat * nar[4:5] + nar[5:6]).astype(BF16)
    post_ref[...] = post
    hidden = x_ref[...].astype(F32) + mm(post, wout[...]) + nar[6:7]
    hhat, hrstd = row_norm(hidden)
    fin = (hhat * nar[7:8] + nar[8:9]).astype(BF16)
    fin_ref[...] = fin

    def lanes(values):
        return jnp.sum(values.reshape(tile, CHUNK // 128, 128), axis=1)

    def inner(j, total):
        at = pl.ds(pl.multiple_of(j * CHUNK, CHUNK), CHUNK)
        u = mm(fin, w1[:, at]) + wide[0:1, at]
        u2 = u * u
        t = jnp.tanh(u * (GELU_A + GELU_A * GELU_B * u2))
        half = 0.5 * (1.0 + t)
        n = u * half
        gp_s[:, at] = (half + n * (1.0 - t) * (GELU_A + 3.0 * GELU_A * GELU_B * u2)).astype(BF16)
        n_s[:, at] = n
        for q in range(CHUNK // 128):
            total = total + n[:, q * 128 : (q + 1) * 128]
        return total

    zero = jnp.zeros((tile, 128), F32)
    total = lax.fori_loop(0, chunks, inner, zero, unroll=8)
    nmean = jnp.sum(total, axis=-1, keepdims=True) / ff

    def square(j, total):
        at = pl.ds(pl.multiple_of(j * 128, 128), 128)
        c = n_s[:, at] - nmean
        return total + c * c

    total = lax.fori_loop(0, ff // 128, square, zero, unroll=4)
    nrstd = lax.rsqrt(jnp.sum(total, axis=-1, keepdims=True) / ff + EPS)
    dyl = dy_s[step // half_tiles, pl.ds(step % half_tiles * tile, tile), :]

    def outer(j, carry):
        acc, s1, s2 = carry
        at = pl.ds(pl.multiple_of(j * CHUNK, CHUNK), CHUNK)
        nh = (n_s[:, at] - nmean) * nrstd
        n_s[:, at] = nh
        act = (nh * wide[1:2, at] + wide[2:3, at]).astype(BF16)
        act_ref[:, at] = act
        acc = acc + mm(act, w2[at, :])
        da = mm(dyl, w2[at, :], NT)
        danh = da * nh
        gw_ref[1, :, at] += fold_rows(danh)
        gw_ref[2, :, at] += fold_rows(da)
        gain = wide[1:2, at]
        dg = da * gain
        dgn = danh * gain
        dn_s[:, at] = dg
        for q in range(CHUNK // 128):
            s1 = s1 + dg[:, q * 128 : (q + 1) * 128]
            s2 = s2 + dgn[:, q * 128 : (q + 1) * 128]
        return acc, s1, s2

    acc, s1, s2 = lax.fori_loop(0, chunks, outer, (jnp.zeros((tile, width), F32), zero, zero), unroll=8)
    lay_ref[...] = (hidden + acc + nar[9:10]).astype(BF16)
    s1 = jnp.sum(s1, axis=-1, keepdims=True) / ff
    s2 = jnp.sum(s2, axis=-1, keepdims=True) / ff

    def inner_back(j, acc):
        at = pl.ds(pl.multiple_of(j * CHUNK, CHUNK), CHUNK)
        dn = nrstd * (dn_s[:, at] - s1 - n_s[:, at] * s2)
        din = (dn * gp_s[:, at].astype(F32)).astype(BF16)
        din_ref[:, at] = din
        gw_ref[0, :, at] += fold_rows(din.astype(F32))
        return acc + mm(din, w1[:, at], NT)

    dffn = lax.fori_loop(0, chunks, inner_back, jnp.zeros((tile, width), F32), unroll=8)
    dy = dyl.astype(F32)
    gn_ref[5] += fold_rows(dy)
    gn_ref[3] += fold_rows(dffn * hhat)
    gn_ref[4] += fold_rows(dffn)
    dhid = dy + row_norm_back(dffn * nar[7:8], hhat, hrstd)
    dhid_ref[...] = dhid
    gn_ref[2] += fold_rows(dhid)
    dlow = dhid.astype(BF16)
    dlow_ref[...] = dlow
    dpost = mm(dlow, wout[...], NT)
    gn_ref[0] += fold_rows(dpost * ahat)
    gn_ref[1] += fold_rows(dpost)
    dsc_ref[...] = row_norm_back(dpost * nar[4:5], ahat, arstd).astype(BF16)


def middle(scaled, x, cot, wout, w1, w2, narrow, wide, depth, collective_id):
    rows, width = x.shape
    ff = w1.shape[1]
    tile = 256
    tiles = rows // tile

    def at(i):
        return ((i + tiles // 2 * lax.axis_index("sp")) % tiles, 0)

    thin = pl.BlockSpec((tile, width), at)
    fat = pl.BlockSpec((tile, ff), at)
    anywhere = pl.BlockSpec(memory_space=pl.ANY)
    keep = lambda shape: pl.BlockSpec(shape, lambda i: (0,) * len(shape))
    out = pl.pallas_call(
        functools.partial(middle_kernel, depth),
        grid=(tiles,),
        in_specs=[
            thin, thin, anywhere,
            resident(wout.shape), resident(w1.shape), resident(w2.shape),
            resident(narrow.shape), resident(wide.shape),
        ],
        out_specs=[thin, thin, thin, fat, fat, thin, thin, thin, keep((6, 8, width)), keep((3, 8, ff)), anywhere],
        out_shape=[
            jax.ShapeDtypeStruct((rows, width), BF16),
            jax.ShapeDtypeStruct((rows, width), BF16),
            jax.ShapeDtypeStruct((rows, width), BF16),
            jax.ShapeDtypeStruct((rows, ff), BF16),
            jax.ShapeDtypeStruct((rows, ff), BF16),
            jax.ShapeDtypeStruct((rows, width), F32),
            jax.ShapeDtypeStruct((rows, width), BF16),
            jax.ShapeDtypeStruct((rows, width), BF16),
            jax.ShapeDtypeStruct((6, 8, width), F32),
            jax.ShapeDtypeStruct((3, 8, ff), F32),
            jax.ShapeDtypeStruct(cot.shape, cot.dtype),
        ],
        scratch_shapes=[
            pltpu.VMEM((tile, ff), F32),
            pltpu.VMEM((tile, ff), BF16),
            pltpu.VMEM((tile, ff), F32),
            pltpu.VMEM(cot.shape, cot.dtype),
            pltpu.SemaphoreType.DMA((3,)),
            pltpu.SemaphoreType.DMA,
            pltpu.SemaphoreType.DMA,
        ],
        compiler_params=pltpu.CompilerParams(
            vmem_limit_bytes=VMEM_CAP, collective_id=collective_id, has_side_effects=True
        ),
        name="middle",
    )(scaled, x, cot, wout, w1, w2, narrow, wide)
    return *out[:10], out[10].reshape(rows, width)


def enter_kernel(depth, counts, *refs):
    me = Place(depth)
    base = len(counts)
    smalls = refs[:base]
    qkv_shard, out_shard, fc1_shard, tok = refs[base : base + 4]
    qkv_whole, out_whole, fc1_whole, x_out, normed_out, qkv_out, narrow, wide, hs = refs[base + 4 : base + 13]
    small, small_stage, small_whole, qkv_stage, out_stage, fc1_stage, weight = refs[base + 13 : base + 20]
    tok_own, tok_got, normed_tiles, qkv_tiles = refs[base + 20 : base + 24]
    local, send, recv, small_sem, tok_sem, go, come, put_sem, tile_sem = refs[base + 24 : base + 33]
    smalls_here = refs[base + 33 :]
    y = me.y
    qrows, frows = qkv_shard.shape[0] // 2, fc1_shard.shape[0] // 2
    sems = lambda n: (local.at[n], send.at[n], recv.at[n])
    tiny = Gather(me, small, small_stage, small_whole, 0, 16, *sems(0))
    q_a = Gather(me, qkv_shard, qkv_stage, weight, 0, qrows, *sems(1))
    q_b = Gather2(me, qkv_shard, qkv_stage, weight, qrows, qrows, *sems(2))
    w_out = Gather2(me, out_shard, out_stage, out_whole, 0, out_shard.shape[0], *sems(3))
    f_a = Gather(me, fc1_shard, fc1_stage, fc1_whole, 0, frows, *sems(4))
    f_b = Gather(me, fc1_shard, fc1_stage, fc1_whole, frows, frows, *sems(5))
    copies = [pltpu.make_async_copy(s, h, small_sem.at[n]) for n, (s, h) in enumerate(zip(smalls, smalls_here))]
    own = pltpu.make_async_copy(tok.at[y], tok_own, tok_sem)
    for copy in copies + [own]:
        copy.start()
    for g in (q_a, q_b, w_out, f_a, f_b):
        g.ready()
    for copy in copies:
        copy.wait()
    rows = []
    for ref, count in zip(smalls_here, counts):
        row = ref[...].astype(F32).reshape(1, count)
        rows.append(row if count == 128 else jnp.concatenate([row, jnp.zeros((1, 128 - count), F32)], axis=1))
    rows.append(jnp.zeros((16 - len(counts), 128), F32))
    small[...] = jnp.concatenate(rows, axis=0).astype(BF16)
    tiny.ready()
    half, width = tok_own.shape
    cut = half // 4

    def trade(n):
        span = pl.ds(n * cut, cut if n == 0 else half - cut)
        return remote(tok.at[1 - y, span], tok_got.at[span], go.at[n], come.at[n], me.next_y)

    me.greet()
    tiny.begin()
    q_a.begin()
    q_b.begin()
    trade(0).start()
    tiny.spread()
    q_b.pass_z()
    q_a.spread()
    tiny.from_y()
    tiny.from_x()
    w_out.begin()
    tiny.from_corner()
    q_a.from_y()
    trade(1).start()
    q_b.pass_x()
    q_b.pass_twin()
    w_out.pass_z()
    tiny.end()
    part = counts[0]
    each = 128 // part
    for d in range(depth * 8 // each):
        tiles = []
        for k in range(d * each, (d + 1) * each):
            tile = small_whole[k // 8, k // 4 % 2, k // 2 % 2, k % 2].astype(F32)
            tiles.append(tile[:, 0:part])
            wide[0:3, k * 128 : (k + 1) * 128] = tile[10:13]
        narrow[:, d * 128 : (d + 1) * 128] = jnp.concatenate(tiles, axis=1)
    hs[...] = jnp.concatenate(
        [small_whole[0, 0, 0, k].astype(F32)[13:14, 0 : counts[13]] for k in range(2)], axis=1
    )
    q_a.from_x()
    q_a.from_corner()
    f_a.begin()
    f_b.begin()
    w_out.pass_x()
    w_out.pass_twin()
    q_b.arrived()
    q_b.pass_twin_far()
    q_a.end()
    q_b.end()
    put_weight = pltpu.make_async_copy(weight, qkv_whole, put_sem.at[0])
    put_weight.start()
    own.wait()
    put_own = pltpu.make_async_copy(tok_own, x_out.at[y], put_sem.at[1])
    put_own.start()
    tile_rows = normed_tiles.shape[1]
    tiles = normed_tiles.shape[0]

    def puts(i, at):
        span = pl.ds(at * half + i * tile_rows, tile_rows)
        return (
            pltpu.make_async_copy(normed_tiles.at[i], normed_out.at[span], tile_sem.at[0, i]),
            pltpu.make_async_copy(qkv_tiles.at[i], qkv_out.at[span], tile_sem.at[1, i]),
        )

    def project(source, at):
        def body(i, _):
            hat, _ = row_norm(source[pl.ds(i * tile_rows, tile_rows), :].astype(F32))
            normed = (hat * narrow[0:1] + narrow[1:2]).astype(BF16)
            normed_tiles[i] = normed
            for j in range(3 * width // 512):
                span = slice(j * 512, (j + 1) * 512)
                piece = mm(normed, weight[:, :, :, :, :, span].reshape(width, 512))
                third, start = j * 512 // width, j * 512 % width
                if third != 1:
                    row = 2 + third // 2
                    piece = piece + narrow[row : row + 1, start : start + 512]
                qkv_tiles[i, :, span] = piece.astype(BF16)
            for put in puts(i, at):
                put.start()
            return 0

        lax.fori_loop(0, tiles, body, 0)

    project(tok_own, y)
    w_out.arrived()
    w_out.pass_twin_far()
    f_a.landed()
    f_a.x_begin()
    f_b.landed()
    for n in range(2):
        trade(n).wait()
    put_got = pltpu.make_async_copy(tok_got, x_out.at[1 - y], put_sem.at[2])
    put_got.start()
    for i in range(tiles):
        for put in puts(i, y):
            put.wait()
    project(tok_got, 1 - y)
    f_a.x_end()
    w_out.end()
    for i in range(tiles):
        for put in puts(i, 1 - y):
            put.wait()
    put_weight.wait()
    put_own.wait()
    put_got.wait()


def enter(smalls, qkv_weight, out_weight, fc1_weight, tokens, depth, collective_id):
    shards = [qkv_weight, out_weight, fc1_weight]
    counts = [s.shape[0] for s in smalls]
    _, half, width = tokens.shape
    tile = 256
    anywhere = pl.BlockSpec(memory_space=pl.ANY)
    vmem = pl.BlockSpec(memory_space=pltpu.VMEM)
    whole = lambda s: (depth, 2, 2, 2) + s.shape
    out = pl.pallas_call(
        functools.partial(enter_kernel, depth, counts),
        in_specs=[anywhere] * (len(counts) + 4),
        out_specs=[anywhere] * 6 + [vmem] * 3,
        out_shape=[jax.ShapeDtypeStruct(whole(s), s.dtype) for s in shards]
        + [
            jax.ShapeDtypeStruct(tokens.shape, tokens.dtype),
            jax.ShapeDtypeStruct((2 * half, width), BF16),
            jax.ShapeDtypeStruct((2 * half, 3 * width), BF16),
            jax.ShapeDtypeStruct((16, depth * 8 * counts[0]), F32),
            jax.ShapeDtypeStruct((8, depth * 8 * counts[10]), F32),
            jax.ShapeDtypeStruct((1, 2 * counts[13]), F32),
        ],
        scratch_shapes=[
            pltpu.VMEM((16, 128), BF16),
            pltpu.VMEM((16, 128), BF16),
            pltpu.VMEM((depth, 2, 2, 2, 16, 128), BF16),
        ]
        + [pltpu.VMEM(s.shape, s.dtype) for s in shards]
        + [
            pltpu.VMEM(whole(qkv_weight), BF16),
            pltpu.VMEM((half, width), BF16),
            pltpu.VMEM((half, width), BF16),
            pltpu.VMEM((half // tile, tile, width), BF16),
            pltpu.VMEM((half // tile, tile, 3 * width), BF16),
            pltpu.SemaphoreType.DMA((6,)),
            pltpu.SemaphoreType.DMA((6, 2 * depth + 3)),
            pltpu.SemaphoreType.DMA((6, 2 * depth + 3)),
            pltpu.SemaphoreType.DMA((len(counts),)),
            pltpu.SemaphoreType.DMA,
            pltpu.SemaphoreType.DMA((2,)),
            pltpu.SemaphoreType.DMA((2,)),
            pltpu.SemaphoreType.DMA((3,)),
            pltpu.SemaphoreType.DMA((2, half // tile)),
        ]
        + [pltpu.VMEM((n,), BF16) for n in counts],
        compiler_params=pltpu.CompilerParams(
            collective_id=collective_id, has_side_effects=True, vmem_limit_bytes=VMEM_CAP
        ),
        name="enter",
    )(*smalls, *shards, tokens)
    return flat(out[0]), flat(out[1]), out[2], out[3].reshape(-1, width), *out[4:]


def flat(whole):
    return whole.reshape((-1,) + whole.shape[5:])


def leave_kernel(depth, part, heads, *refs):
    dq_ref, dk_ref, dv_ref, x_ref, dhid_ref, w_ref, p_ref = refs[:7]
    parts = refs[7:10]
    thin_ref, fat_ref, delta_ref, hs_ref = refs[10:14]
    out, qkv_sum, small_sum = refs[14:17]
    local, send, recv, go, come, store, g_acc, thin, fat, small, leaving, landing, stage = refs[17:30]
    scratch = refs[30:]
    me = Place(depth)
    step = pl.program_id(0)
    half_tiles = leaving.shape[0]
    tile, width = x_ref.shape
    rows = parts[0].shape[4]
    scatters = [
        Scatter(
            me, parts[n], 0, rows, *scratch[4 * n : 4 * n + 4], local.at[n], send.at[n], recv.at[n],
            qkv_sum.at[:, pl.ds(n * width, width)],
        )
        for n in range(3)
    ]
    smalls = Scatter(me, small, 0, 16, *scratch[12:16], local.at[3], send.at[3], recv.at[3], small_sum)

    def trade(j):
        return remote(leaving.at[j], landing.at[j], go.at[j], come.at[j], me.next_y)

    def put(y, j):
        return pltpu.make_async_copy(stage.at[j], out.at[y, pl.ds(j * tile, tile)], store.at[j])

    @pl.when(step == 0)
    def _():
        g_acc[...] = jnp.zeros_like(g_acc)
        me.greet()
        for s in scatters:
            s.begin()

    @pl.when(step == 2)
    def _():
        for s in scatters:
            s.across()

    hat, rstd = row_norm(x_ref[...].astype(F32))
    dnormed = mm(dq_ref[...], w_ref[:, 0:width], NT)
    dnormed = dnormed + mm(dk_ref[...], w_ref[:, width : 2 * width], NT)
    dnormed = dnormed + mm(dv_ref[...], w_ref[:, 2 * width : 3 * width], NT)
    g_acc[0] += fold_rows(dnormed * hat)
    g_acc[1] += fold_rows(dnormed)
    g_acc[2] += fold_rows(dq_ref[...].astype(F32))
    g_acc[3] += fold_rows(dv_ref[...].astype(F32))
    grad = dhid_ref[...] + row_norm_back(dnormed * p_ref[0:1], hat, rstd)

    @pl.when(step < half_tiles)
    def _():
        leaving[step] = grad.astype(BF16)
        trade(step).start()

    @pl.when(step >= half_tiles)
    def _():
        stage[step - half_tiles] = grad
        put(me.y, step - half_tiles).start()

    @pl.when(step == pl.num_programs(0) - 1)
    def _():
        thin[...] = jnp.zeros_like(thin)
        fat[...] = jnp.zeros_like(fat)
        for k in range(4):
            thin[k : k + 1, :] = jnp.sum(g_acc[k], axis=0, keepdims=True)
        for k in range(6):
            thin[4 + k : 5 + k, :] = jnp.sum(thin_ref[k], axis=0, keepdims=True)
        for k in range(3):
            fat[10 + k : 11 + k, :] = jnp.sum(fat_ref[k], axis=0, keepdims=True)
        lanes = lax.broadcasted_iota(jnp.int32, (1, 128), 1)
        scale = jnp.zeros((1, 128), F32)
        for p in range(delta_ref.shape[0]):
            for h in range(2):
                scale = jnp.where(lanes == 2 * p + h, jnp.sum(delta_ref[p, h]), scale)
        scale = scale / jnp.concatenate([hs_ref[...], jnp.ones((1, 128 - 2 * heads), F32)], axis=1)
        each = 128 // part
        is_scale = lax.broadcasted_iota(jnp.int32, (16, 128), 0) == 13
        for d in range(depth * 8):
            block = thin[:, d // each * 128 : (d // each + 1) * 128]
            turn = d % each * part
            block = pltpu.roll(block, 128 - turn, 1) if turn else block
            block = block + fat[:, d * 128 : (d + 1) * 128]
            row = pltpu.roll(scale, 128 - heads, 1) if d % 2 else scale
            small[d // 8, d // 4 % 2, d // 2 % 2, d % 2] = jnp.where(is_scale, row, block)
        smalls.begin()
        v, k, q = scatters[2], scatters[1], scatters[0]
        v.along_x()
        smalls.across()
        k.along_x()
        v.along_y()
        smalls.along_x()
        q.along_x()
        k.along_y()
        smalls.along_y()
        v.end()
        q.along_y()
        for j in range(half_tiles):
            trade(j).wait()
            put(me.y, j).wait()
            stage[j] = landing[j].astype(F32)
            put(1 - me.y, j).start()
        k.end()
        smalls.end()
        q.end()
        for j in range(half_tiles):
            put(1 - me.y, j).wait()


def leave(dq, dk, dv, x, dhid, weight, params, parts, thin, fat, delta, hs, depth, collective_id):
    rows, width = x.shape
    tile = 256
    tiles = rows // tile
    parts = [shard_view(p, depth) for p in parts]
    part = width // (depth * 8)
    heads = hs.shape[1] // 2

    def at(i):
        return ((i + tiles // 2 * (1 - lax.axis_index("sp"))) % tiles, 0)

    block = pl.BlockSpec((tile, width), at)
    anywhere = pl.BlockSpec(memory_space=pl.ANY)
    pieces = [(p.shape[4], p.shape[5], p.dtype) for p in parts] + [(16, 128, F32)]
    keep = lambda shape: pl.BlockSpec(shape, lambda i: (0,) * len(shape))
    out_shape = [
        jax.ShapeDtypeStruct((2, rows // 2, width), F32),
        jax.ShapeDtypeStruct((parts[0].shape[4], 3 * width), F32),
        jax.ShapeDtypeStruct((16, 128), F32),
    ]
    return pl.pallas_call(
        functools.partial(leave_kernel, depth, part, heads),
        grid=(tiles,),
        in_specs=[block] * 5
        + [resident(weight.shape), resident(params.shape)]
        + [anywhere] * 3
        + [resident(a.shape) for a in (thin, fat, delta, hs)],
        out_specs=[anywhere, keep(out_shape[1].shape), keep(out_shape[2].shape)],
        out_shape=out_shape,
        scratch_shapes=[
            pltpu.SemaphoreType.DMA((4,)),
            pltpu.SemaphoreType.DMA((4, 3 + depth)),
            pltpu.SemaphoreType.DMA((4, 3 + depth)),
            pltpu.SemaphoreType.DMA((tiles // 2,)),
            pltpu.SemaphoreType.DMA((tiles // 2,)),
            pltpu.SemaphoreType.DMA((tiles // 2,)),
            pltpu.VMEM((4, 8, width), F32),
            pltpu.VMEM((16, width), F32),
            pltpu.VMEM((16, fat.shape[2]), F32),
            pltpu.VMEM((depth, 2, 2, 2, 16, 128), F32),
            pltpu.VMEM((tiles // 2, tile, width), BF16),
            pltpu.VMEM((tiles // 2, tile, width), BF16),
            pltpu.VMEM((tiles // 2, tile, width), F32),
        ]
        + scatter_scratch(pieces, depth),
        compiler_params=pltpu.CompilerParams(
            collective_id=collective_id, has_side_effects=True, vmem_limit_bytes=VMEM_CAP
        ),
        name="leave",
    )(dq, dk, dv, x, dhid, weight, params, *parts, thin, fat, delta, hs)


def fast_shards(
    tokens, doc_lengths, out_cotangent, in_gain, in_bias, qkv_weight, q_bias, v_bias, head_scale, attn_gain,
    attn_bias, out_weight, out_bias, ffn_gain, ffn_bias, fc1_weight, fc1_bias, mid_gain, mid_bias, fc2_weight,
    fc2_bias,
):
    depth = lax.axis_size("dp") // 4
    devices = depth * 8
    half = tokens.shape[1]
    rows = 2 * half
    width = tokens.shape[2]
    me = lax.axis_index("sp")

    narrow_in = [in_gain, in_bias, q_bias, v_bias, attn_gain, attn_bias, out_bias, ffn_gain, ffn_bias, fc2_bias]
    wide_in = [fc1_bias, mid_gain, mid_bias]
    part = width // devices
    heads_each = head_scale.shape[0]
    wqkv, wout, begun, x, normed, qkv, narrow, wide, hs = enter(
        narrow_in + wide_in + [head_scale], qkv_weight, out_weight, fc1_weight, tokens, depth, 0
    )
    scaled, mixed, lse, w1, w2 = attend_fwd(qkv, doc_lengths, hs, begun, fc2_weight, depth, 1)
    w1, w2 = flat(w1), flat(w2)
    layer, post, ffn_in, active, d_inner, d_hidden, d_low, d_scaled, grads_narrow, grads_wide, dy = middle(
        scaled, x, out_cotangent, wout, w1, w2, narrow, wide, depth, 4
    )

    def weight_grad(left, right):
        return jnp.einsum("ti,tj->ij", left, right, preferred_element_type=F32).astype(BF16)

    g_fc2 = weight_grad(active, dy)
    g_fc1 = weight_grad(ffn_in, d_inner)
    g_out = weight_grad(post, d_low)
    (dq, dk, dv, delta), (s_fc2, s_fc1, s_out), layer_out = attend_bwd(
        qkv, mixed, d_scaled, lse, doc_lengths, hs, [g_fc2, g_fc1, g_out], layer, depth, 2
    )
    g_q = weight_grad(normed, dq)
    g_k = weight_grad(normed, dk)
    g_v = weight_grad(normed, dv)
    input_grad, s_qkv, s_small = leave(
        dq, dk, dv, x, d_hidden, wqkv, narrow, [g_q, g_k, g_v], grads_narrow, grads_wide, delta, hs, depth, 3
    )
    nar = [s_small[k, :part] for k in range(10)]
    wid = [s_small[10 + k] for k in range(3)]
    s_hs = s_small[13, :heads_each]
    return (
        layer_out, input_grad, nar[0], nar[1], s_qkv, nar[2], nar[3], s_hs, nar[4], nar[5], s_out, nar[6], nar[7],
        nar[8], s_fc1, wid[0], wid[1], wid[2], s_fc2, nar[9],
    )


LONGEST = 2048


def layer_norm(values, norm_gain, norm_shift):
    center = values - jnp.mean(values, axis=-1, keepdims=True)
    spread = jnp.mean(center * center, axis=-1, keepdims=True)
    return center * lax.rsqrt(spread + EPS) * norm_gain + norm_shift


def doc_index(lengths, row_count):
    seq_ends = jnp.cumsum(lengths)
    places = jnp.arange(row_count, dtype=jnp.int32)
    return jnp.sum((places[:, None] >= seq_ends[None, :]).astype(jnp.int32), axis=1)


def block_scores(query_block, key_heads, doc_query, doc_keys, pos_query, pos_keys, score_scale):
    scores = (
        jnp.einsum("qhd,khd->hqk", query_block, key_heads, preferred_element_type=jnp.float32)
        * score_scale
    )
    allowed = (doc_query[:, None] == doc_keys[None, :]) & (pos_keys[None, :] <= pos_query[:, None])
    return jnp.where(allowed[None], scores, -1e30)


def reduce_grads(grad_set):
    return (
        lax.psum_scatter(grad_set[0], ("dp", "sp"), scatter_dimension=0, tiled=True),
        lax.psum_scatter(grad_set[1], ("dp", "sp"), scatter_dimension=0, tiled=True),
        lax.psum_scatter(grad_set[2], ("dp", "sp"), scatter_dimension=0, tiled=True),
        lax.psum_scatter(grad_set[3], ("dp", "sp"), scatter_dimension=0, tiled=True),
        lax.psum_scatter(grad_set[4], ("dp", "sp"), scatter_dimension=0, tiled=True),
        lax.psum_scatter(grad_set[5], ("dp", "sp"), scatter_dimension=0, tiled=True),
        lax.psum_scatter(grad_set[6], ("dp", "sp"), scatter_dimension=0, tiled=True),
        lax.psum_scatter(grad_set[7], ("dp", "sp"), scatter_dimension=0, tiled=True),
        lax.psum_scatter(grad_set[8], ("dp", "sp"), scatter_dimension=0, tiled=True),
        lax.psum_scatter(grad_set[9], ("dp", "sp"), scatter_dimension=0, tiled=True),
        lax.psum_scatter(grad_set[10], ("dp", "sp"), scatter_dimension=0, tiled=True),
        lax.psum_scatter(grad_set[11], ("dp", "sp"), scatter_dimension=0, tiled=True),
        lax.psum_scatter(grad_set[12], ("dp", "sp"), scatter_dimension=0, tiled=True),
        lax.psum_scatter(grad_set[13], ("dp", "sp"), scatter_dimension=0, tiled=True),
        lax.psum_scatter(grad_set[14], ("dp", "sp"), scatter_dimension=0, tiled=True),
        lax.psum_scatter(grad_set[15], ("dp", "sp"), scatter_dimension=0, tiled=True),
        lax.psum_scatter(grad_set[16], ("dp", "sp"), scatter_dimension=0, tiled=True),
    )


def shards(
    tokens,
    doc_lengths,
    out_cotangent,
    in_gain,
    in_bias,
    qkv_weight,
    q_bias,
    v_bias,
    head_scale,
    attn_gain,
    attn_bias,
    out_weight,
    out_bias,
    ffn_gain,
    ffn_bias,
    fc1_weight,
    fc1_bias,
    mid_gain,
    mid_bias,
    fc2_weight,
    fc2_bias,
):
    micro_count = tokens.shape[0]
    tok_count = tokens.shape[1]
    model_width = tokens.shape[2]
    sp_count = lax.axis_size("sp")
    group_rows = tok_count * sp_count
    local_width = model_width // sp_count
    head_local = head_scale.shape[0]
    head_dim = local_width // head_local
    score_scale = 1.0 / math.sqrt(head_dim)
    window_rows = LONGEST
    block_rows = min(512, window_rows)
    block_count = group_rows // block_rows
    head_gains = head_scale.astype(jnp.float32)
    positions = jnp.arange(group_rows, dtype=jnp.int32)
    starts = jnp.arange(block_count, dtype=jnp.int32) * block_rows

    def collect():
        return (
            lax.all_gather(in_gain, ("dp", "sp"), axis=0, tiled=True),
            lax.all_gather(in_bias, ("dp", "sp"), axis=0, tiled=True),
            lax.all_gather(qkv_weight, ("dp", "sp"), axis=0, tiled=True),
            lax.all_gather(q_bias, ("dp", "sp"), axis=0, tiled=True),
            lax.all_gather(v_bias, ("dp", "sp"), axis=0, tiled=True),
            lax.all_gather(attn_gain, ("dp", "sp"), axis=0, tiled=True),
            lax.all_gather(attn_bias, ("dp", "sp"), axis=0, tiled=True),
            lax.all_gather(out_weight, ("dp", "sp"), axis=0, tiled=True),
            lax.all_gather(out_bias, ("dp", "sp"), axis=0, tiled=True),
            lax.all_gather(ffn_gain, ("dp", "sp"), axis=0, tiled=True),
            lax.all_gather(ffn_bias, ("dp", "sp"), axis=0, tiled=True),
            lax.all_gather(fc1_weight, ("dp", "sp"), axis=0, tiled=True),
            lax.all_gather(fc1_bias, ("dp", "sp"), axis=0, tiled=True),
            lax.all_gather(mid_gain, ("dp", "sp"), axis=0, tiled=True),
            lax.all_gather(mid_bias, ("dp", "sp"), axis=0, tiled=True),
            lax.all_gather(fc2_weight, ("dp", "sp"), axis=0, tiled=True),
            lax.all_gather(fc2_bias, ("dp", "sp"), axis=0, tiled=True),
        )

    def split_heads(heads_in):
        query_heads = heads_in[:, 0].reshape(group_rows, head_local, head_dim)
        key_heads = heads_in[:, 1].reshape(group_rows, head_local, head_dim)
        value_heads = heads_in[:, 2].reshape(group_rows, head_local, head_dim)
        return (query_heads, key_heads, value_heads)

    def attend_back(heads_in, lengths, log_total, grad_mixed):
        query_heads, key_heads, value_heads = split_heads(heads_in)
        doc_ids = doc_index(lengths, group_rows)

        def one_block(block_carry, pair):
            grad_keys, grad_values = block_carry
            row_start, block_lse = pair
            query_block = lax.dynamic_slice_in_dim(query_heads, row_start, block_rows, 0)
            grad_block = lax.dynamic_slice_in_dim(grad_mixed, row_start, block_rows, 0)
            masked = block_scores(
                query_block,
                key_heads,
                lax.dynamic_slice_in_dim(doc_ids, row_start, block_rows, 0),
                doc_ids,
                lax.dynamic_slice_in_dim(positions, row_start, block_rows, 0),
                positions,
                score_scale,
            )
            prob_rows = jnp.exp(masked - block_lse[:, :, None])
            value_part = jnp.einsum(
                "hqk,qhd->khd",
                prob_rows.astype(jnp.bfloat16),
                grad_block,
                preferred_element_type=jnp.float32,
            )
            grad_probs = jnp.einsum(
                "qhd,khd->hqk", grad_block, value_heads, preferred_element_type=jnp.float32
            )
            row_inner = jnp.sum(prob_rows * grad_probs, axis=-1, keepdims=True)
            grad_scores = (prob_rows * (grad_probs - row_inner)).astype(jnp.bfloat16)
            grad_query = (
                jnp.einsum(
                    "hqk,khd->qhd", grad_scores, key_heads, preferred_element_type=jnp.float32
                )
                * score_scale
            )
            key_part = jnp.einsum(
                "hqk,qhd->khd", grad_scores, query_block, preferred_element_type=jnp.float32
            )
            grad_keys = grad_keys + key_part
            grad_values = grad_values + value_part
            return ((grad_keys, grad_values), grad_query)

        zero_heads = jnp.zeros((group_rows, head_local, head_dim), jnp.float32)
        (grad_keys, grad_values), grad_queries = lax.scan(
            one_block, (zero_heads, zero_heads), (starts, log_total)
        )
        stacked = jnp.stack(
            [
                grad_queries.reshape(group_rows, local_width),
                (grad_keys * score_scale).reshape(group_rows, local_width),
                grad_values.reshape(group_rows, local_width),
            ],
            axis=1,
        )
        return stacked.astype(jnp.bfloat16)

    outputs = []
    input_grads = []
    total_grads = None
    scale_total = jnp.zeros((head_local,), jnp.float32)
    for micro_index in range(micro_count):
        forward_set = collect()
        (
            forward_wide_in_gain,
            forward_wide_in_bias,
            forward_wide_qkv,
            forward_wide_q_bias,
            forward_wide_v_bias,
            forward_wide_attn_gain,
            forward_wide_attn_bias,
            forward_wide_out,
            forward_wide_out_bias,
            forward_wide_ffn_gain,
            forward_wide_ffn_bias,
            forward_wide_fc1,
            forward_wide_fc1_bias,
            forward_wide_mid_gain,
            forward_wide_mid_bias,
            forward_wide_fc2,
            forward_wide_fc2_bias,
        ) = forward_set
        forward_tok_rows = tokens[micro_index].astype(jnp.float32)
        forward_lengths = doc_lengths[0, micro_index]
        forward_normed = layer_norm(
            forward_tok_rows,
            forward_wide_in_gain.astype(jnp.float32),
            forward_wide_in_bias.astype(jnp.float32),
        ).astype(jnp.bfloat16)
        bias_row = jnp.concatenate(
            [forward_wide_q_bias, jnp.zeros_like(forward_wide_q_bias), forward_wide_v_bias]
        ).astype(jnp.float32)
        projected = (
            jnp.dot(forward_normed, forward_wide_qkv, preferred_element_type=jnp.float32) + bias_row
        )
        qkv_sent = projected.astype(jnp.bfloat16).reshape(tok_count, 3, model_width)
        forward_heads_in = lax.all_to_all(qkv_sent, "sp", split_axis=2, concat_axis=0, tiled=True)
        attend_query_heads, attend_key_heads, attend_value_heads = split_heads(forward_heads_in)
        attend_doc_ids = doc_index(forward_lengths, group_rows)

        def attend_one_block(row_start):
            query_block = lax.dynamic_slice_in_dim(attend_query_heads, row_start, block_rows, 0)
            masked = block_scores(
                query_block,
                attend_key_heads,
                lax.dynamic_slice_in_dim(attend_doc_ids, row_start, block_rows, 0),
                attend_doc_ids,
                lax.dynamic_slice_in_dim(positions, row_start, block_rows, 0),
                positions,
                score_scale,
            )
            row_max = jnp.max(masked, axis=-1, keepdims=True)
            raised = jnp.exp(masked - row_max)
            row_total = jnp.sum(raised, axis=-1, keepdims=True)
            prob_rows = (raised / row_total).astype(jnp.bfloat16)
            head_mixed = jnp.einsum(
                "hqk,khd->qhd", prob_rows, attend_value_heads, preferred_element_type=jnp.float32
            )
            return (head_mixed, (row_max + jnp.log(row_total))[:, :, 0])

        head_mixed, attend_log_total = lax.map(attend_one_block, starts)
        forward_head_mixed = head_mixed.reshape(group_rows, head_local, head_dim)
        scaled = (
            (forward_head_mixed * head_gains[None, :, None])
            .reshape(group_rows, local_width)
            .astype(jnp.bfloat16)
        )
        forward_attn_rows = lax.all_to_all(
            scaled, "sp", split_axis=0, concat_axis=1, tiled=True
        ).astype(jnp.float32)
        forward_post_norm = layer_norm(
            forward_attn_rows,
            forward_wide_attn_gain.astype(jnp.float32),
            forward_wide_attn_bias.astype(jnp.float32),
        ).astype(jnp.bfloat16)
        forward_hidden = (
            forward_tok_rows
            + jnp.dot(forward_post_norm, forward_wide_out, preferred_element_type=jnp.float32)
            + forward_wide_out_bias.astype(jnp.float32)
        )
        forward_ffn_in = layer_norm(
            forward_hidden,
            forward_wide_ffn_gain.astype(jnp.float32),
            forward_wide_ffn_bias.astype(jnp.float32),
        ).astype(jnp.bfloat16)
        forward_ffn_inner = jnp.dot(
            forward_ffn_in, forward_wide_fc1, preferred_element_type=jnp.float32
        ) + forward_wide_fc1_bias.astype(jnp.float32)
        forward_active = layer_norm(
            jax.nn.gelu(forward_ffn_inner),
            forward_wide_mid_gain.astype(jnp.float32),
            forward_wide_mid_bias.astype(jnp.float32),
        ).astype(jnp.bfloat16)
        output = (
            forward_hidden
            + jnp.dot(forward_active, forward_wide_fc2, preferred_element_type=jnp.float32)
            + forward_wide_fc2_bias.astype(jnp.float32)
        )
        forward_kept_values = (
            forward_normed,
            forward_heads_in,
            forward_head_mixed,
            attend_log_total,
            forward_attn_rows,
            forward_post_norm,
            forward_hidden,
            forward_ffn_in,
            forward_ffn_inner,
            forward_active,
        )
        output, kept_values = (output, forward_kept_values)
        backward_set = collect()
        (
            wide_in_gain,
            wide_in_bias,
            wide_qkv,
            wide_q_bias,
            wide_v_bias,
            wide_attn_gain,
            wide_attn_bias,
            wide_out,
            wide_out_bias,
            wide_ffn_gain,
            wide_ffn_bias,
            wide_fc1,
            wide_fc1_bias,
            wide_mid_gain,
            wide_mid_bias,
            wide_fc2,
            wide_fc2_bias,
        ) = backward_set
        (
            normed,
            backward_heads_in,
            backward_head_mixed,
            backward_log_total,
            attn_rows,
            post_norm,
            hidden,
            ffn_in,
            ffn_inner,
            active,
        ) = kept_values
        tok_rows = tokens[micro_index].astype(jnp.float32)
        backward_lengths = doc_lengths[0, micro_index]
        grad_out = out_cotangent[micro_index].astype(jnp.float32)
        fc2_bias_grad = jnp.sum(grad_out, axis=0)
        grad_low = grad_out.astype(jnp.bfloat16)
        fc2_grad = jnp.einsum("ti,tj->ij", active, grad_low, preferred_element_type=jnp.float32)
        grad_active = jnp.einsum(
            "tj,ij->ti", grad_low, wide_fc2, preferred_element_type=jnp.float32
        )
        gelu_out, gelu_back = jax.vjp(jax.nn.gelu, ffn_inner)
        _, mid_back = jax.vjp(
            layer_norm,
            gelu_out,
            wide_mid_gain.astype(jnp.float32),
            wide_mid_bias.astype(jnp.float32),
        )
        grad_gelu, mid_gain_grad, mid_bias_grad = mid_back(grad_active)
        (grad_inner,) = gelu_back(grad_gelu)
        inner_low = grad_inner.astype(jnp.bfloat16)
        fc1_bias_grad = jnp.sum(inner_low.astype(jnp.float32), axis=0)
        fc1_grad = jnp.einsum("ti,tj->ij", ffn_in, inner_low, preferred_element_type=jnp.float32)
        grad_ffn = jnp.einsum("tj,ij->ti", inner_low, wide_fc1, preferred_element_type=jnp.float32)
        _, ffn_back = jax.vjp(
            layer_norm, hidden, wide_ffn_gain.astype(jnp.float32), wide_ffn_bias.astype(jnp.float32)
        )
        grad_hid, ffn_gain_grad, ffn_bias_grad = ffn_back(grad_ffn)
        grad_hidden = grad_out + grad_hid
        out_bias_grad = jnp.sum(grad_hidden, axis=0)
        hidden_low = grad_hidden.astype(jnp.bfloat16)
        out_grad = jnp.einsum(
            "ti,tj->ij", post_norm, hidden_low, preferred_element_type=jnp.float32
        )
        grad_post = jnp.einsum(
            "tj,ij->ti", hidden_low, wide_out, preferred_element_type=jnp.float32
        )
        _, attn_back = jax.vjp(
            layer_norm,
            attn_rows,
            wide_attn_gain.astype(jnp.float32),
            wide_attn_bias.astype(jnp.float32),
        )
        grad_attn, attn_gain_grad, attn_bias_grad = attn_back(grad_post)
        grad_heads = lax.all_to_all(
            grad_attn.astype(jnp.bfloat16), "sp", split_axis=1, concat_axis=0, tiled=True
        )
        grad_scaled = grad_heads.astype(jnp.float32).reshape(group_rows, head_local, head_dim)
        scale_grad = jnp.sum(grad_scaled * backward_head_mixed, axis=(0, 2))
        backward_grad_mixed = (grad_scaled * head_gains[None, :, None]).astype(jnp.bfloat16)
        grad_qkv = attend_back(
            backward_heads_in, backward_lengths, backward_log_total, backward_grad_mixed
        )
        returned = lax.all_to_all(grad_qkv, "sp", split_axis=0, concat_axis=2, tiled=True).reshape(
            tok_count, 3 * model_width
        )
        column_sums = jnp.sum(returned.astype(jnp.float32), axis=0)
        q_bias_grad = column_sums[:model_width]
        v_bias_grad = column_sums[2 * model_width :]
        qkv_grad = jnp.einsum("ti,tj->ij", normed, returned, preferred_element_type=jnp.float32)
        grad_normed = jnp.einsum(
            "tj,ij->ti", returned, wide_qkv, preferred_element_type=jnp.float32
        )
        _, in_back = jax.vjp(
            layer_norm, tok_rows, wide_in_gain.astype(jnp.float32), wide_in_bias.astype(jnp.float32)
        )
        grad_rows, in_gain_grad, in_bias_grad = in_back(grad_normed)
        input_grad = grad_hidden + grad_rows
        grad_set = (
            in_gain_grad,
            in_bias_grad,
            qkv_grad,
            q_bias_grad,
            v_bias_grad,
            attn_gain_grad,
            attn_bias_grad,
            out_grad,
            out_bias_grad,
            ffn_gain_grad,
            ffn_bias_grad,
            fc1_grad,
            fc1_bias_grad,
            mid_gain_grad,
            mid_bias_grad,
            fc2_grad,
            fc2_bias_grad,
        )
        input_grad, grad_set, scale_grad = (input_grad, grad_set, scale_grad)
        grad_set = reduce_grads(grad_set)
        total_grads = (
            grad_set if total_grads is None else jax.tree.map(jnp.add, total_grads, grad_set)
        )
        scale_total = scale_total + scale_grad
        outputs.append(output)
        input_grads.append(input_grad)
    scale_sum = lax.psum(scale_total, "dp")
    layer_out = jnp.stack(outputs).astype(jnp.bfloat16)
    input_grad = jnp.stack(input_grads)
    return (
        layer_out,
        input_grad,
        total_grads[0],
        total_grads[1],
        total_grads[2],
        total_grads[3],
        total_grads[4],
        scale_sum,
        total_grads[5],
        total_grads[6],
        total_grads[7],
        total_grads[8],
        total_grads[9],
        total_grads[10],
        total_grads[11],
        total_grads[12],
        total_grads[13],
        total_grads[14],
        total_grads[15],
        total_grads[16],
    )


def fits(args):
    dp, sp = lax.axis_size("dp"), lax.axis_size("sp")
    tokens, lengths, in_gain, fc1_bias = args[0], args[1], args[3], args[16]
    return (
        sp == 2
        and tokens.shape[0] == 2
        and dp % 4 == 0
        and dp >= 8
        and 2 * tokens.shape[1] == LONGEST
        and lengths.shape[2] * BLOCK == LONGEST
        and 128 % in_gain.shape[0] == 0
        and fc1_bias.shape[0] == 128
        and tokens.shape[2] == 128 * args[8].shape[0]
    )


def body(*args):
    return fast_shards(*args) if fits(args) else shards(*args)


def solution(mesh):
    return jax.shard_map(
        body,
        mesh=mesh,
        in_specs=(
            P(None, ("dp", "sp"), None),
            P("dp", None, None),
            P(None, ("dp", "sp"), None),
            P(("dp", "sp")),
            P(("dp", "sp")),
            P(("dp", "sp"), None),
            P(("dp", "sp")),
            P(("dp", "sp")),
            P("sp"),
            P(("dp", "sp")),
            P(("dp", "sp")),
            P(("dp", "sp"), None),
            P(("dp", "sp")),
            P(("dp", "sp")),
            P(("dp", "sp")),
            P(("dp", "sp"), None),
            P(("dp", "sp")),
            P(("dp", "sp")),
            P(("dp", "sp")),
            P(("dp", "sp"), None),
            P(("dp", "sp")),
        ),
        out_specs=(
            P(None, ("dp", "sp"), None),
            P(None, ("dp", "sp"), None),
            P(("dp", "sp")),
            P(("dp", "sp")),
            P(("dp", "sp"), None),
            P(("dp", "sp")),
            P(("dp", "sp")),
            P("sp"),
            P(("dp", "sp")),
            P(("dp", "sp")),
            P(("dp", "sp"), None),
            P(("dp", "sp")),
            P(("dp", "sp")),
            P(("dp", "sp")),
            P(("dp", "sp"), None),
            P(("dp", "sp")),
            P(("dp", "sp")),
            P(("dp", "sp")),
            P(("dp", "sp"), None),
            P(("dp", "sp")),
        ),
        check_vma=False,
    )
```

```python
import functools
import math

import jax
import jax.numpy as jnp
from jax import lax
from jax.experimental import pallas as pl
from jax.experimental.pallas import tpu as pltpu
from jax.sharding import PartitionSpec as P

EPS = 1e-05
BLOCK = 512
LOG2E = math.log2(math.e)
NEG = -1e30
F32 = jnp.float32
BF16 = jnp.bfloat16
VMEM_CAP = 60 * 1024 * 1024
NT = (((1,), (1,)), ((), ()))
NN = (((1,), (0,)), ((), ()))
FWD_STEPS = ((0, 0, 10, 11), (9, 12, 25, 26), (20, 21, 30, 31), (24, 25, 32, 32))
BWD_STEPS = ((1, 2, 3, 4, 5), (9, 15, 20, 26, 28), (14, 19, 24, 29, 30), (18, 23, 28, 32, 32))


def mm(a, b, dims=NN):
    return lax.dot_general(a, b, dims, preferred_element_type=F32)


def same_sequence(lengths, y):
    ends = []
    for k in range(lengths.shape[2]):
        ends.append(lengths[0, y, k] + (ends[-1] if ends else 0))

    def same(i, kb):
        between = [((e > kb * BLOCK) & (e <= i * BLOCK)).astype(jnp.int32) for e in ends]
        return sum(between) == 0

    return same


class Place:
    def __init__(self, depth):
        d = lax.axis_index("dp")
        self.depth = depth
        self.y = lax.axis_index("sp")
        self.c = d % 2
        self.x = (d // 2) % 2
        self.z = d // 4
        self.next_y = self.device(self.z, self.x, self.c, 1 - self.y)
        self.next_x = self.device(self.z, 1 - self.x, self.c, self.y)
        self.twin = self.device(self.z, self.x, 1 - self.c, self.y)

    def device(self, z, x, c, y):
        return ((z * 2 + x) * 2 + c, y)

    def along(self, step):
        return (self.z + step) % self.depth

    def column(self, step):
        return self.device(self.along(step), self.x, self.c, self.y)

    def greet(self):
        barrier = pltpu.get_barrier_semaphore()
        peers = [self.column(s) for s in range(1, self.depth)] + [self.next_x, self.next_y, self.twin]
        for peer in peers:
            pl.semaphore_signal(barrier, inc=1, device_id=peer, device_id_type=pl.DeviceIdType.MESH)
        pl.semaphore_wait(barrier, len(peers))


def remote(src, dst, send, recv, peer):
    return pltpu.make_async_remote_copy(
        src_ref=src, dst_ref=dst, send_sem=send, recv_sem=recv, device_id=peer, device_id_type=pl.DeviceIdType.MESH
    )


class Gather:
    def __init__(self, me, shard, stage, whole, at, count, local, send, recv, early=False):
        self.me, self.whole, self.early = me, whole, early
        if shard is not None:
            self.shard, self.stage = shard.at[pl.ds(at, count)], stage.at[pl.ds(at, count)]
        self.rows = pl.ds(at, count)
        self.local, self.send, self.recv = local, send, recv

    def own(self, z):
        me = self.me
        return self.whole.at[z, me.x, me.c, me.y, self.rows]

    def load(self):
        return pltpu.make_async_copy(self.shard, self.stage, self.local)

    def keep(self):
        return pltpu.make_async_copy(self.stage, self.own(self.me.z), self.local)

    def depth_hop(self, s, landed):
        me = self.me
        z = me.along(me.depth - s) if landed else me.z
        return remote(self.stage, self.own(z), self.send.at[6 + s], self.recv.at[6 + s], me.column(s))

    def hop(self, x, y, n, peer, c=None):
        group = self.whole.at[:, x, self.me.c if c is None else c, y, self.rows]
        return remote(group, group, self.send.at[n], self.recv.at[n], peer)

    def path(self, n, c=None):
        me = self.me
        x, y = me.x, me.y
        gx = 1 - x if n in (5, 6) else x
        gy = 1 - y if n in (2, 4, 6) else y
        peer = me.next_y if n == 0 else me.next_x if n < 3 else me.twin
        return self.hop(gx, gy, n, peer, c)

    def ready(self):
        self.load().start()

    def begin(self):
        self.load().wait()
        self.keep().start()
        for s in range(1, self.me.depth):
            self.depth_hop(s, False).start()

    def landed(self):
        self.keep().wait()
        for s in range(1, self.me.depth):
            self.depth_hop(s, True).wait()

    def launch(self):
        for n in (0, 3) if self.early else (0, 1, 3):
            self.path(n).start()

    def x_begin(self):
        self.path(1).start()

    def x_end(self):
        self.path(1).wait_send()
        self.hop(1 - self.me.x, self.me.y, 1, self.me.next_x).wait_recv()

    def spread(self):
        self.landed()
        self.launch()

    def from_y(self):
        me = self.me
        self.hop(me.x, 1 - me.y, 0, me.next_y).wait_recv()
        self.path(2).start()
        self.path(4).start()

    def from_x(self):
        me = self.me
        if not self.early:
            self.hop(1 - me.x, me.y, 1, me.next_x).wait_recv()
        self.path(5).start()

    def from_corner(self):
        me = self.me
        self.hop(1 - me.x, 1 - me.y, 2, me.next_x).wait_recv()
        self.path(6).start()

    def end(self):
        for n in range(7):
            if n != 1 or not self.early:
                self.path(n).wait_send()
        for n in range(3, 7):
            self.path(n, 1 - self.me.c).wait_recv()


class Gather2:
    def __init__(self, me, shard, stage, whole, at, count, local, send, recv):
        self.me, self.whole = me, whole
        self.rows = pl.ds(at, count)
        if shard is not None:
            self.shard, self.stage = shard.at[self.rows], stage.at[self.rows]
        self.local, self.send, self.recv = local, send, recv

    def one(self, z, y):
        me = self.me
        return self.whole.at[z, me.x, me.c, y, self.rows]

    def load(self):
        return pltpu.make_async_copy(self.shard, self.stage, self.local)

    def keep(self):
        return pltpu.make_async_copy(self.stage, self.one(self.me.z, self.me.y), self.local)

    def y_hop(self, y):
        me = self.me
        return remote(self.stage, self.one(me.z, y), self.send.at[0], self.recv.at[0], me.next_y)

    def z_hop(self, s, n, landed):
        me = self.me
        z = me.along(me.depth - s) if landed else me.z
        y = 1 - me.y if n else me.y
        src = self.one(me.z, y) if n else self.stage
        k = 1 + n * (me.depth - 1) + s
        return remote(src, self.one(z, y), self.send.at[k], self.recv.at[k], me.column(s))

    def plane(self, x, n, peer, c):
        k = 2 * self.me.depth + n
        plane = self.whole.at[:, x, c, :, self.rows]
        return remote(plane, plane, self.send.at[k], self.recv.at[k], peer)

    def x_hop(self, landed):
        me = self.me
        return self.plane(1 - me.x if landed else me.x, 0, me.next_x, me.c)

    def twin_hop(self, n, landed):
        me = self.me
        return self.plane(1 - me.x if n else me.x, 1 + n, me.twin, 1 - me.c if landed else me.c)

    def ready(self):
        self.load().start()

    def begin(self):
        self.load().wait()
        self.keep().start()
        self.y_hop(self.me.y).start()
        for s in range(1, self.me.depth):
            self.z_hop(s, 0, False).start()

    def pass_z(self):
        self.y_hop(self.me.y).wait_send()
        self.y_hop(1 - self.me.y).wait_recv()
        for s in range(1, self.me.depth):
            self.z_hop(s, 1, False).start()

    def landed(self):
        self.keep().wait()
        for n in range(2):
            for s in range(1, self.me.depth):
                self.z_hop(s, n, True).wait()

    def pass_x(self):
        self.landed()
        self.x_hop(False).start()

    def pass_twin(self):
        self.twin_hop(0, False).start()

    def arrived(self):
        self.x_hop(False).wait_send()
        self.x_hop(True).wait_recv()

    def pass_twin_far(self):
        self.twin_hop(1, False).start()

    def end(self):
        for n in range(2):
            self.twin_hop(n, False).wait_send()
            self.twin_hop(n, True).wait_recv()


class Swap:
    def __init__(self, me, sent, landing, kept, stage, place, local, send, recv):
        self.out = remote(sent, landing(me.y), send, recv, me.next_y)
        self.into = remote(sent, landing(1 - me.y), send, recv, me.next_y)
        self.load = pltpu.make_async_copy(kept, stage, local)
        self.keep = pltpu.make_async_copy(stage, place, local)

    def ready(self):
        self.load.start()

    def begin(self):
        self.out.start()
        self.load.wait()
        self.keep.start()

    def end(self):
        self.out.wait_send()
        self.into.wait_recv()
        self.keep.wait()


def add_group(own, x, y, taken):
    def body(s, _):
        own[s, x, y] = (own[s, x, y].astype(F32) + taken(s).astype(F32)).astype(own.dtype)
        return 0

    lax.fori_loop(0, own.shape[0], body, 0)


class Scatter:
    def __init__(self, me, part, at, count, own, got0, got1, got3, local, send, recv, total):
        self.me, self.part, self.rows = me, part, pl.ds(at, count)
        self.own, self.got0, self.got1, self.got3 = own, got0, got1, got3
        self.local, self.send, self.recv, self.total = local, send, recv, total

    def mine(self):
        return pltpu.make_async_copy(self.part.at[:, :, self.me.c, :, self.rows], self.own, self.local)

    def halves(self):
        return remote(
            self.part.at[:, :, 1 - self.me.c, :, self.rows], self.got0, self.send.at[0], self.recv.at[0], self.me.twin
        )

    def to_x(self, n):
        me = self.me
        y = me.y if n == 0 else 1 - me.y
        return remote(self.own.at[:, 1 - me.x, y], self.got1.at[n], self.send.at[1 + n], self.recv.at[1 + n], me.next_x)

    def to_y(self):
        me = self.me
        return remote(self.own.at[:, me.x, 1 - me.y], self.got1.at[2], self.send.at[3], self.recv.at[3], me.next_y)

    def to_z(self, s):
        me = self.me
        return remote(
            self.own.at[me.along(s), me.x, me.y], self.got3.at[s - 1], self.send.at[3 + s], self.recv.at[3 + s],
            me.column(s),
        )

    def begin(self):
        self.mine().start()
        self.halves().start()

    def across(self):
        me, own, got = self.me, self.own, self.got0
        self.mine().wait()
        self.halves().wait()
        for n, x, y in ((1, 1 - me.x, 1 - me.y), (0, 1 - me.x, me.y)):
            add_group(own, x, y, lambda s: got[s, x, y])
            self.to_x(n).start()
        for x, y in ((me.x, 1 - me.y), (me.x, me.y)):
            add_group(own, x, y, lambda s: got[s, x, y])

    def along_x(self):
        me, own, got = self.me, self.own, self.got1
        self.to_x(1).wait_recv()
        add_group(own, me.x, 1 - me.y, lambda s: got[1, s])
        self.to_y().start()
        self.to_x(0).wait_recv()
        add_group(own, me.x, me.y, lambda s: got[0, s])

    def along_y(self):
        me, own, got = self.me, self.own, self.got1
        self.to_y().wait_recv()
        add_group(own, me.x, me.y, lambda s: got[2, s])
        for s in range(1, me.depth):
            self.to_z(s).start()

    def end(self):
        me = self.me
        total = self.own[me.z, me.x, me.y].astype(F32)
        for s in range(1, me.depth):
            self.to_z(s).wait_recv()
            total = total + self.got3[s - 1].astype(F32)
        self.total[self.rows] = total
        self.to_x(0).wait_send()
        self.to_x(1).wait_send()
        self.to_y().wait_send()
        for s in range(1, me.depth):
            self.to_z(s).wait_send()


def scatter_scratch(pieces, depth):
    out = []
    for rows, cols, dtype in pieces:
        for lead in ((depth, 2, 2), (depth, 2, 2), (3, depth), (depth - 1,)):
            out.append(pltpu.VMEM(lead + (rows, cols), dtype))
    return out


def perform(step, plan):
    for due in sorted(plan):

        @pl.when(step == due)
        def _(actions=plan[due]):
            for action in actions:
                action()


def due(plan, step, action):
    plan.setdefault(step, []).append(action)


def head_pair_masks():
    lanes = lax.broadcasted_iota(jnp.int32, (1, 128), 1)
    return (lanes < 64, lanes >= 64)


def attend_fwd_kernel(depth, pieces, *refs):
    lengths, hs, q_ref, k_ref, v_ref = refs[:5]
    shard = refs[6]
    o_ref, mixed_ref, lse_ref = refs[7:10]
    wholes = refs[10:12]
    vt, local, send, recv, shard_stage = refs[12:]
    pair = pl.program_id(0)
    me = Place(depth)
    same = same_sequence(lengths, me.y)
    gathers = [
        Gather(
            me, shard if a else None, shard_stage, wholes[a], at, count, local.at[n], send.at[n], recv.at[n], n == 0
        )
        for n, (a, at, count) in enumerate(pieces)
    ]
    plan = {}
    due(plan, 0, me.greet)
    for n, g in enumerate(gathers):
        if pieces[n][0]:
            due(plan, 0, g.ready)
    for n, g in enumerate(gathers):
        due(plan, 0, g.begin if pieces[n][0] else g.launch)
        if pieces[n][0]:
            due(plan, FWD_STEPS[0][n], g.spread)
        due(plan, FWD_STEPS[1][n], g.from_y)
        due(plan, FWD_STEPS[2][n], g.from_x)
        due(plan, FWD_STEPS[3][n], g.from_corner)
        due(plan, 32, g.end)
    last = plan.pop(32)
    rows = q_ref.shape[0]
    blocks = rows // BLOCK
    factor = LOG2E / 8.0
    masks = head_pair_masks()
    gains = jnp.where(masks[0], hs[0, 2 * pair], hs[0, 2 * pair + 1])
    for j in range(blocks):
        vtr = v_ref[j * BLOCK : (j + 1) * BLOCK, :].astype(F32).T.astype(BF16)
        for h in range(2):
            vt[j, h, 0:64, :] = vtr[h * 64 : (h + 1) * 64]
            vt[j, h, 64:80, :] = jnp.ones((16, BLOCK), BF16)
    key_at = lax.broadcasted_iota(jnp.int32, (BLOCK, BLOCK), 0)
    query_at = lax.broadcasted_iota(jnp.int32, (BLOCK, BLOCK), 1)

    def one_query(i):
        perform(pair, {k // blocks: plan[k] for k in plan if k % blocks == i})
        q = q_ref[pl.ds(i * BLOCK, BLOCK), :]
        qh = [jnp.where(m, q, jnp.zeros_like(q)) for m in masks]

        def step(kb, carry, diag):
            k = k_ref[pl.ds(kb * BLOCK, BLOCK), :]
            out = []
            for h in range(2):
                s = mm(k, qh[h], NT)
                if diag:
                    s = jnp.where(key_at <= query_at, s, NEG)
                    m = jnp.max(s, axis=0, keepdims=True)
                    p = jnp.exp2(s * factor - m * factor).astype(BF16)
                    out.append((m, mm(vt[kb, h], p)))
                else:
                    bias = jnp.where(same(i, kb), 0.0, NEG)
                    m_old, acc = carry[h]
                    m = jnp.maximum(m_old, jnp.max(s, axis=0, keepdims=True) + bias)
                    p = jnp.exp2(s * factor - (m - bias) * factor).astype(BF16)
                    alpha = jnp.exp2((m_old - m) * factor)
                    out.append((m, acc * alpha + mm(vt[kb, h], p)))
            return tuple(out)

        carry = step(i, None, True)
        for kb in range(i):
            carry = step(kb, carry, False)
        outs = []
        for h in range(2):
            m, acc = carry[h]
            total = acc[64:65]
            outs.append(acc[:64] / total)
            lse_ref[0, h, pl.ds(i, 1), :] = m * factor + jnp.log2(total)
        both = jnp.concatenate(outs, axis=0).T
        mixed_ref[pl.ds(i * BLOCK, BLOCK), :] = both
        o_ref[pl.ds(i * BLOCK, BLOCK), :] = (both * gains).astype(BF16)

    for i in range(blocks):
        one_query(i)
    perform(pair, {pl.num_programs(0) - 1: last})


def attend_fwd(qkv, lengths, hs, begun, shard, depth, collective_id):
    rows, width3 = qkv.shape
    width = width3 // 3
    pairs = width // 128
    blocks = rows // BLOCK
    spec = lambda part: pl.BlockSpec((rows, 128), lambda p, part=part: (0, part * pairs + p))
    smem = pl.BlockSpec(memory_space=pltpu.SMEM)
    anywhere = pl.BlockSpec(memory_space=pl.ANY)
    pieces = []
    for a, count in enumerate((begun.shape[4], shard.shape[0])):
        part = count // 2
        pieces += [(a, 0, part), (a, part, part)]
    count = len(pieces)
    out = pl.pallas_call(
        functools.partial(attend_fwd_kernel, depth, pieces),
        grid=(pairs,),
        in_specs=[smem, smem, spec(0), spec(1), spec(2)] + [anywhere] * 2,
        out_specs=[
            pl.BlockSpec((rows, 128), lambda p: (0, p)),
            pl.BlockSpec((rows, 128), lambda p: (0, p)),
            pl.BlockSpec((1, 2, blocks, BLOCK), lambda p: (p, 0, 0, 0)),
        ]
        + [anywhere] * 2,
        out_shape=[
            jax.ShapeDtypeStruct((rows, width), BF16),
            jax.ShapeDtypeStruct((rows, width), F32),
            jax.ShapeDtypeStruct((pairs, 2, blocks, BLOCK), F32),
            jax.ShapeDtypeStruct(begun.shape, begun.dtype),
            jax.ShapeDtypeStruct((depth, 2, 2, 2) + shard.shape, shard.dtype),
        ],
        input_output_aliases={5: 3},
        scratch_shapes=[
            pltpu.VMEM((blocks, 2, 80, BLOCK), BF16),
            pltpu.SemaphoreType.DMA((count,)),
            pltpu.SemaphoreType.DMA((count, 6 + depth)),
            pltpu.SemaphoreType.DMA((count, 6 + depth)),
            pltpu.VMEM(shard.shape, shard.dtype),
        ],
        compiler_params=pltpu.CompilerParams(
            vmem_limit_bytes=VMEM_CAP, collective_id=collective_id, has_side_effects=True
        ),
        name="attend_fwd",
    )(lengths, hs, qkv, qkv, qkv, begun, shard)
    return out[0], out[1], out[2], out[3], out[4]


def attend_bwd_kernel(depth, pieces, *refs):
    lengths, hs, q_ref, k_ref, v_ref, o_ref, g_ref, lse_ref = refs[:8]
    parts = refs[8:11]
    layer = refs[11]
    dq_ref, dk_ref, dv_ref, delta_ref = refs[12:16]
    sums = refs[16:19]
    layer_out = refs[19]
    kt, dk_acc, dv_acc, local, send, recv, layer_stage = refs[20:27]
    scratch = refs[27:]
    pair = pl.program_id(0)
    me = Place(depth)
    same = same_sequence(lengths, me.y)
    scatters = [
        Scatter(
            me, parts[a], at, count, *scratch[4 * n : 4 * n + 4], local.at[n], send.at[n], recv.at[n], sums[a]
        )
        for n, (a, at, count) in enumerate(pieces)
    ]
    n = len(pieces)
    half = layer_out.shape[1]
    swap = Swap(
        me, layer.at[pl.ds((1 - me.y) * half, half)], lambda y: layer_out.at[y],
        layer.at[pl.ds(me.y * half, half)], layer_stage, layer_out.at[me.y], local.at[n], send.at[n, 0], recv.at[n, 0],
    )
    plan = {}
    due(plan, 0, swap.ready)
    due(plan, 0, me.greet)
    for s in scatters:
        due(plan, 0, s.begin)
    for n, s in enumerate(scatters):
        due(plan, BWD_STEPS[0][n], s.across)
        due(plan, BWD_STEPS[1][n], s.along_x)
        due(plan, BWD_STEPS[2][n], s.along_y)
        due(plan, BWD_STEPS[3][n], s.end)
    due(plan, 0, swap.begin)
    due(plan, 32, swap.end)
    last = plan.pop(32)
    rows = q_ref.shape[0]
    blocks = rows // BLOCK
    factor = LOG2E / 8.0
    masks = head_pair_masks()
    for j in range(blocks):
        kt[j] = k_ref[j * BLOCK : (j + 1) * BLOCK, :].astype(F32).T.astype(BF16)
    key_at = lax.broadcasted_iota(jnp.int32, (BLOCK, BLOCK), 0)
    query_at = lax.broadcasted_iota(jnp.int32, (BLOCK, BLOCK), 1)
    gains = jnp.where(masks[0], hs[0, 2 * pair], hs[0, 2 * pair + 1])
    picks = jnp.concatenate([m.astype(F32) for m in masks] + [jnp.zeros((6, 128), F32)], axis=0).astype(BF16)

    def one_query(i):
        perform(pair, {k // blocks: plan[k] for k in plan if k % blocks == i})
        at = pl.ds(i * BLOCK, BLOCK)
        q = q_ref[at, :]
        g = (g_ref[at, :].astype(F32) * gains).astype(BF16)
        prod = g.astype(F32) * o_ref[at, :]
        hi = prod.astype(BF16)
        lo = (prod - hi.astype(F32)).astype(BF16)
        deltas = mm(picks, hi, NT) + mm(picks, lo, NT)
        qh = [jnp.where(m, q, jnp.zeros_like(q)) for m in masks]
        gh = [jnp.where(m, g, jnp.zeros_like(g)) for m in masks]
        delta = [deltas[h : h + 1] for h in range(2)]
        lse = [lse_ref[0, h, pl.ds(i, 1), :] for h in range(2)]
        for h in range(2):
            delta_ref[0, h, pl.ds(i, 1), :] = delta[h]

        def step(kb, carry, diag):
            ks = pl.ds(kb * BLOCK, BLOCK)
            k = k_ref[ks, :]
            v = v_ref[ks, :]
            out = []
            dk_part = None
            dv_part = None
            for h in range(2):
                s = mm(k, qh[h], NT)
                dp = mm(v, gh[h], NT)
                if diag:
                    p = jnp.exp2(s * factor - lse[h])
                    p = jnp.where(key_at <= query_at, p, 0.0)
                else:
                    bias = jnp.where(same(i, kb), 0.0, -NEG)
                    p = jnp.exp2(s * factor - (lse[h] + bias))
                ds = (p * (dp - delta[h])).astype(BF16)
                dvh = mm(p.astype(BF16), gh[h])
                dkh = mm(ds, qh[h])
                dk_part = dkh if dk_part is None else dk_part + dkh
                dv_part = dvh if dv_part is None else dv_part + dvh
                dqh = mm(kt[kb, h * 64 : (h + 1) * 64, :], ds)
                out.append(dqh if diag else carry[h] + dqh)
            if diag:
                dk_acc[ks, :] = dk_part
                dv_acc[ks, :] = dv_part
            else:
                dk_acc[ks, :] += dk_part
                dv_acc[ks, :] += dv_part
            return tuple(out)

        carry = step(i, None, True)
        for kb in range(i):
            carry = step(kb, carry, False)
        both = jnp.concatenate(carry, axis=0) * 0.125
        dq_ref[at, :] = both.T.astype(BF16)

    for i in range(blocks):
        one_query(i)
    dk_ref[...] = (dk_acc[...] * 0.125).astype(BF16)
    dv_ref[...] = dv_acc[...].astype(BF16)
    perform(pair, {pl.num_programs(0) - 1: last})


def shard_view(part, depth):
    return part.reshape((depth, 2, 2, 2, part.shape[0] // (depth * 8)) + part.shape[1:])


def attend_bwd(qkv, mixed, d_scaled, lse, lengths, hs, parts, layer, depth, collective_id):
    rows, width3 = qkv.shape
    width = width3 // 3
    pairs = width // 128
    blocks = rows // BLOCK
    spec = lambda part: pl.BlockSpec((rows, 128), lambda p, part=part: (0, part * pairs + p))
    col = pl.BlockSpec((rows, 128), lambda p: (0, p))
    stat = pl.BlockSpec((1, 2, blocks, BLOCK), lambda p: (p, 0, 0, 0))
    smem = pl.BlockSpec(memory_space=pltpu.SMEM)
    anywhere = pl.BlockSpec(memory_space=pl.ANY)
    parts = [shard_view(p, depth) for p in parts]
    pieces = []
    for a in (0, 1):
        part = parts[a].shape[4] // 2
        pieces += [(a, 0, part), (a, part, part)]
    pieces.append((2, 0, parts[2].shape[4]))
    count = len(pieces) + 1
    out = pl.pallas_call(
        functools.partial(attend_bwd_kernel, depth, pieces),
        grid=(pairs,),
        in_specs=[smem, smem, spec(0), spec(1), spec(2), col, col, stat] + [anywhere] * 4,
        out_specs=[col, col, col, stat]
        + [pl.BlockSpec(p.shape[4:], lambda p: (0, 0)) for p in parts]
        + [anywhere],
        out_shape=[jax.ShapeDtypeStruct((rows, width), BF16)] * 3
        + [jax.ShapeDtypeStruct((pairs, 2, blocks, BLOCK), F32)]
        + [jax.ShapeDtypeStruct(p.shape[4:], F32) for p in parts]
        + [jax.ShapeDtypeStruct((2, rows // 2, width), BF16)],
        scratch_shapes=[
            pltpu.VMEM((blocks, 128, BLOCK), BF16),
            pltpu.VMEM((rows, 128), F32),
            pltpu.VMEM((rows, 128), F32),
            pltpu.SemaphoreType.DMA((count,)),
            pltpu.SemaphoreType.DMA((count, 3 + depth)),
            pltpu.SemaphoreType.DMA((count, 3 + depth)),
            pltpu.VMEM((rows // 2, width), BF16),
        ]
        + scatter_scratch([(count, parts[a].shape[5], parts[a].dtype) for a, _, count in pieces], depth),
        compiler_params=pltpu.CompilerParams(
            vmem_limit_bytes=VMEM_CAP, collective_id=collective_id, has_side_effects=True
        ),
        name="attend_bwd",
    )(lengths, hs, qkv, qkv, qkv, mixed, d_scaled, lse, *parts, layer)
    return out[:4], out[4:7], out[7]


def row_norm(values):
    center = values - jnp.mean(values, axis=-1, keepdims=True)
    spread = jnp.mean(center * center, axis=-1, keepdims=True)
    rstd = lax.rsqrt(spread + EPS)
    return center * rstd, rstd


def row_norm_back(grad, hat, rstd):
    first = jnp.mean(grad, axis=-1, keepdims=True)
    second = jnp.mean(grad * hat, axis=-1, keepdims=True)
    return rstd * (grad - first - hat * second)


def fold_rows(values):
    return jnp.sum(values.reshape(values.shape[0] // 8, 8, values.shape[1]), axis=0)


def resident(shape):
    return pl.BlockSpec(shape, lambda i: (0,) * len(shape), pipeline_mode=pl.Buffered(1))


GELU_A = math.sqrt(2.0 / math.pi)
GELU_B = 0.044715
CHUNK = 1024


def middle_kernel(
    depth, sc_ref, x_ref, cot, wout, w1, w2, nar, wide,
    lay_ref, post_ref, fin_ref, act_ref, din_ref, dhid_ref, dlow_ref, dsc_ref, gn_ref, gw_ref, dy_out,
    n_s, gp_s, da_s, dy_s, local, go, come,
):
    me = Place(depth)
    step = pl.program_id(0)
    half_tiles = dy_s.shape[1] // x_ref.shape[0]
    load = pltpu.make_async_copy(cot.at[me.y], dy_s.at[0], local.at[0])
    trade = remote(cot.at[1 - me.y], dy_s.at[1], go, come, me.next_y)
    puts = [
        pltpu.make_async_copy(dy_s.at[n], dy_out.at[1 - me.y if n else me.y], local.at[1 + n]) for n in range(2)
    ]

    @pl.when(step == 0)
    def _():
        load.start()
        me.greet()
        trade.start()
        load.wait()
        puts[0].start()

    @pl.when(step == half_tiles)
    def _():
        trade.wait()
        puts[1].start()

    @pl.when(step == pl.num_programs(0) - 1)
    def _():
        for put in puts:
            put.wait()

    @pl.when(step == 0)
    def _():
        gn_ref[...] = jnp.zeros_like(gn_ref)
        gw_ref[...] = jnp.zeros_like(gw_ref)

    tile, width = x_ref.shape
    ff = w1.shape[1]
    chunks = ff // CHUNK
    ahat, arstd = row_norm(sc_ref[...].astype(F32))
    post = (ahat * nar[4:5] + nar[5:6]).astype(BF16)
    post_ref[...] = post
    hidden = x_ref[...].astype(F32) + mm(post, wout[...]) + nar[6:7]
    hhat, hrstd = row_norm(hidden)
    fin = (hhat * nar[7:8] + nar[8:9]).astype(BF16)
    fin_ref[...] = fin

    dyl = dy_s[step // half_tiles, pl.ds(step % half_tiles * tile, tile), :]
    spans = [slice(j * CHUNK, (j + 1) * CHUNK) for j in range(chunks)]

    def lanes(values):
        total = values[:, 0:128]
        for q in range(1, CHUNK // 128):
            total = total + values[:, q * 128 : (q + 1) * 128]
        return total

    first = jnp.zeros((tile, 128), F32)
    second = jnp.zeros((tile, 128), F32)
    near = None
    for at in spans:
        u = mm(fin, w1[:, at]) + wide[0:1, at]
        da_s[:, at] = mm(dyl, w2[at, :], NT)
        u2 = u * u
        t = jnp.tanh(u * (GELU_A + GELU_A * GELU_B * u2))
        half = 0.5 * (1.0 + t)
        n = u * half
        gp_s[:, at] = (half + n * (1.0 - t) * (GELU_A + 3.0 * GELU_A * GELU_B * u2)).astype(BF16)
        if near is None:
            near = jnp.mean(n, axis=-1, keepdims=True)
        n = n - near
        n_s[:, at] = n
        first = first + lanes(n)
        second = second + lanes(n * n)
    nmean = jnp.sum(first, axis=-1, keepdims=True) / ff
    spread = jnp.sum(second, axis=-1, keepdims=True) / ff - nmean * nmean
    nrstd = lax.rsqrt(jnp.maximum(spread, 0.0) + EPS)

    acc = jnp.zeros((tile, width), F32)
    s1 = jnp.zeros((tile, 128), F32)
    s2 = jnp.zeros((tile, 128), F32)
    for at in spans:
        nh = (n_s[:, at] - nmean) * nrstd
        n_s[:, at] = nh
        gain = wide[1:2, at]
        act = (nh * gain + wide[2:3, at]).astype(BF16)
        act_ref[:, at] = act
        acc = acc + mm(act, w2[at, :])
        da = da_s[:, at]
        danh = da * nh
        gw_ref[1, :, at] += fold_rows(danh)
        gw_ref[2, :, at] += fold_rows(da)
        s1 = s1 + lanes(da * gain)
        s2 = s2 + lanes(danh * gain)
    lay_ref[...] = (hidden + acc + nar[9:10]).astype(BF16)
    s1 = jnp.sum(s1, axis=-1, keepdims=True) / ff
    s2 = jnp.sum(s2, axis=-1, keepdims=True) / ff

    dffn = jnp.zeros((tile, width), F32)
    for at in spans:
        dn = nrstd * (da_s[:, at] * wide[1:2, at] - s1 - n_s[:, at] * s2)
        din = (dn * gp_s[:, at].astype(F32)).astype(BF16)
        din_ref[:, at] = din
        gw_ref[0, :, at] += fold_rows(din.astype(F32))
        dffn = dffn + mm(din, w1[:, at], NT)
    dy = dyl.astype(F32)
    gn_ref[5] += fold_rows(dy)
    gn_ref[3] += fold_rows(dffn * hhat)
    gn_ref[4] += fold_rows(dffn)
    dhid = dy + row_norm_back(dffn * nar[7:8], hhat, hrstd)
    dhid_ref[...] = dhid
    gn_ref[2] += fold_rows(dhid)
    dlow = dhid.astype(BF16)
    dlow_ref[...] = dlow
    dpost = mm(dlow, wout[...], NT)
    gn_ref[0] += fold_rows(dpost * ahat)
    gn_ref[1] += fold_rows(dpost)
    dsc_ref[...] = row_norm_back(dpost * nar[4:5], ahat, arstd).astype(BF16)


def middle(scaled, x, cot, wout, w1, w2, narrow, wide, depth, collective_id):
    rows, width = x.shape
    ff = w1.shape[1]
    tile = 256
    tiles = rows // tile

    def at(i):
        return ((i + tiles // 2 * lax.axis_index("sp")) % tiles, 0)

    thin = pl.BlockSpec((tile, width), at)
    fat = pl.BlockSpec((tile, ff), at)
    anywhere = pl.BlockSpec(memory_space=pl.ANY)
    keep = lambda shape: pl.BlockSpec(shape, lambda i: (0,) * len(shape))
    out = pl.pallas_call(
        functools.partial(middle_kernel, depth),
        grid=(tiles,),
        in_specs=[
            thin, thin, anywhere,
            resident(wout.shape), resident(w1.shape), resident(w2.shape),
            resident(narrow.shape), resident(wide.shape),
        ],
        out_specs=[thin, thin, thin, fat, fat, thin, thin, thin, keep((6, 8, width)), keep((3, 8, ff)), anywhere],
        out_shape=[
            jax.ShapeDtypeStruct((rows, width), BF16),
            jax.ShapeDtypeStruct((rows, width), BF16),
            jax.ShapeDtypeStruct((rows, width), BF16),
            jax.ShapeDtypeStruct((rows, ff), BF16),
            jax.ShapeDtypeStruct((rows, ff), BF16),
            jax.ShapeDtypeStruct((rows, width), F32),
            jax.ShapeDtypeStruct((rows, width), BF16),
            jax.ShapeDtypeStruct((rows, width), BF16),
            jax.ShapeDtypeStruct((6, 8, width), F32),
            jax.ShapeDtypeStruct((3, 8, ff), F32),
            jax.ShapeDtypeStruct(cot.shape, cot.dtype),
        ],
        scratch_shapes=[
            pltpu.VMEM((tile, ff), F32),
            pltpu.VMEM((tile, ff), BF16),
            pltpu.VMEM((tile, ff), F32),
            pltpu.VMEM(cot.shape, cot.dtype),
            pltpu.SemaphoreType.DMA((3,)),
            pltpu.SemaphoreType.DMA,
            pltpu.SemaphoreType.DMA,
        ],
        compiler_params=pltpu.CompilerParams(
            vmem_limit_bytes=VMEM_CAP, collective_id=collective_id, has_side_effects=True
        ),
        name="middle",
    )(scaled, x, cot, wout, w1, w2, narrow, wide)
    return *out[:10], out[10].reshape(rows, width)


def enter_kernel(depth, counts, *refs):
    me = Place(depth)
    base = len(counts)
    smalls = refs[:base]
    qkv_shard, out_shard, fc1_shard, tok = refs[base : base + 4]
    qkv_whole, out_whole, fc1_whole, x_out, normed_out, qkv_out, narrow, wide, hs = refs[base + 4 : base + 13]
    small, small_stage, small_whole, qkv_stage, out_stage, fc1_stage, weight = refs[base + 13 : base + 20]
    tok_own, tok_got, normed_tiles, qkv_tiles = refs[base + 20 : base + 24]
    local, send, recv, small_sem, tok_sem, go, come, put_sem, tile_sem = refs[base + 24 : base + 33]
    smalls_here = refs[base + 33 :]
    y = me.y
    qrows, frows = qkv_shard.shape[0] // 2, fc1_shard.shape[0] // 2
    sems = lambda n: (local.at[n], send.at[n], recv.at[n])
    tiny = Gather(me, small, small_stage, small_whole, 0, 16, *sems(0))
    q_a = Gather(me, qkv_shard, qkv_stage, weight, 0, qrows, *sems(1))
    q_b = Gather2(me, qkv_shard, qkv_stage, weight, qrows, qrows, *sems(2))
    w_out = Gather2(me, out_shard, out_stage, out_whole, 0, out_shard.shape[0], *sems(3))
    f_a = Gather(me, fc1_shard, fc1_stage, fc1_whole, 0, frows, *sems(4))
    f_b = Gather(me, fc1_shard, fc1_stage, fc1_whole, frows, frows, *sems(5))
    copies = [pltpu.make_async_copy(s, h, small_sem.at[n]) for n, (s, h) in enumerate(zip(smalls, smalls_here))]
    own = pltpu.make_async_copy(tok.at[y], tok_own, tok_sem)
    for copy in copies + [own]:
        copy.start()
    for g in (q_a, q_b, w_out, f_a, f_b):
        g.ready()
    for copy in copies:
        copy.wait()
    rows = []
    for ref, count in zip(smalls_here, counts):
        row = ref[...].astype(F32).reshape(1, count)
        rows.append(row if count == 128 else jnp.concatenate([row, jnp.zeros((1, 128 - count), F32)], axis=1))
    rows.append(jnp.zeros((16 - len(counts), 128), F32))
    small[...] = jnp.concatenate(rows, axis=0).astype(BF16)
    tiny.ready()
    half, width = tok_own.shape
    cut = half // 4

    def trade(n):
        span = pl.ds(n * cut, cut if n == 0 else half - cut)
        return remote(tok.at[1 - y, span], tok_got.at[span], go.at[n], come.at[n], me.next_y)

    me.greet()
    tiny.begin()
    q_a.begin()
    q_b.begin()
    trade(0).start()
    tiny.spread()
    q_b.pass_z()
    q_a.spread()
    tiny.from_y()
    tiny.from_x()
    w_out.begin()
    tiny.from_corner()
    q_a.from_y()
    trade(1).start()
    q_b.pass_x()
    q_b.pass_twin()
    w_out.pass_z()
    tiny.end()
    part = counts[0]
    each = 128 // part
    for d in range(depth * 8 // each):
        tiles = []
        for k in range(d * each, (d + 1) * each):
            tile = small_whole[k // 8, k // 4 % 2, k // 2 % 2, k % 2].astype(F32)
            tiles.append(tile[:, 0:part])
            wide[0:3, k * 128 : (k + 1) * 128] = tile[10:13]
        narrow[:, d * 128 : (d + 1) * 128] = jnp.concatenate(tiles, axis=1)
    hs[...] = jnp.concatenate(
        [small_whole[0, 0, 0, k].astype(F32)[13:14, 0 : counts[13]] for k in range(2)], axis=1
    )
    q_a.from_x()
    q_a.from_corner()
    f_a.begin()
    f_b.begin()
    w_out.pass_x()
    w_out.pass_twin()
    q_b.arrived()
    q_b.pass_twin_far()
    q_a.end()
    q_b.end()
    put_weight = pltpu.make_async_copy(weight, qkv_whole, put_sem.at[0])
    put_weight.start()
    own.wait()
    put_own = pltpu.make_async_copy(tok_own, x_out.at[y], put_sem.at[1])
    put_own.start()
    tile_rows = normed_tiles.shape[1]
    tiles = normed_tiles.shape[0]

    def puts(i, at):
        span = pl.ds(at * half + i * tile_rows, tile_rows)
        return (
            pltpu.make_async_copy(normed_tiles.at[i], normed_out.at[span], tile_sem.at[0, i]),
            pltpu.make_async_copy(qkv_tiles.at[i], qkv_out.at[span], tile_sem.at[1, i]),
        )

    def project(source, at):
        def body(i, _):
            hat, _ = row_norm(source[pl.ds(i * tile_rows, tile_rows), :].astype(F32))
            normed = (hat * narrow[0:1] + narrow[1:2]).astype(BF16)
            normed_tiles[i] = normed
            for j in range(3 * width // 512):
                span = slice(j * 512, (j + 1) * 512)
                piece = mm(normed, weight[:, :, :, :, :, span].reshape(width, 512))
                third, start = j * 512 // width, j * 512 % width
                if third != 1:
                    row = 2 + third // 2
                    piece = piece + narrow[row : row + 1, start : start + 512]
                qkv_tiles[i, :, span] = piece.astype(BF16)
            for put in puts(i, at):
                put.start()
            return 0

        lax.fori_loop(0, tiles, body, 0)

    project(tok_own, y)
    w_out.arrived()
    w_out.pass_twin_far()
    f_a.landed()
    f_a.x_begin()
    f_b.landed()
    for n in range(2):
        trade(n).wait()
    put_got = pltpu.make_async_copy(tok_got, x_out.at[1 - y], put_sem.at[2])
    put_got.start()
    for i in range(tiles):
        for put in puts(i, y):
            put.wait()
    project(tok_got, 1 - y)
    f_a.x_end()
    w_out.end()
    for i in range(tiles):
        for put in puts(i, 1 - y):
            put.wait()
    put_weight.wait()
    put_own.wait()
    put_got.wait()


def enter(smalls, qkv_weight, out_weight, fc1_weight, tokens, depth, collective_id):
    shards = [qkv_weight, out_weight, fc1_weight]
    counts = [s.shape[0] for s in smalls]
    _, half, width = tokens.shape
    tile = 256
    anywhere = pl.BlockSpec(memory_space=pl.ANY)
    vmem = pl.BlockSpec(memory_space=pltpu.VMEM)
    whole = lambda s: (depth, 2, 2, 2) + s.shape
    out = pl.pallas_call(
        functools.partial(enter_kernel, depth, counts),
        in_specs=[anywhere] * (len(counts) + 4),
        out_specs=[anywhere] * 6 + [vmem] * 3,
        out_shape=[jax.ShapeDtypeStruct(whole(s), s.dtype) for s in shards]
        + [
            jax.ShapeDtypeStruct(tokens.shape, tokens.dtype),
            jax.ShapeDtypeStruct((2 * half, width), BF16),
            jax.ShapeDtypeStruct((2 * half, 3 * width), BF16),
            jax.ShapeDtypeStruct((16, depth * 8 * counts[0]), F32),
            jax.ShapeDtypeStruct((8, depth * 8 * counts[10]), F32),
            jax.ShapeDtypeStruct((1, 2 * counts[13]), F32),
        ],
        scratch_shapes=[
            pltpu.VMEM((16, 128), BF16),
            pltpu.VMEM((16, 128), BF16),
            pltpu.VMEM((depth, 2, 2, 2, 16, 128), BF16),
        ]
        + [pltpu.VMEM(s.shape, s.dtype) for s in shards]
        + [
            pltpu.VMEM(whole(qkv_weight), BF16),
            pltpu.VMEM((half, width), BF16),
            pltpu.VMEM((half, width), BF16),
            pltpu.VMEM((half // tile, tile, width), BF16),
            pltpu.VMEM((half // tile, tile, 3 * width), BF16),
            pltpu.SemaphoreType.DMA((6,)),
            pltpu.SemaphoreType.DMA((6, 2 * depth + 3)),
            pltpu.SemaphoreType.DMA((6, 2 * depth + 3)),
            pltpu.SemaphoreType.DMA((len(counts),)),
            pltpu.SemaphoreType.DMA,
            pltpu.SemaphoreType.DMA((2,)),
            pltpu.SemaphoreType.DMA((2,)),
            pltpu.SemaphoreType.DMA((3,)),
            pltpu.SemaphoreType.DMA((2, half // tile)),
        ]
        + [pltpu.VMEM((n,), BF16) for n in counts],
        compiler_params=pltpu.CompilerParams(
            collective_id=collective_id, has_side_effects=True, vmem_limit_bytes=VMEM_CAP
        ),
        name="enter",
    )(*smalls, *shards, tokens)
    return flat(out[0]), flat(out[1]), out[2], out[3].reshape(-1, width), *out[4:]


def flat(whole):
    return whole.reshape((-1,) + whole.shape[5:])


def leave_kernel(depth, part, heads, *refs):
    dq_ref, dk_ref, dv_ref, x_ref, dhid_ref, w_ref, p_ref = refs[:7]
    parts = refs[7:10]
    thin_ref, fat_ref, delta_ref, hs_ref = refs[10:14]
    out, qkv_sum, small_sum = refs[14:17]
    local, send, recv, go, come, store, g_acc, thin, fat, small, leaving, landing, stage = refs[17:30]
    scratch = refs[30:]
    me = Place(depth)
    step = pl.program_id(0)
    half_tiles = leaving.shape[0]
    tile, width = x_ref.shape
    rows = parts[0].shape[4]
    scatters = [
        Scatter(
            me, parts[n], 0, rows, *scratch[4 * n : 4 * n + 4], local.at[n], send.at[n], recv.at[n],
            qkv_sum.at[:, pl.ds(n * width, width)],
        )
        for n in range(3)
    ]
    smalls = Scatter(me, small, 0, 16, *scratch[12:16], local.at[3], send.at[3], recv.at[3], small_sum)

    def trade(j):
        return remote(leaving.at[j], landing.at[j], go.at[j], come.at[j], me.next_y)

    def put(y, j):
        return pltpu.make_async_copy(stage.at[j], out.at[y, pl.ds(j * tile, tile)], store.at[j])

    @pl.when(step == 0)
    def _():
        g_acc[...] = jnp.zeros_like(g_acc)
        me.greet()
        for s in scatters:
            s.begin()

    @pl.when(step == 2)
    def _():
        for s in scatters:
            s.across()

    hat, rstd = row_norm(x_ref[...].astype(F32))
    dnormed = mm(dq_ref[...], w_ref[:, 0:width], NT)
    dnormed = dnormed + mm(dk_ref[...], w_ref[:, width : 2 * width], NT)
    dnormed = dnormed + mm(dv_ref[...], w_ref[:, 2 * width : 3 * width], NT)
    g_acc[0] += fold_rows(dnormed * hat)
    g_acc[1] += fold_rows(dnormed)
    g_acc[2] += fold_rows(dq_ref[...].astype(F32))
    g_acc[3] += fold_rows(dv_ref[...].astype(F32))
    grad = dhid_ref[...] + row_norm_back(dnormed * p_ref[0:1], hat, rstd)

    @pl.when(step < half_tiles)
    def _():
        leaving[step] = grad.astype(BF16)
        trade(step).start()

    @pl.when(step >= half_tiles)
    def _():
        stage[step - half_tiles] = grad
        put(me.y, step - half_tiles).start()

    @pl.when(step == pl.num_programs(0) - 1)
    def _():
        thin[...] = jnp.zeros_like(thin)
        fat[...] = jnp.zeros_like(fat)
        for k in range(4):
            thin[k : k + 1, :] = jnp.sum(g_acc[k], axis=0, keepdims=True)
        for k in range(6):
            thin[4 + k : 5 + k, :] = jnp.sum(thin_ref[k], axis=0, keepdims=True)
        for k in range(3):
            fat[10 + k : 11 + k, :] = jnp.sum(fat_ref[k], axis=0, keepdims=True)
        lanes = lax.broadcasted_iota(jnp.int32, (1, 128), 1)
        scale = jnp.zeros((1, 128), F32)
        for p in range(delta_ref.shape[0]):
            for h in range(2):
                scale = jnp.where(lanes == 2 * p + h, jnp.sum(delta_ref[p, h]), scale)
        scale = scale / jnp.concatenate([hs_ref[...], jnp.ones((1, 128 - 2 * heads), F32)], axis=1)
        each = 128 // part
        is_scale = lax.broadcasted_iota(jnp.int32, (16, 128), 0) == 13
        for d in range(depth * 8):
            block = thin[:, d // each * 128 : (d // each + 1) * 128]
            turn = d % each * part
            block = pltpu.roll(block, 128 - turn, 1) if turn else block
            block = block + fat[:, d * 128 : (d + 1) * 128]
            row = pltpu.roll(scale, 128 - heads, 1) if d % 2 else scale
            small[d // 8, d // 4 % 2, d // 2 % 2, d % 2] = jnp.where(is_scale, row, block)
        smalls.begin()
        v, k, q = scatters[2], scatters[1], scatters[0]
        v.along_x()
        smalls.across()
        k.along_x()
        v.along_y()
        smalls.along_x()
        q.along_x()
        k.along_y()
        smalls.along_y()
        v.end()
        q.along_y()
        for j in range(half_tiles):
            trade(j).wait()
            put(me.y, j).wait()
            stage[j] = landing[j].astype(F32)
            put(1 - me.y, j).start()
        k.end()
        smalls.end()
        q.end()
        for j in range(half_tiles):
            put(1 - me.y, j).wait()


def leave(dq, dk, dv, x, dhid, weight, params, parts, thin, fat, delta, hs, depth, collective_id):
    rows, width = x.shape
    tile = 256
    tiles = rows // tile
    parts = [shard_view(p, depth) for p in parts]
    part = width // (depth * 8)
    heads = hs.shape[1] // 2

    def at(i):
        return ((i + tiles // 2 * (1 - lax.axis_index("sp"))) % tiles, 0)

    block = pl.BlockSpec((tile, width), at)
    anywhere = pl.BlockSpec(memory_space=pl.ANY)
    pieces = [(p.shape[4], p.shape[5], p.dtype) for p in parts] + [(16, 128, F32)]
    keep = lambda shape: pl.BlockSpec(shape, lambda i: (0,) * len(shape))
    out_shape = [
        jax.ShapeDtypeStruct((2, rows // 2, width), F32),
        jax.ShapeDtypeStruct((parts[0].shape[4], 3 * width), F32),
        jax.ShapeDtypeStruct((16, 128), F32),
    ]
    return pl.pallas_call(
        functools.partial(leave_kernel, depth, part, heads),
        grid=(tiles,),
        in_specs=[block] * 5
        + [resident(weight.shape), resident(params.shape)]
        + [anywhere] * 3
        + [resident(a.shape) for a in (thin, fat, delta, hs)],
        out_specs=[anywhere, keep(out_shape[1].shape), keep(out_shape[2].shape)],
        out_shape=out_shape,
        scratch_shapes=[
            pltpu.SemaphoreType.DMA((4,)),
            pltpu.SemaphoreType.DMA((4, 3 + depth)),
            pltpu.SemaphoreType.DMA((4, 3 + depth)),
            pltpu.SemaphoreType.DMA((tiles // 2,)),
            pltpu.SemaphoreType.DMA((tiles // 2,)),
            pltpu.SemaphoreType.DMA((tiles // 2,)),
            pltpu.VMEM((4, 8, width), F32),
            pltpu.VMEM((16, width), F32),
            pltpu.VMEM((16, fat.shape[2]), F32),
            pltpu.VMEM((depth, 2, 2, 2, 16, 128), F32),
            pltpu.VMEM((tiles // 2, tile, width), BF16),
            pltpu.VMEM((tiles // 2, tile, width), BF16),
            pltpu.VMEM((tiles // 2, tile, width), F32),
        ]
        + scatter_scratch(pieces, depth),
        compiler_params=pltpu.CompilerParams(
            collective_id=collective_id, has_side_effects=True, vmem_limit_bytes=VMEM_CAP
        ),
        name="leave",
    )(dq, dk, dv, x, dhid, weight, params, *parts, thin, fat, delta, hs)


def fast_shards(
    tokens, doc_lengths, out_cotangent, in_gain, in_bias, qkv_weight, q_bias, v_bias, head_scale, attn_gain,
    attn_bias, out_weight, out_bias, ffn_gain, ffn_bias, fc1_weight, fc1_bias, mid_gain, mid_bias, fc2_weight,
    fc2_bias,
):
    depth = lax.axis_size("dp") // 4
    devices = depth * 8
    half = tokens.shape[1]
    rows = 2 * half
    width = tokens.shape[2]
    me = lax.axis_index("sp")

    narrow_in = [in_gain, in_bias, q_bias, v_bias, attn_gain, attn_bias, out_bias, ffn_gain, ffn_bias, fc2_bias]
    wide_in = [fc1_bias, mid_gain, mid_bias]
    part = width // devices
    heads_each = head_scale.shape[0]
    wqkv, wout, begun, x, normed, qkv, narrow, wide, hs = enter(
        narrow_in + wide_in + [head_scale], qkv_weight, out_weight, fc1_weight, tokens, depth, 0
    )
    scaled, mixed, lse, w1, w2 = attend_fwd(qkv, doc_lengths, hs, begun, fc2_weight, depth, 1)
    w1, w2 = flat(w1), flat(w2)
    layer, post, ffn_in, active, d_inner, d_hidden, d_low, d_scaled, grads_narrow, grads_wide, dy = middle(
        scaled, x, out_cotangent, wout, w1, w2, narrow, wide, depth, 4
    )

    def weight_grad(left, right):
        return jnp.einsum("ti,tj->ij", left, right, preferred_element_type=F32).astype(BF16)

    g_fc2 = weight_grad(active, dy)
    g_fc1 = weight_grad(ffn_in, d_inner)
    g_out = weight_grad(post, d_low)
    (dq, dk, dv, delta), (s_fc2, s_fc1, s_out), layer_out = attend_bwd(
        qkv, mixed, d_scaled, lse, doc_lengths, hs, [g_fc2, g_fc1, g_out], layer, depth, 2
    )
    g_q = weight_grad(normed, dq)
    g_k = weight_grad(normed, dk)
    g_v = weight_grad(normed, dv)
    input_grad, s_qkv, s_small = leave(
        dq, dk, dv, x, d_hidden, wqkv, narrow, [g_q, g_k, g_v], grads_narrow, grads_wide, delta, hs, depth, 3
    )
    nar = [s_small[k, :part] for k in range(10)]
    wid = [s_small[10 + k] for k in range(3)]
    s_hs = s_small[13, :heads_each]
    return (
        layer_out, input_grad, nar[0], nar[1], s_qkv, nar[2], nar[3], s_hs, nar[4], nar[5], s_out, nar[6], nar[7],
        nar[8], s_fc1, wid[0], wid[1], wid[2], s_fc2, nar[9],
    )


LONGEST = 2048


def layer_norm(values, norm_gain, norm_shift):
    center = values - jnp.mean(values, axis=-1, keepdims=True)
    spread = jnp.mean(center * center, axis=-1, keepdims=True)
    return center * lax.rsqrt(spread + EPS) * norm_gain + norm_shift


def doc_index(lengths, row_count):
    seq_ends = jnp.cumsum(lengths)
    places = jnp.arange(row_count, dtype=jnp.int32)
    return jnp.sum((places[:, None] >= seq_ends[None, :]).astype(jnp.int32), axis=1)


def block_scores(query_block, key_heads, doc_query, doc_keys, pos_query, pos_keys, score_scale):
    scores = (
        jnp.einsum("qhd,khd->hqk", query_block, key_heads, preferred_element_type=jnp.float32)
        * score_scale
    )
    allowed = (doc_query[:, None] == doc_keys[None, :]) & (pos_keys[None, :] <= pos_query[:, None])
    return jnp.where(allowed[None], scores, -1e30)


def reduce_grads(grad_set):
    return (
        lax.psum_scatter(grad_set[0], ("dp", "sp"), scatter_dimension=0, tiled=True),
        lax.psum_scatter(grad_set[1], ("dp", "sp"), scatter_dimension=0, tiled=True),
        lax.psum_scatter(grad_set[2], ("dp", "sp"), scatter_dimension=0, tiled=True),
        lax.psum_scatter(grad_set[3], ("dp", "sp"), scatter_dimension=0, tiled=True),
        lax.psum_scatter(grad_set[4], ("dp", "sp"), scatter_dimension=0, tiled=True),
        lax.psum_scatter(grad_set[5], ("dp", "sp"), scatter_dimension=0, tiled=True),
        lax.psum_scatter(grad_set[6], ("dp", "sp"), scatter_dimension=0, tiled=True),
        lax.psum_scatter(grad_set[7], ("dp", "sp"), scatter_dimension=0, tiled=True),
        lax.psum_scatter(grad_set[8], ("dp", "sp"), scatter_dimension=0, tiled=True),
        lax.psum_scatter(grad_set[9], ("dp", "sp"), scatter_dimension=0, tiled=True),
        lax.psum_scatter(grad_set[10], ("dp", "sp"), scatter_dimension=0, tiled=True),
        lax.psum_scatter(grad_set[11], ("dp", "sp"), scatter_dimension=0, tiled=True),
        lax.psum_scatter(grad_set[12], ("dp", "sp"), scatter_dimension=0, tiled=True),
        lax.psum_scatter(grad_set[13], ("dp", "sp"), scatter_dimension=0, tiled=True),
        lax.psum_scatter(grad_set[14], ("dp", "sp"), scatter_dimension=0, tiled=True),
        lax.psum_scatter(grad_set[15], ("dp", "sp"), scatter_dimension=0, tiled=True),
        lax.psum_scatter(grad_set[16], ("dp", "sp"), scatter_dimension=0, tiled=True),
    )


def shards(
    tokens,
    doc_lengths,
    out_cotangent,
    in_gain,
    in_bias,
    qkv_weight,
    q_bias,
    v_bias,
    head_scale,
    attn_gain,
    attn_bias,
    out_weight,
    out_bias,
    ffn_gain,
    ffn_bias,
    fc1_weight,
    fc1_bias,
    mid_gain,
    mid_bias,
    fc2_weight,
    fc2_bias,
):
    micro_count = tokens.shape[0]
    tok_count = tokens.shape[1]
    model_width = tokens.shape[2]
    sp_count = lax.axis_size("sp")
    group_rows = tok_count * sp_count
    local_width = model_width // sp_count
    head_local = head_scale.shape[0]
    head_dim = local_width // head_local
    score_scale = 1.0 / math.sqrt(head_dim)
    window_rows = LONGEST
    block_rows = min(512, window_rows)
    block_count = group_rows // block_rows
    head_gains = head_scale.astype(jnp.float32)
    positions = jnp.arange(group_rows, dtype=jnp.int32)
    starts = jnp.arange(block_count, dtype=jnp.int32) * block_rows

    def collect():
        return (
            lax.all_gather(in_gain, ("dp", "sp"), axis=0, tiled=True),
            lax.all_gather(in_bias, ("dp", "sp"), axis=0, tiled=True),
            lax.all_gather(qkv_weight, ("dp", "sp"), axis=0, tiled=True),
            lax.all_gather(q_bias, ("dp", "sp"), axis=0, tiled=True),
            lax.all_gather(v_bias, ("dp", "sp"), axis=0, tiled=True),
            lax.all_gather(attn_gain, ("dp", "sp"), axis=0, tiled=True),
            lax.all_gather(attn_bias, ("dp", "sp"), axis=0, tiled=True),
            lax.all_gather(out_weight, ("dp", "sp"), axis=0, tiled=True),
            lax.all_gather(out_bias, ("dp", "sp"), axis=0, tiled=True),
            lax.all_gather(ffn_gain, ("dp", "sp"), axis=0, tiled=True),
            lax.all_gather(ffn_bias, ("dp", "sp"), axis=0, tiled=True),
            lax.all_gather(fc1_weight, ("dp", "sp"), axis=0, tiled=True),
            lax.all_gather(fc1_bias, ("dp", "sp"), axis=0, tiled=True),
            lax.all_gather(mid_gain, ("dp", "sp"), axis=0, tiled=True),
            lax.all_gather(mid_bias, ("dp", "sp"), axis=0, tiled=True),
            lax.all_gather(fc2_weight, ("dp", "sp"), axis=0, tiled=True),
            lax.all_gather(fc2_bias, ("dp", "sp"), axis=0, tiled=True),
        )

    def split_heads(heads_in):
        query_heads = heads_in[:, 0].reshape(group_rows, head_local, head_dim)
        key_heads = heads_in[:, 1].reshape(group_rows, head_local, head_dim)
        value_heads = heads_in[:, 2].reshape(group_rows, head_local, head_dim)
        return (query_heads, key_heads, value_heads)

    def attend_back(heads_in, lengths, log_total, grad_mixed):
        query_heads, key_heads, value_heads = split_heads(heads_in)
        doc_ids = doc_index(lengths, group_rows)

        def one_block(block_carry, pair):
            grad_keys, grad_values = block_carry
            row_start, block_lse = pair
            query_block = lax.dynamic_slice_in_dim(query_heads, row_start, block_rows, 0)
            grad_block = lax.dynamic_slice_in_dim(grad_mixed, row_start, block_rows, 0)
            masked = block_scores(
                query_block,
                key_heads,
                lax.dynamic_slice_in_dim(doc_ids, row_start, block_rows, 0),
                doc_ids,
                lax.dynamic_slice_in_dim(positions, row_start, block_rows, 0),
                positions,
                score_scale,
            )
            prob_rows = jnp.exp(masked - block_lse[:, :, None])
            value_part = jnp.einsum(
                "hqk,qhd->khd",
                prob_rows.astype(jnp.bfloat16),
                grad_block,
                preferred_element_type=jnp.float32,
            )
            grad_probs = jnp.einsum(
                "qhd,khd->hqk", grad_block, value_heads, preferred_element_type=jnp.float32
            )
            row_inner = jnp.sum(prob_rows * grad_probs, axis=-1, keepdims=True)
            grad_scores = (prob_rows * (grad_probs - row_inner)).astype(jnp.bfloat16)
            grad_query = (
                jnp.einsum(
                    "hqk,khd->qhd", grad_scores, key_heads, preferred_element_type=jnp.float32
                )
                * score_scale
            )
            key_part = jnp.einsum(
                "hqk,qhd->khd", grad_scores, query_block, preferred_element_type=jnp.float32
            )
            grad_keys = grad_keys + key_part
            grad_values = grad_values + value_part
            return ((grad_keys, grad_values), grad_query)

        zero_heads = jnp.zeros((group_rows, head_local, head_dim), jnp.float32)
        (grad_keys, grad_values), grad_queries = lax.scan(
            one_block, (zero_heads, zero_heads), (starts, log_total)
        )
        stacked = jnp.stack(
            [
                grad_queries.reshape(group_rows, local_width),
                (grad_keys * score_scale).reshape(group_rows, local_width),
                grad_values.reshape(group_rows, local_width),
            ],
            axis=1,
        )
        return stacked.astype(jnp.bfloat16)

    outputs = []
    input_grads = []
    total_grads = None
    scale_total = jnp.zeros((head_local,), jnp.float32)
    for micro_index in range(micro_count):
        forward_set = collect()
        (
            forward_wide_in_gain,
            forward_wide_in_bias,
            forward_wide_qkv,
            forward_wide_q_bias,
            forward_wide_v_bias,
            forward_wide_attn_gain,
            forward_wide_attn_bias,
            forward_wide_out,
            forward_wide_out_bias,
            forward_wide_ffn_gain,
            forward_wide_ffn_bias,
            forward_wide_fc1,
            forward_wide_fc1_bias,
            forward_wide_mid_gain,
            forward_wide_mid_bias,
            forward_wide_fc2,
            forward_wide_fc2_bias,
        ) = forward_set
        forward_tok_rows = tokens[micro_index].astype(jnp.float32)
        forward_lengths = doc_lengths[0, micro_index]
        forward_normed = layer_norm(
            forward_tok_rows,
            forward_wide_in_gain.astype(jnp.float32),
            forward_wide_in_bias.astype(jnp.float32),
        ).astype(jnp.bfloat16)
        bias_row = jnp.concatenate(
            [forward_wide_q_bias, jnp.zeros_like(forward_wide_q_bias), forward_wide_v_bias]
        ).astype(jnp.float32)
        projected = (
            jnp.dot(forward_normed, forward_wide_qkv, preferred_element_type=jnp.float32) + bias_row
        )
        qkv_sent = projected.astype(jnp.bfloat16).reshape(tok_count, 3, model_width)
        forward_heads_in = lax.all_to_all(qkv_sent, "sp", split_axis=2, concat_axis=0, tiled=True)
        attend_query_heads, attend_key_heads, attend_value_heads = split_heads(forward_heads_in)
        attend_doc_ids = doc_index(forward_lengths, group_rows)

        def attend_one_block(row_start):
            query_block = lax.dynamic_slice_in_dim(attend_query_heads, row_start, block_rows, 0)
            masked = block_scores(
                query_block,
                attend_key_heads,
                lax.dynamic_slice_in_dim(attend_doc_ids, row_start, block_rows, 0),
                attend_doc_ids,
                lax.dynamic_slice_in_dim(positions, row_start, block_rows, 0),
                positions,
                score_scale,
            )
            row_max = jnp.max(masked, axis=-1, keepdims=True)
            raised = jnp.exp(masked - row_max)
            row_total = jnp.sum(raised, axis=-1, keepdims=True)
            prob_rows = (raised / row_total).astype(jnp.bfloat16)
            head_mixed = jnp.einsum(
                "hqk,khd->qhd", prob_rows, attend_value_heads, preferred_element_type=jnp.float32
            )
            return (head_mixed, (row_max + jnp.log(row_total))[:, :, 0])

        head_mixed, attend_log_total = lax.map(attend_one_block, starts)
        forward_head_mixed = head_mixed.reshape(group_rows, head_local, head_dim)
        scaled = (
            (forward_head_mixed * head_gains[None, :, None])
            .reshape(group_rows, local_width)
            .astype(jnp.bfloat16)
        )
        forward_attn_rows = lax.all_to_all(
            scaled, "sp", split_axis=0, concat_axis=1, tiled=True
        ).astype(jnp.float32)
        forward_post_norm = layer_norm(
            forward_attn_rows,
            forward_wide_attn_gain.astype(jnp.float32),
            forward_wide_attn_bias.astype(jnp.float32),
        ).astype(jnp.bfloat16)
        forward_hidden = (
            forward_tok_rows
            + jnp.dot(forward_post_norm, forward_wide_out, preferred_element_type=jnp.float32)
            + forward_wide_out_bias.astype(jnp.float32)
        )
        forward_ffn_in = layer_norm(
            forward_hidden,
            forward_wide_ffn_gain.astype(jnp.float32),
            forward_wide_ffn_bias.astype(jnp.float32),
        ).astype(jnp.bfloat16)
        forward_ffn_inner = jnp.dot(
            forward_ffn_in, forward_wide_fc1, preferred_element_type=jnp.float32
        ) + forward_wide_fc1_bias.astype(jnp.float32)
        forward_active = layer_norm(
            jax.nn.gelu(forward_ffn_inner),
            forward_wide_mid_gain.astype(jnp.float32),
            forward_wide_mid_bias.astype(jnp.float32),
        ).astype(jnp.bfloat16)
        output = (
            forward_hidden
            + jnp.dot(forward_active, forward_wide_fc2, preferred_element_type=jnp.float32)
            + forward_wide_fc2_bias.astype(jnp.float32)
        )
        forward_kept_values = (
            forward_normed,
            forward_heads_in,
            forward_head_mixed,
            attend_log_total,
            forward_attn_rows,
            forward_post_norm,
            forward_hidden,
            forward_ffn_in,
            forward_ffn_inner,
            forward_active,
        )
        output, kept_values = (output, forward_kept_values)
        backward_set = collect()
        (
            wide_in_gain,
            wide_in_bias,
            wide_qkv,
            wide_q_bias,
            wide_v_bias,
            wide_attn_gain,
            wide_attn_bias,
            wide_out,
            wide_out_bias,
            wide_ffn_gain,
            wide_ffn_bias,
            wide_fc1,
            wide_fc1_bias,
            wide_mid_gain,
            wide_mid_bias,
            wide_fc2,
            wide_fc2_bias,
        ) = backward_set
        (
            normed,
            backward_heads_in,
            backward_head_mixed,
            backward_log_total,
            attn_rows,
            post_norm,
            hidden,
            ffn_in,
            ffn_inner,
            active,
        ) = kept_values
        tok_rows = tokens[micro_index].astype(jnp.float32)
        backward_lengths = doc_lengths[0, micro_index]
        grad_out = out_cotangent[micro_index].astype(jnp.float32)
        fc2_bias_grad = jnp.sum(grad_out, axis=0)
        grad_low = grad_out.astype(jnp.bfloat16)
        fc2_grad = jnp.einsum("ti,tj->ij", active, grad_low, preferred_element_type=jnp.float32)
        grad_active = jnp.einsum(
            "tj,ij->ti", grad_low, wide_fc2, preferred_element_type=jnp.float32
        )
        gelu_out, gelu_back = jax.vjp(jax.nn.gelu, ffn_inner)
        _, mid_back = jax.vjp(
            layer_norm,
            gelu_out,
            wide_mid_gain.astype(jnp.float32),
            wide_mid_bias.astype(jnp.float32),
        )
        grad_gelu, mid_gain_grad, mid_bias_grad = mid_back(grad_active)
        (grad_inner,) = gelu_back(grad_gelu)
        inner_low = grad_inner.astype(jnp.bfloat16)
        fc1_bias_grad = jnp.sum(inner_low.astype(jnp.float32), axis=0)
        fc1_grad = jnp.einsum("ti,tj->ij", ffn_in, inner_low, preferred_element_type=jnp.float32)
        grad_ffn = jnp.einsum("tj,ij->ti", inner_low, wide_fc1, preferred_element_type=jnp.float32)
        _, ffn_back = jax.vjp(
            layer_norm, hidden, wide_ffn_gain.astype(jnp.float32), wide_ffn_bias.astype(jnp.float32)
        )
        grad_hid, ffn_gain_grad, ffn_bias_grad = ffn_back(grad_ffn)
        grad_hidden = grad_out + grad_hid
        out_bias_grad = jnp.sum(grad_hidden, axis=0)
        hidden_low = grad_hidden.astype(jnp.bfloat16)
        out_grad = jnp.einsum(
            "ti,tj->ij", post_norm, hidden_low, preferred_element_type=jnp.float32
        )
        grad_post = jnp.einsum(
            "tj,ij->ti", hidden_low, wide_out, preferred_element_type=jnp.float32
        )
        _, attn_back = jax.vjp(
            layer_norm,
            attn_rows,
            wide_attn_gain.astype(jnp.float32),
            wide_attn_bias.astype(jnp.float32),
        )
        grad_attn, attn_gain_grad, attn_bias_grad = attn_back(grad_post)
        grad_heads = lax.all_to_all(
            grad_attn.astype(jnp.bfloat16), "sp", split_axis=1, concat_axis=0, tiled=True
        )
        grad_scaled = grad_heads.astype(jnp.float32).reshape(group_rows, head_local, head_dim)
        scale_grad = jnp.sum(grad_scaled * backward_head_mixed, axis=(0, 2))
        backward_grad_mixed = (grad_scaled * head_gains[None, :, None]).astype(jnp.bfloat16)
        grad_qkv = attend_back(
            backward_heads_in, backward_lengths, backward_log_total, backward_grad_mixed
        )
        returned = lax.all_to_all(grad_qkv, "sp", split_axis=0, concat_axis=2, tiled=True).reshape(
            tok_count, 3 * model_width
        )
        column_sums = jnp.sum(returned.astype(jnp.float32), axis=0)
        q_bias_grad = column_sums[:model_width]
        v_bias_grad = column_sums[2 * model_width :]
        qkv_grad = jnp.einsum("ti,tj->ij", normed, returned, preferred_element_type=jnp.float32)
        grad_normed = jnp.einsum(
            "tj,ij->ti", returned, wide_qkv, preferred_element_type=jnp.float32
        )
        _, in_back = jax.vjp(
            layer_norm, tok_rows, wide_in_gain.astype(jnp.float32), wide_in_bias.astype(jnp.float32)
        )
        grad_rows, in_gain_grad, in_bias_grad = in_back(grad_normed)
        input_grad = grad_hidden + grad_rows
        grad_set = (
            in_gain_grad,
            in_bias_grad,
            qkv_grad,
            q_bias_grad,
            v_bias_grad,
            attn_gain_grad,
            attn_bias_grad,
            out_grad,
            out_bias_grad,
            ffn_gain_grad,
            ffn_bias_grad,
            fc1_grad,
            fc1_bias_grad,
            mid_gain_grad,
            mid_bias_grad,
            fc2_grad,
            fc2_bias_grad,
        )
        input_grad, grad_set, scale_grad = (input_grad, grad_set, scale_grad)
        grad_set = reduce_grads(grad_set)
        total_grads = (
            grad_set if total_grads is None else jax.tree.map(jnp.add, total_grads, grad_set)
        )
        scale_total = scale_total + scale_grad
        outputs.append(output)
        input_grads.append(input_grad)
    scale_sum = lax.psum(scale_total, "dp")
    layer_out = jnp.stack(outputs).astype(jnp.bfloat16)
    input_grad = jnp.stack(input_grads)
    return (
        layer_out,
        input_grad,
        total_grads[0],
        total_grads[1],
        total_grads[2],
        total_grads[3],
        total_grads[4],
        scale_sum,
        total_grads[5],
        total_grads[6],
        total_grads[7],
        total_grads[8],
        total_grads[9],
        total_grads[10],
        total_grads[11],
        total_grads[12],
        total_grads[13],
        total_grads[14],
        total_grads[15],
        total_grads[16],
    )


def fits(args):
    dp, sp = lax.axis_size("dp"), lax.axis_size("sp")
    tokens, lengths, in_gain, fc1_bias = args[0], args[1], args[3], args[16]
    return (
        sp == 2
        and tokens.shape[0] == 2
        and dp % 4 == 0
        and dp >= 8
        and 2 * tokens.shape[1] == LONGEST
        and lengths.shape[2] * BLOCK == LONGEST
        and 128 % in_gain.shape[0] == 0
        and fc1_bias.shape[0] == 128
        and tokens.shape[2] == 128 * args[8].shape[0]
    )


def body(*args):
    return fast_shards(*args) if fits(args) else shards(*args)


def solution(mesh):
    return jax.shard_map(
        body,
        mesh=mesh,
        in_specs=(
            P(None, ("dp", "sp"), None),
            P("dp", None, None),
            P(None, ("dp", "sp"), None),
            P(("dp", "sp")),
            P(("dp", "sp")),
            P(("dp", "sp"), None),
            P(("dp", "sp")),
            P(("dp", "sp")),
            P("sp"),
            P(("dp", "sp")),
            P(("dp", "sp")),
            P(("dp", "sp"), None),
            P(("dp", "sp")),
            P(("dp", "sp")),
            P(("dp", "sp")),
            P(("dp", "sp"), None),
            P(("dp", "sp")),
            P(("dp", "sp")),
            P(("dp", "sp")),
            P(("dp", "sp"), None),
            P(("dp", "sp")),
        ),
        out_specs=(
            P(None, ("dp", "sp"), None),
            P(None, ("dp", "sp"), None),
            P(("dp", "sp")),
            P(("dp", "sp")),
            P(("dp", "sp"), None),
            P(("dp", "sp")),
            P(("dp", "sp")),
            P("sp"),
            P(("dp", "sp")),
            P(("dp", "sp")),
            P(("dp", "sp"), None),
            P(("dp", "sp")),
            P(("dp", "sp")),
            P(("dp", "sp")),
            P(("dp", "sp"), None),
            P(("dp", "sp")),
            P(("dp", "sp")),
            P(("dp", "sp")),
            P(("dp", "sp"), None),
            P(("dp", "sp")),
        ),
        check_vma=False,
    )
```
